32 devices in a mesh: expert: 16 (over z, y, x), tensor: 2 (over core).
Axes of the slice: x: 2, y: 2, z: 4, core: 2. Of those that a mesh axis runs over, the one named last changes fastest.
Arguments:
- tokens: bfloat16 [16384, 1024], P(('expert', 'tensor')), may hold values from -6 to 6
- norm1_gain: float32 [1024], replicated, may hold values from 0.5 to 1.5
- w_qkv: bfloat16 [3, 1024, 1024], P(None, None, 'tensor'), may hold values from -0.1875 to 0.1875
- w_out: bfloat16 [1024, 1024], P('tensor'), may hold values from -2 to 2
- norm2_gain: float32 [1024], replicated, may hold values from 0.5 to 1.5
- w_up: bfloat16 [1024, 4096], P(None, 'tensor'), may hold values from -0.1875 to 0.1875
- w_down: bfloat16 [4096, 1024], P('tensor'), may hold values from -0.09375 to 0.09375
- w_router: bfloat16 [1024, 16], replicated, may hold values from -0.125 to 0.125
- w_mix: bfloat16 [1024, 2], replicated, may hold values from -0.25 to 0.25
- w_exp_up: bfloat16 [16, 1024, 4096], P('expert', None, 'tensor'), may hold values from -0.1875 to 0.1875
- w_exp_down: bfloat16 [16, 4096, 1024], P('expert', 'tensor'), may hold values from -1.5 to 1.5
- routes: int32 [16384, 1], P('expert'), may hold values from 0 to 15
- segments: int32 [16, 512], P('expert'), may hold values from 0 to 2, never falling along the last dimension, each value on 1 to 256 neighbouring positions
- cotangent: bfloat16 [16384, 1024], P(('expert', 'tensor')), may hold values from -6 to 6
Outputs:
- output: bfloat16 [16384, 1024], P(('expert', 'tensor'))
- grad_tokens: float32 [16384, 1024], P(('expert', 'tensor'))
- grad_gain1: float32 [1024], replicated
- grad_w_qkv: float32 [3, 1024, 1024], P(None, None, 'tensor')
- grad_w_out: float32 [1024, 1024], P('tensor')
- grad_gain2: float32 [1024], replicated
- grad_w_up: float32 [1024, 4096], P(None, 'tensor')
- grad_w_down: float32 [4096, 1024], P('tensor')
- grad_router: float32 [1024, 16], replicated
- grad_mix: float32 [1024, 2], replicated
- grad_w_exp_up: float32 [16, 1024, 4096], P('expert', None, 'tensor')
- grad_w_exp_down: float32 [16, 4096, 1024], P('expert', 'tensor')
The draws below stay inside these ranges and needn't reach their ends.
Inputs may be any that keep to these rules, and one draw needn't show every extreme that they name: `routes`: every expert is the route of some token. `segments`: in each group the continuation numbers never fall; each of the 3 continuations has 1 to 256 tokens, one has exactly 256.
All inputs are finite; a program needn't handle non-finite values.
Results may differ from the reference program's by a relative error of at most 0.019.
Values may be sent and summed in bfloat16 or wider, within the bound.
A program may use at most 320 MiB of HBM per device.

```python
import math
import jax
import jax.numpy as jnp
import numpy as np
from jax import lax

D = 1024
HEADS = 16
HEAD = 64
FF = 4096
EXP_DEV = 1
PROMPT = 512
CONT_LEN = 256
CONT_TOK = 512
NCONT = 3
GROUP = 1024
GROUPS = 16
TOKENS = 16384
EXPERTS = 16
N_EXPERT = 16


def shard_levels(key, dims, split, low, high):
    def one(dim, blocks):
        heights = jax.random.uniform(jax.random.fold_in(jax.random.fold_in(key, 6), dim), (blocks,), jnp.float32, low / len(split), high / len(split))
        return jnp.repeat(jnp.exp(heights), dims[dim] // blocks).reshape((-1,) + (1,) * (len(dims) - dim - 1))

    factor_of = one(*split[0])
    for cut in split[1:]:
        factor_of = factor_of * one(*cut)
    return factor_of


def different_ones(key, rows, number_of, top, lift):
    ranking = jax.random.permutation(jax.random.fold_in(key, 1), number_of)
    favour = ranking
    for power in range(3):
        favour = favour * favour // number_of
    favour = favour * lift // number_of
    lots = jax.random.randint(jax.random.fold_in(key, 2), (rows, number_of), 0, 4096) + favour
    sure = jax.random.permutation(jax.random.fold_in(key, 3), rows)[jnp.arange(number_of) % rows]
    lots = jnp.where(jnp.arange(rows)[:, None] == sure[None, :], 1 << 14, lots)
    score = lots * number_of + jnp.arange(number_of)
    return lax.top_k(score.astype(jnp.int32), top)[1].astype(jnp.int32)


def length_profile(count, total, reach, skew):
    portions = [(1 << 20) // math.isqrt(rank ** skew) + 1 for rank in range(2, count + 1)]
    surplus, given = total - reach - (count - 1), [1] * (count - 1)
    while surplus > 0:
        candidates = [i for i in range(count - 1) if given[i] < reach]
        whole, budget = sum([portions[i] for i in candidates]), surplus
        for i in candidates:
            extra = min(reach - given[i], max(1, budget * portions[i] // whole), surplus)
            given[i] = given[i] + extra
            surplus = surplus - extra
    return np.array([reach] + given)


def ragged(rng, amount, total, limit, slope):
    if amount == 2:
        one = jax.random.randint(rng, (), max(1, total - limit), min(limit, total - 1) + 1)
        return jnp.stack([one, total - one])
    tallies = jnp.asarray(length_profile(amount, total, limit, slope), jnp.int32)
    twos = (amount - 1) // 2
    source_of, taker = tallies[1:1 + 2 * twos:2], tallies[2:2 + 2 * twos:2]
    margin = jnp.minimum(source_of - 1, limit - taker)
    shifted = jax.random.randint(jax.random.fold_in(rng, 1), (twos,), 0, 1 << 20) % (margin + 1)
    tallies = tallies.at[1:1 + 2 * twos:2].set(source_of - shifted).at[2:2 + 2 * twos:2].set(taker + shifted)
    return tallies[jax.random.permutation(jax.random.fold_in(rng, 2), amount)]


def bell_draw(stream_key, extent, deviation, limit, shards=(), kind=jnp.bfloat16):
    entries = jax.random.normal(stream_key, extent, jnp.float32) * deviation
    if len(shards) > 0:
        entries = shard_levels(stream_key, extent, shards, -0.22, 0.18) * entries
    return jnp.clip(entries, min=-limit, max=limit).astype(kind)


def setup_inputs(seed: int = 0) -> dict:
    key_list = jax.random.split(jax.random.key(seed), 15)
    return {
        "tokens": bell_draw(key_list[0], (TOKENS, D), 1.0, 6.0, ((0, 32),)),
        "norm1_gain": jnp.clip(1.0 + 0.1 * jax.random.normal(key_list[1], (D,), jnp.float32), 0.5, 1.5),
        "w_qkv": bell_draw(key_list[2], (3, D, D), D ** -0.5, 0.1875, ((2, 2),)),
        "w_out": bell_draw(key_list[3], (D, D), (max(D * 8 // GROUP, 1)) ** -0.5, 2.0, ((0, 2),)),
        "norm2_gain": jnp.clip(1.0 + 0.1 * jax.random.normal(key_list[4], (D,), jnp.float32), 0.5, 1.5),
        "w_up": bell_draw(key_list[5], (D, FF), D ** -0.5, 0.1875, ((1, 2),)),
        "w_down": bell_draw(key_list[6], (FF, D), FF ** -0.5, 0.09375, ((0, 2),)),
        "w_router": bell_draw(key_list[7], (D, EXPERTS), (2 * D) ** -0.5, 0.125),
        "w_mix": bell_draw(key_list[8], (D, 2), (D // 2) ** -0.5, 0.25),
        "w_exp_up": bell_draw(key_list[9], (EXPERTS, D, FF), D ** -0.5, 0.1875, ((0, 16), (2, 2))),
        "w_exp_down": bell_draw(key_list[10], (EXPERTS, FF, D), (max(FF // EXPERTS ** 2, 1)) ** -0.5, 1.5, ((0, 16), (1, 2))),
        "routes": different_ones(key_list[11], TOKENS, EXPERTS, 1, 512),
        "segments": jax.vmap(lambda own: jnp.searchsorted(jnp.cumsum(ragged(own, NCONT, CONT_TOK, CONT_LEN, 1)), jnp.arange(CONT_TOK), side="right"))(jax.random.split(key_list[12], GROUPS)).reshape((GROUPS, CONT_TOK)).astype(jnp.int32),
        "cotangent": bell_draw(key_list[13], (TOKENS, D), 1.0, 6.0, ((0, 32),)),
    }


@jax.custom_vjp
def low(v):
    return lax.optimization_barrier(v.astype(jnp.bfloat16)).astype(jnp.float32)

@jax.custom_vjp
def low_back(v):
    return v

def low_keep(v):
    return (low(v), None)

def low_pass(kept, grad):
    return (grad,)

def back_keep(v):
    return (v, None)

def back_low(kept, grad):
    return (low(grad),)
low.defvjp(low_keep, low_pass)
low_back.defvjp(back_keep, back_low)
epsilon = 1e-05
highest = lax.Precision.HIGHEST

def layer_norm(values, norm_gain):
    centred = values - lax.optimization_barrier(jnp.mean(values, axis=-1, keepdims=True))
    variance = lax.optimization_barrier(jnp.mean(centred * centred, axis=-1, keepdims=True))
    return centred * lax.rsqrt(variance + epsilon) * norm_gain

def reference(tokens, norm1_gain, w_qkv, w_out, norm2_gain, w_up, w_down, w_router, w_mix, w_exp_up, w_exp_down, routes, segments, cotangent):
    group_rows = PROMPT + CONT_TOK
    groups_all = N_EXPERT
    experts_all = EXP_DEV * N_EXPERT
    capacity = group_rows // experts_all
    score_scale = HEAD ** (-0.5)
    route_ids = routes[:, 0].astype(jnp.int32)
    grouped_ids = route_ids.reshape(groups_all, group_rows)
    one_hot = (grouped_ids[:, :, None] == jnp.arange(experts_all, dtype=jnp.int32)[None, None, :]).astype(jnp.int32)
    earlier = jnp.cumsum(one_hot, axis=1) - one_hot
    slot_index = lax.optimization_barrier(jnp.sum(earlier * one_hot, axis=-1))
    kept_mask = (slot_index < capacity).reshape(-1)
    global_slot = (jnp.arange(groups_all, dtype=jnp.int32)[:, None] * capacity + slot_index).reshape(-1)
    target_slot = jnp.where(kept_mask, global_slot, groups_all * capacity).astype(jnp.int32)
    safe_slot = jnp.where(kept_mask, global_slot, 0).astype(jnp.int32)
    kept_float = kept_mask.astype(jnp.float32)
    labels = jnp.concatenate([jnp.full((groups_all, PROMPT), -1, jnp.int32), segments.astype(jnp.int32)], axis=1)
    positions = jnp.arange(group_rows, dtype=jnp.int32)

    def forward(x_in, gain_one, qkv_w, out_w, gain_two, up_w, down_w, router_w, mix_w, exp_up_w, exp_down_w):

        def attend(packed):
            block_x, block_labels = packed
            normed = low(layer_norm(block_x, gain_one))
            projected = low_back(low(jnp.einsum('gd,cdk->cgk', normed, qkv_w, precision=highest)))
            queries = projected[0].reshape(group_rows, HEADS, HEAD)
            keys_all = projected[1].reshape(group_rows, HEADS, HEAD)
            values_all = projected[2].reshape(group_rows, HEADS, HEAD)
            scores = low_back(jnp.einsum('qhe,khe->hqk', queries, keys_all, precision=highest) * score_scale)
            allowed = (positions[None, :] <= positions[:, None]) & ((positions[None, :] < PROMPT) | (block_labels[None, :] == block_labels[:, None]))
            scores = jnp.where(allowed[None], scores, -1e+30)
            weights = low(jax.nn.softmax(scores, axis=-1))
            mixed_heads = jnp.einsum('hqk,khe->qhe', weights, values_all, precision=highest).reshape(group_rows, HEADS * HEAD)
            mixed_heads = low_back(low(mixed_heads))
            return block_x + low_back(jnp.dot(mixed_heads, out_w, precision=highest))
        middle = lax.map(jax.checkpoint(attend), (x_in.reshape(groups_all, group_rows, D), labels))
        hidden = low(layer_norm(middle, gain_two))

        def dense(block_h):
            pre_act = low_back(jnp.dot(block_h, up_w, precision=highest))
            return low_back(jnp.dot(low(jax.nn.gelu(pre_act)), down_w, precision=highest))
        dense_out = lax.map(jax.checkpoint(dense), hidden).reshape(-1, D)
        hidden_flat = hidden.reshape(-1, D)
        router_soft = jax.nn.softmax(jnp.dot(hidden_flat, router_w, precision=highest), axis=-1)
        gate_value = jnp.take_along_axis(router_soft, route_ids[:, None], axis=1)[:, 0]
        mix_coef = jax.nn.softmax(jnp.dot(hidden_flat, mix_w, precision=highest), axis=-1)
        slot_rows = jnp.zeros((experts_all, groups_all * capacity, D), jnp.float32).at[route_ids, target_slot].set(hidden_flat, mode='drop')

        def expert(packed):
            first_w, second_w, slot_block = packed
            pre_act = low_back(jnp.dot(slot_block, first_w, precision=highest))
            return low_back(jnp.dot(low(jax.nn.gelu(pre_act)), second_w, precision=highest))
        slot_out = lax.map(jax.checkpoint(expert), (exp_up_w, exp_down_w, slot_rows))
        expert_rows = slot_out[route_ids, safe_slot] * kept_float[:, None]
        return middle.reshape(-1, D) + mix_coef[:, 0:1] * dense_out + (mix_coef[:, 1] * gate_value)[:, None] * expert_rows
    floats = (tokens.astype(jnp.float32), norm1_gain.astype(jnp.float32), w_qkv.astype(jnp.float32), w_out.astype(jnp.float32), norm2_gain.astype(jnp.float32), w_up.astype(jnp.float32), w_down.astype(jnp.float32), w_router.astype(jnp.float32), w_mix.astype(jnp.float32), w_exp_up.astype(jnp.float32), w_exp_down.astype(jnp.float32))
    result, pull = jax.vjp(forward, *floats)
    grads = pull(cotangent.astype(jnp.float32))
    return (result.astype(jnp.bfloat16), grads[0], grads[1], grads[2], grads[3], grads[4], grads[5], grads[6], grads[7], grads[8], grads[9], grads[10])
```

```python
import functools

import jax
import jax.numpy as jnp
from jax import lax
from jax.experimental import pallas as pl
from jax.experimental.pallas import tpu as pltpu
from jax.sharding import PartitionSpec as P

HEAD = 64
PROMPT = 512
BLOCK = 256
LANES = 128
PIECE = 256
MASKED = -1e30

epsilon = 1e-05
highest = lax.Precision.HIGHEST
f32 = jnp.float32
bf16 = jnp.bfloat16


def layer_norm(values, norm_gain):
    centred = values - jnp.mean(values, axis=-1, keepdims=True)
    variance = jnp.mean(centred * centred, axis=-1, keepdims=True)
    return centred * lax.rsqrt(variance + epsilon) * norm_gain


def gelu_grad(pre_act, upstream):
    return jax.vjp(jax.nn.gelu, pre_act)[1](upstream)[0]


def nt_dot(left, right):
    return lax.dot_general(left, right, (((1,), (1,)), ((), ())), preferred_element_type=f32)


def nn_dot(left, right):
    return lax.dot_general(left, right, (((1,), (0,)), ((), ())), preferred_element_type=f32)


def tn_dot(left, right):
    return lax.dot_general(left, right, (((0,), (0,)), ((), ())), preferred_element_type=f32)


def fill_bias(row_labels_ref, col_labels_ref, cont_bias, tri_bias, transposed):
    size = cont_bias.shape[0]
    down = lax.broadcasted_iota(jnp.int32, (size, size), 0)
    across = lax.broadcasted_iota(jnp.int32, (size, size), 1)
    ordered = (down <= across) if transposed else (across <= down)
    same = row_labels_ref[...] == col_labels_ref[...]
    cont_bias[...] = jnp.where(ordered & same, 0.0, MASKED)
    down = lax.broadcasted_iota(jnp.int32, (BLOCK, BLOCK), 0)
    across = lax.broadcasted_iota(jnp.int32, (BLOCK, BLOCK), 1)
    ordered = (down <= across) if transposed else (across <= down)
    tri_bias[...] = jnp.where(ordered, 0.0, MASKED)


def head_lanes(half):
    lane = lax.broadcasted_iota(jnp.int32, (1, LANES), 1)
    return (lane < HEAD) if half == 0 else (lane >= HEAD)


def attend_kernel(col_ref, row_ref, q_ref, k_ref, v_ref, o_ref, cont_bias, tri_bias):
    @pl.when(pl.program_id(0) == 0)
    def _():
        fill_bias(col_ref, row_ref, cont_bias, tri_bias, False)

    rows = q_ref.shape[0]
    scale = HEAD**-0.5
    for block in range(rows // BLOCK):
        start = block * BLOCK
        width = start + BLOCK
        mixed = []
        for half in range(2):
            query = jnp.where(head_lanes(half), q_ref[start:width, :] * scale, 0.0).astype(bf16)
            if start < PROMPT:
                cut, bias = start, tri_bias[...]
            else:
                cut = PROMPT
                bias = cont_bias[start - PROMPT : width - PROMPT, : width - PROMPT]
            tail = nt_dot(query, k_ref[cut:width, :]) + bias
            top = jnp.max(tail, axis=1, keepdims=True)
            if cut:
                lead = nt_dot(query, k_ref[:cut, :])
                top = jnp.maximum(top, jnp.max(lead, axis=1, keepdims=True))
            tail = jnp.exp(tail - top)
            total = jnp.sum(tail, axis=1, keepdims=True)
            out = nn_dot(tail.astype(bf16), v_ref[cut:width, :])
            if cut:
                lead = jnp.exp(lead - top)
                total = total + jnp.sum(lead, axis=1, keepdims=True)
                out = out + nn_dot(lead.astype(bf16), v_ref[:cut, :])
            mixed.append(out / total)
        o_ref[start:width, :] = jnp.where(head_lanes(0), mixed[0], mixed[1]).astype(bf16)


def attend_back_kernel(
    col_ref, row_ref, q_ref, k_ref, v_ref, g_ref, d_ref, cont_bias, tri_bias, dk_acc, dv_acc
):
    @pl.when(pl.program_id(0) == 0)
    def _():
        fill_bias(col_ref, row_ref, cont_bias, tri_bias, True)

    rows = q_ref.shape[0]
    scale = HEAD**-0.5
    dk_acc[...] = jnp.zeros_like(dk_acc)
    dv_acc[...] = jnp.zeros_like(dv_acc)
    for block in range(rows // BLOCK):
        start = block * BLOCK
        width = start + BLOCK
        dq = None
        for half in range(2):
            lanes = head_lanes(half)
            query = jnp.where(lanes, q_ref[start:width, :] * scale, 0.0).astype(bf16)
            grad = jnp.where(lanes, g_ref[start:width, :], 0.0).astype(bf16)
            key = jnp.where(lanes, k_ref[:width, :] * scale, 0.0).astype(bf16)
            if start < PROMPT:
                cut, bias = start, tri_bias[...]
            else:
                cut = PROMPT
                bias = cont_bias[: width - PROMPT, start - PROMPT : width - PROMPT]
            scores = nt_dot(k_ref[cut:width, :], query) + bias
            if cut:
                scores = jnp.concatenate([nt_dot(k_ref[:cut, :], query), scores], axis=0)
            top = jnp.max(scores, axis=0, keepdims=True)
            weights = jnp.exp(scores - top)
            weights = weights * (1.0 / jnp.sum(weights, axis=0, keepdims=True))
            grad_weights = nt_dot(v_ref[:width, :], grad)
            row_dot = jnp.sum(weights * grad_weights, axis=0, keepdims=True)
            grad_scores = (weights * (grad_weights - row_dot)).astype(bf16)
            dv_acc[:width, :] += nn_dot(weights.astype(bf16), grad)
            dk_acc[:width, :] += nn_dot(grad_scores, query)
            part = tn_dot(grad_scores, key)
            dq = part if dq is None else dq + part
        d_ref[0, start:width, :] = dq.astype(bf16)
    d_ref[1] = dk_acc[...].astype(bf16)
    d_ref[2] = dv_acc[...].astype(bf16)


def head_specs(rows):
    return [
        pl.BlockSpec((pl.Squeezed(), rows, LANES), functools.partial(lambda c, i: (c, 0, i), c))
        for c in range(3)
    ]


def attend(labels, projected):
    rows, cols = projected.shape[1:]
    cont = rows - PROMPT
    work = 2 * rows * rows * cols
    return pl.pallas_call(
        attend_kernel,
        grid=(cols // LANES,),
        in_specs=[
            pl.BlockSpec((cont, 1), lambda i: (0, 0)),
            pl.BlockSpec((1, cont), lambda i: (0, 0)),
            *head_specs(rows),
        ],
        out_specs=pl.BlockSpec((rows, LANES), lambda i: (0, i)),
        out_shape=jax.ShapeDtypeStruct((rows, cols), bf16),
        scratch_shapes=[pltpu.VMEM((cont, cont), f32), pltpu.VMEM((BLOCK, BLOCK), f32)],
        cost_estimate=pl.CostEstimate(
            flops=2 * work, bytes_accessed=8 * rows * cols, transcendentals=rows * rows * 4
        ),
        name="attend",
    )(labels[:, None], labels[None, :], projected, projected, projected)


def attend_back(labels, projected, grad_heads):
    rows, cols = projected.shape[1:]
    cont = rows - PROMPT
    work = 2 * rows * rows * cols
    return pl.pallas_call(
        attend_back_kernel,
        grid=(cols // LANES,),
        in_specs=[
            pl.BlockSpec((cont, 1), lambda i: (0, 0)),
            pl.BlockSpec((1, cont), lambda i: (0, 0)),
            *head_specs(rows),
            pl.BlockSpec((rows, LANES), lambda i: (0, i)),
        ],
        out_specs=pl.BlockSpec((3, rows, LANES), lambda i: (0, 0, i)),
        out_shape=jax.ShapeDtypeStruct((3, rows, cols), bf16),
        scratch_shapes=[
            pltpu.VMEM((cont, cont), f32),
            pltpu.VMEM((BLOCK, BLOCK), f32),
            pltpu.VMEM((rows, LANES), f32),
            pltpu.VMEM((rows, LANES), f32),
        ],
        cost_estimate=pl.CostEstimate(
            flops=5 * work, bytes_accessed=14 * rows * cols, transcendentals=rows * rows * 4
        ),
        name="attend_back",
    )(labels[:, None], labels[None, :], projected, projected, projected, grad_heads)


def partner_of(bit):
    me = lax.axis_index("expert")
    side = lax.rem(me // bit, 2)
    return me + bit * (1 - 2 * side), side


def sum_kernel(layout, orders, counts, *refs):
    n_in = len(layout)
    ins, small_in = refs[:n_in], refs[n_in]
    outs, small_out = refs[n_in + 1 : 2 * n_in + 1], refs[2 * n_in + 1]
    rest = refs[2 * n_in + 2 :]
    depth = len(orders[0])
    held, full, small, small_got = rest[:4]
    got = rest[4 : 4 + depth]
    send_sem, recv_sem, load_sem, store_sem, small_sem = rest[4 + depth :]
    bits = sorted(orders[0])
    rank = lax.axis_index("tensor")

    def small_copy(step):
        if step < depth:
            target = {"expert": partner_of(bits[step])[0]}
        else:
            target = {"tensor": 1 - rank}
        return pltpu.make_async_remote_copy(
            small.at[step],
            small_got.at[step],
            small_sem.at[0, step],
            small_sem.at[1, step],
            device_id=target,
            device_id_type=pl.DeviceIdType.MESH,
        )

    barrier = pltpu.get_barrier_semaphore()
    for bit in bits:
        pl.semaphore_signal(
            barrier,
            1,
            device_id={"expert": partner_of(bit)[0]},
            device_id_type=pl.DeviceIdType.MESH,
        )
    pl.semaphore_signal(
        barrier, 1, device_id={"tensor": 1 - rank}, device_id_type=pl.DeviceIdType.MESH
    )

    where = [(a, piece) for a, pieces in enumerate(layout) for piece in pieces]

    def load(piece):
        a, parts = where[piece]
        return [
            pltpu.make_async_copy(
                ins[a].at[src], held.at[(piece, *dst)], load_sem.at[piece]
            )
            for src, dst in parts
        ]

    def store(piece):
        a, parts = where[piece]
        return [
            pltpu.make_async_copy(
                full.at[(piece, *dst)], outs[a].at[src], store_sem.at[piece]
            )
            for src, dst in parts
        ]

    for piece in range(len(where)):
        for copy in load(piece):
            copy.start()
    pltpu.make_async_copy(small_in, small.at[0], small_sem.at[2, 0]).start()
    pl.semaphore_wait(barrier, depth + 1)

    sides = {bit: partner_of(bit) for bit in bits}

    def offset(order, levels):
        total = 0
        for level in range(levels):
            total = total + sides[order[level]][1] * (PIECE >> (level + 1))
        return pl.multiple_of(total, 16)

    def reduce_copy(color, stage, piece):
        order = orders[color]
        target, side = sides[order[stage]]
        size = PIECE >> (stage + 1)
        away = pl.multiple_of(offset(order, stage) + (1 - side) * size, 16)
        return pltpu.make_async_remote_copy(
            held.at[piece, pl.ds(away, size)],
            got[stage].at[piece],
            send_sem.at[stage, piece],
            recv_sem.at[stage, piece],
            device_id={"expert": target},
            device_id_type=pl.DeviceIdType.MESH,
        )

    def gather_copy(color, stage, piece):
        order = orders[color]
        target, _ = sides[order[depth - 1 - stage]]
        size = PIECE >> (depth - stage)
        mine = offset(order, depth - stage)
        return pltpu.make_async_remote_copy(
            full.at[piece, pl.ds(mine, size)],
            full.at[piece, pl.ds(mine, size)],
            send_sem.at[depth + stage, piece],
            recv_sem.at[depth + stage, piece],
            device_id={"expert": target},
            device_id_type=pl.DeviceIdType.MESH,
        )

    def run(color, stage, piece):
        order = orders[color]
        if stage == 0:
            a = pltpu.make_async_copy(held.at[piece], held.at[piece], load_sem.at[piece])
            a.wait()
        elif stage <= depth:
            reduce_copy(color, stage - 1, piece).wait()
            size = PIECE >> stage
            at = offset(order, stage)
            total = held[piece, pl.ds(at, size), :].astype(f32) + got[stage - 1][piece].astype(f32)
            if stage < depth:
                held[piece, pl.ds(at, size), :] = total.astype(bf16)
            else:
                full[piece, pl.ds(at, size), :] = total.astype(bf16)
        else:
            gather_copy(color, stage - depth - 1, piece).wait()
        if stage < depth:
            reduce_copy(color, stage, piece).start()
        elif stage < 2 * depth:
            gather_copy(color, stage - depth, piece).start()
        else:
            for number in range(len(where)):

                @pl.when(piece == number)
                def _(number=number):
                    for copy in store(number):
                        copy.start()

    firsts = [sum(counts[:color]) for color in range(len(counts))]

    def step(t, _):
        for stage in range(2 * depth, -1, -1):
            for color, count in enumerate(counts):

                @pl.when((t >= stage) & (t - stage < count))
                def _(color=color, stage=stage):
                    run(color, stage, firsts[color] + t - stage)

        for number in range(depth + 2):

            @pl.when(t == number)
            def _(number=number):
                if number == 0:
                    pltpu.make_async_copy(small_in, small.at[0], small_sem.at[2, 0]).wait()
                else:
                    small_copy(number - 1).wait()
                    small[number] = small[number - 1] + small_got[number - 1]
                if number < depth + 1:
                    small_copy(number).start()

        return 0

    lax.fori_loop(0, max(counts) + 2 * depth, step, 0)
    out = pltpu.make_async_copy(small.at[depth + 1], small_out, small_sem.at[2, 1])
    out.start()
    for piece in range(len(where)):
        for copy in store(piece):
            copy.wait()
    out.wait()


def split_layout(shapes):
    layout = []
    for shape in shapes:
        pieces = []
        if len(shape) == 3:
            cols = shape[2]
            blocks = [
                (c, slice(r, r + PIECE)) for c in range(shape[0]) for r in range(0, shape[1], PIECE)
            ]
            for first in range(0, len(blocks), 2):
                pieces.append(
                    [
                        (blocks[first + j], (slice(None), slice(j * cols, (j + 1) * cols)))
                        for j in range(2)
                    ]
                )
        else:
            for c in range(0, shape[1], 1024):
                for r in range(0, shape[0], PIECE):
                    pieces.append([((slice(r, r + PIECE), slice(c, c + 1024)), ())])
        layout.append(pieces)
    return layout


def sum_over_experts(grads, small_rows, share=(10, 8, 6)):
    layout = split_layout([g.shape for g in grads])
    pieces = sum(map(len, layout))
    orders = ((1, 2, 4, 8), (2, 4, 1, 8), (4, 1, 2, 8))
    counts = share
    depth = 4
    return pl.pallas_call(
        functools.partial(sum_kernel, layout, orders, counts),
        in_specs=[pl.BlockSpec(memory_space=pl.ANY)] * (len(grads) + 1),
        out_specs=[pl.BlockSpec(memory_space=pl.ANY)] * (len(grads) + 1),
        out_shape=[jax.ShapeDtypeStruct(g.shape, bf16) for g in grads]
        + [jax.ShapeDtypeStruct(small_rows.shape, f32)],
        scratch_shapes=[
            pltpu.VMEM((pieces, PIECE, 1024), bf16),
            pltpu.VMEM((pieces, PIECE, 1024), bf16),
            pltpu.VMEM((depth + 2, *small_rows.shape), f32),
            pltpu.VMEM((depth + 1, *small_rows.shape), f32),
            *[pltpu.VMEM((pieces, PIECE >> (s + 1), 1024), bf16) for s in range(depth)],
            pltpu.SemaphoreType.DMA((2 * depth, pieces)),
            pltpu.SemaphoreType.DMA((2 * depth, pieces)),
            pltpu.SemaphoreType.DMA((pieces,)),
            pltpu.SemaphoreType.DMA((pieces,)),
            pltpu.SemaphoreType.DMA((3, depth + 1)),
        ],
        compiler_params=pltpu.CompilerParams(
            collective_id=1, has_side_effects=True, vmem_limit_bytes=60 * 1024 * 1024
        ),
        name="sum_over_experts",
    )(*grads, small_rows)


def swap(values):
    return lax.ppermute(values, "tensor", [(0, 1), (1, 0)])


def in_order(own, other, axis):
    rank = lax.axis_index("tensor")
    return jnp.where(
        rank == 0,
        jnp.concatenate([own, other], axis=axis),
        jnp.concatenate([other, own], axis=axis),
    )


def gather_pair(own, axis=0):
    if lax.axis_size("tensor") != 2:
        return lax.all_gather(own, "tensor", axis=axis, tiled=True)
    return in_order(own, swap(own), axis)


def scatter_pair(partial, axis=0, kind=bf16):
    if lax.axis_size("tensor") != 2:
        return lax.psum_scatter(
            partial.astype(kind), "tensor", scatter_dimension=axis, tiled=True
        ).astype(f32)
    rank = lax.axis_index("tensor")
    size = partial.shape[axis] // 2
    keep = lax.dynamic_slice_in_dim(partial, rank * size, size, axis)
    away = lax.dynamic_slice_in_dim(partial, (1 - rank) * size, size, axis).astype(kind)
    return keep + swap(away).astype(f32)


def turn_pair(cols_mine):
    if lax.axis_size("tensor") != 2:
        return lax.all_to_all(cols_mine, "tensor", 0, 1, tiled=True)
    rank = lax.axis_index("tensor")
    size = cols_mine.shape[0] // 2
    keep = lax.dynamic_slice_in_dim(cols_mine, rank * size, size, 0)
    away = lax.dynamic_slice_in_dim(cols_mine, (1 - rank) * size, size, 0)
    return in_order(keep, swap(away), 1)


def body(
    tokens,
    norm1_gain,
    w_qkv,
    w_out,
    norm2_gain,
    w_up,
    w_down,
    w_router,
    w_mix,
    w_exp_up,
    w_exp_down,
    routes,
    segments,
    cotangent,
):
    own_rows = tokens.shape[0]
    model_width = tokens.shape[1]
    tensor_size = lax.axis_size("tensor")
    tensor_rank = lax.axis_index("tensor")
    owner_count = lax.axis_size("expert")
    group_rows = own_rows * tensor_size
    own_start = tensor_rank * own_rows
    own_cols = model_width // tensor_size
    experts_all = w_router.shape[1]
    local_experts = w_exp_up.shape[0]
    capacity = group_rows // experts_all
    slots = experts_all * capacity

    def my_cols(values):
        return lax.dynamic_slice_in_dim(values, tensor_rank * own_cols, own_cols, 1)

    def my_rows(values):
        return lax.dynamic_slice_in_dim(values, own_start, own_rows, 0)

    route_ids = routes[:, 0]
    route_hot = route_ids[:, None] == jnp.arange(experts_all, dtype=jnp.int32)[None, :]
    hot_float = route_hot.astype(f32)
    positions = jnp.arange(group_rows, dtype=jnp.int32)
    before = (positions[None, :] < positions[:, None]).astype(bf16)
    earlier = jnp.dot(before, route_hot.astype(bf16), preferred_element_type=f32)
    slot_index = jnp.sum(earlier * hot_float, axis=1).astype(jnp.int32)
    slot_of = jnp.where(slot_index < capacity, route_ids * capacity + slot_index, slots)
    slot_ids = jnp.arange(slots, dtype=jnp.int32)
    pick_rows = (slot_ids[:, None] == slot_of[None, :]).astype(bf16)
    pick_slots = (slot_of[:, None] == slot_ids[None, :]).astype(bf16)

    def send_slots(cols_mine):
        picked = jnp.dot(pick_rows, cols_mine, preferred_element_type=f32).astype(bf16)
        picked = picked.reshape(owner_count, local_experts * capacity, own_cols)
        arrived = lax.all_to_all(picked, "expert", split_axis=0, concat_axis=0, tiled=True)
        arrived = arrived.reshape(owner_count, local_experts, capacity, own_cols)
        arrived = arrived.transpose(1, 0, 2, 3).reshape(
            local_experts, owner_count * capacity, own_cols
        )
        return gather_pair(arrived, 2)

    def return_slots(partial):
        mine = scatter_pair(partial, 2).astype(bf16)
        mine = mine.reshape(local_experts, owner_count, capacity, own_cols).transpose(1, 0, 2, 3)
        mine = mine.reshape(owner_count, local_experts * capacity, own_cols)
        back = lax.all_to_all(mine, "expert", split_axis=0, concat_axis=0, tiled=True)
        back = back.reshape(slots, own_cols)
        rows = jnp.dot(pick_slots, back, preferred_element_type=f32).astype(bf16)
        return turn_pair(rows).astype(f32)

    token_f32 = tokens.astype(f32)
    normed_one = layer_norm(token_f32, norm1_gain).astype(bf16)
    normed_all = gather_pair(normed_one)
    projected = jnp.einsum("gd,cdk->cgk", normed_all, w_qkv, preferred_element_type=f32).astype(
        bf16
    )
    labels = segments[0]
    attn_heads = attend(labels, projected)
    attn_own = scatter_pair(jnp.dot(attn_heads, w_out, preferred_element_type=f32), 0, f32)
    middle = token_f32 + attn_own
    normed_two = layer_norm(middle, norm2_gain).astype(bf16)
    hidden_all = gather_pair(normed_two)
    cot_all = gather_pair(cotangent)

    gate_w = jnp.concatenate([w_router, w_mix], axis=1)

    def gates(logits, hot):
        router_soft = jax.nn.softmax(logits[:, :experts_all], axis=-1)
        return jax.nn.softmax(logits[:, experts_all:], axis=-1), jnp.sum(
            router_soft * hot, axis=-1
        )

    logits = jnp.dot(hidden_all, gate_w, preferred_element_type=f32)
    mix_all, gate_all = gates(logits, hot_float)

    slots_in = send_slots(my_cols(hidden_all))
    expert_grad_rows = (my_cols(cot_all) * (mix_all[:, 1] * gate_all)[:, None]).astype(bf16)
    grad_slots_in = send_slots(expert_grad_rows)

    pre_up = jnp.dot(hidden_all, w_up, preferred_element_type=f32)
    act_up = jax.nn.gelu(pre_up).astype(bf16)
    dense_part = jnp.dot(act_up, w_down, preferred_element_type=f32)
    dense_own = scatter_pair(dense_part)
    dense_grad_rows = (cot_all * mix_all[:, 0:1]).astype(bf16)
    grad_act_up = jnp.einsum("gd,fd->gf", dense_grad_rows, w_down, preferred_element_type=f32)
    grad_pre_up = gelu_grad(pre_up, grad_act_up).astype(bf16)
    grad_w_down = jnp.einsum("gf,gd->fd", act_up, dense_grad_rows, preferred_element_type=f32)
    grad_w_up = jnp.einsum("gd,gf->df", hidden_all, grad_pre_up, preferred_element_type=f32)
    dense_back = jnp.einsum("gf,df->gd", grad_pre_up, w_up, preferred_element_type=f32)
    dense_back_own = scatter_pair(dense_back)

    pre_exp = jnp.einsum("lsd,ldf->lsf", slots_in, w_exp_up, preferred_element_type=f32)
    act_exp = jax.nn.gelu(pre_exp).astype(bf16)
    out_exp = jnp.einsum("lsf,lfd->lsd", act_exp, w_exp_down, preferred_element_type=f32)
    expert_own = return_slots(out_exp)
    grad_act_exp = jnp.einsum("lsd,lfd->lsf", grad_slots_in, w_exp_down, preferred_element_type=f32)
    grad_pre_exp = gelu_grad(pre_exp, grad_act_exp).astype(bf16)
    grad_slots_out = jnp.einsum("lsf,ldf->lsd", grad_pre_exp, w_exp_up, preferred_element_type=f32)
    grad_expert_own = return_slots(grad_slots_out)
    grad_w_exp_down = jnp.einsum("lsf,lsd->lfd", act_exp, grad_slots_in, preferred_element_type=f32)
    grad_w_exp_up = jnp.einsum("lsd,lsf->ldf", slots_in, grad_pre_exp, preferred_element_type=f32)

    logits_own, hot_own = my_rows(logits), my_rows(hot_float)
    (mix_own, gate_own), gates_pull = jax.vjp(lambda z: gates(z, hot_own), logits_own)
    output = (
        middle + mix_own[:, 0:1] * dense_own + (mix_own[:, 1] * gate_own)[:, None] * expert_own
    ).astype(bf16)
    grad_out = cotangent.astype(f32)
    dense_dot = jnp.sum(grad_out * dense_own, axis=1)
    expert_dot = jnp.sum(grad_out * expert_own, axis=1)
    grad_mix_coef = jnp.stack([dense_dot, gate_own * expert_dot], axis=1)
    (grad_logits,) = gates_pull((grad_mix_coef, mix_own[:, 1] * expert_dot))
    grad_gate_w = lax.dot_general(
        grad_logits,
        normed_two.astype(f32),
        (((0,), (0,)), ((), ())),
        precision=highest,
        preferred_element_type=f32,
    )
    grad_hidden_gate = lax.dot_general(
        grad_logits,
        gate_w.astype(f32),
        (((1,), (1,)), ((), ())),
        precision=highest,
        preferred_element_type=f32,
    )
    grad_hidden_own = dense_back_own + grad_expert_own + grad_hidden_gate
    _, norm_two_pull = jax.vjp(layer_norm, middle, norm2_gain)
    grad_middle_norm, grad_gain2 = norm_two_pull(grad_hidden_own)
    grad_middle = grad_out + grad_middle_norm

    grad_attn_all = gather_pair(grad_middle.astype(bf16))
    grad_w_out = jnp.einsum("gk,gd->kd", attn_heads, grad_attn_all, preferred_element_type=f32)
    grad_heads = jnp.einsum("gd,kd->gk", grad_attn_all, w_out, preferred_element_type=f32).astype(
        bf16
    )
    grad_qkv = attend_back(labels, projected, grad_heads)
    grad_w_qkv = jnp.einsum("gd,cgk->cdk", normed_all, grad_qkv, preferred_element_type=f32)
    grad_normed_one = scatter_pair(
        jnp.einsum("cgk,cdk->gd", grad_qkv, w_qkv, preferred_element_type=f32)
    )
    _, norm_one_pull = jax.vjp(layer_norm, token_f32, norm1_gain)
    grad_token_norm, grad_gain1 = norm_one_pull(grad_normed_one)
    grad_tokens = grad_middle + grad_token_norm

    wide = [g.astype(bf16) for g in (grad_w_qkv, grad_w_out, grad_w_up, grad_w_down)]
    small = jnp.concatenate([grad_gain1[None], grad_gain2[None], grad_gate_w], axis=0)
    if owner_count == 16 and tensor_size == 2:
        padding = -small.shape[0] % 8
        *wide, small = sum_over_experts(wide, jnp.pad(small, ((0, padding), (0, 0))))
    else:
        wide = lax.psum(wide, "expert")
        small = lax.psum(small, ("expert", "tensor"))
    grad_w_qkv, grad_w_out, grad_w_up, grad_w_down = (g.astype(f32) for g in wide)
    return (
        output,
        grad_tokens,
        small[0],
        grad_w_qkv,
        grad_w_out,
        small[1],
        grad_w_up,
        grad_w_down,
        small[2 : 2 + experts_all].T,
        small[2 + experts_all : 4 + experts_all].T,
        grad_w_exp_up,
        grad_w_exp_down,
    )


def solution(mesh):
    return jax.shard_map(
        body,
        mesh=mesh,
        in_specs=(
            P(("expert", "tensor"), None),
            P(),
            P(None, None, "tensor"),
            P("tensor", None),
            P(),
            P(None, "tensor"),
            P("tensor", None),
            P(),
            P(),
            P("expert", None, "tensor"),
            P("expert", "tensor", None),
            P("expert", None),
            P("expert", None),
            P(("expert", "tensor"), None),
        ),
        out_specs=(
            P(("expert", "tensor"), None),
            P(("expert", "tensor"), None),
            P(),
            P(None, None, "tensor"),
            P("tensor", None),
            P(),
            P(None, "tensor"),
            P("tensor", None),
            P(),
            P(),
            P("expert", None, "tensor"),
            P("expert", "tensor", None),
        ),
        check_vma=False,
    )
```

```python
import functools

import jax
import jax.numpy as jnp
from jax import lax
from jax.experimental import pallas as pl
from jax.experimental.pallas import tpu as pltpu
from jax.sharding import PartitionSpec as P

HEAD = 64
PROMPT = 512
BLOCK = 256
LANES = 128
PIECE = 256
MASKED = -1e30

epsilon = 1e-05
highest = lax.Precision.HIGHEST
f32 = jnp.float32
bf16 = jnp.bfloat16


def layer_norm(values, norm_gain):
    centred = values - jnp.mean(values, axis=-1, keepdims=True)
    variance = jnp.mean(centred * centred, axis=-1, keepdims=True)
    return centred * lax.rsqrt(variance + epsilon) * norm_gain


def gelu_grad(pre_act, upstream):
    return jax.vjp(jax.nn.gelu, pre_act)[1](upstream)[0]


def nt_dot(left, right):
    return lax.dot_general(left, right, (((1,), (1,)), ((), ())), preferred_element_type=f32)


def nn_dot(left, right):
    return lax.dot_general(left, right, (((1,), (0,)), ((), ())), preferred_element_type=f32)


def tn_dot(left, right):
    return lax.dot_general(left, right, (((0,), (0,)), ((), ())), preferred_element_type=f32)


def fill_bias(row_labels_ref, col_labels_ref, cont_bias, tri_bias, transposed):
    size = cont_bias.shape[0]
    down = lax.broadcasted_iota(jnp.int32, (size, size), 0)
    across = lax.broadcasted_iota(jnp.int32, (size, size), 1)
    ordered = (down <= across) if transposed else (across <= down)
    same = row_labels_ref[...] == col_labels_ref[...]
    cont_bias[...] = jnp.where(ordered & same, 0.0, MASKED)
    down = lax.broadcasted_iota(jnp.int32, (BLOCK, BLOCK), 0)
    across = lax.broadcasted_iota(jnp.int32, (BLOCK, BLOCK), 1)
    ordered = (down <= across) if transposed else (across <= down)
    tri_bias[...] = jnp.where(ordered, 0.0, MASKED)


def head_lanes(half):
    lane = lax.broadcasted_iota(jnp.int32, (1, LANES), 1)
    return (lane < HEAD) if half == 0 else (lane >= HEAD)


def turned(pair):
    return lax.axis_index("tensor") if pair else 0


def attend_kernel(pair, col_ref, row_ref, qp, qc, kp, kc, vp, vc, o_ref, cont_bias, tri_bias):
    @pl.when(pl.program_id(0) == 0)
    def _():
        fill_bias(col_ref, row_ref, cont_bias, tri_bias, False)

    turn = turned(pair)
    scale = HEAD**-0.5
    for part in range(2):
        for inner in range(0, PROMPT, BLOCK):
            upto = inner + BLOCK
            mixed = []
            for half in range(2):
                source = (qc if part else qp)[inner:upto, :]
                query = jnp.where(head_lanes(half), source * scale, 0.0).astype(bf16)
                pieces = []
                if part:
                    pieces.append((kp[...], vp[...], None))
                    pieces.append((kc[:upto, :], vc[:upto, :], cont_bias[inner:upto, :upto]))
                else:
                    if inner:
                        pieces.append((kp[:inner, :], vp[:inner, :], None))
                    pieces.append((kp[inner:upto, :], vp[inner:upto, :], tri_bias[...]))
                scores = []
                for key, _, bias in pieces:
                    score = nt_dot(query, key)
                    scores.append(score if bias is None else score + bias)
                top = functools.reduce(
                    jnp.maximum, [jnp.max(score, axis=1, keepdims=True) for score in scores]
                )
                total, out = 0.0, 0.0
                for score, (_, value, _) in zip(scores, pieces, strict=True):
                    weights = jnp.exp(score - top)
                    total = total + jnp.sum(weights, axis=1, keepdims=True)
                    out = out + nn_dot(weights.astype(bf16), value)
                mixed.append(out / total)
            which = (1 - turn) if part else turn
            o_ref[which, inner:upto, :] = jnp.where(head_lanes(0), mixed[0], mixed[1]).astype(bf16)


def attend_back_part(
    part, pair, qp, qc, kp, kc, vp, vc, gp, gc, d_ref, cont_bias, tri_bias, *accs
):
    turn = turned(pair)
    scale = HEAD**-0.5
    dkp, dkc, dvp, dvc = accs
    for inner in range(0, PROMPT, BLOCK):
        upto = inner + BLOCK
        dq = 0.0
        for half in range(2):
            lanes = head_lanes(half)
            query = jnp.where(lanes, (qc if part else qp)[inner:upto, :] * scale, 0.0)
            query = query.astype(bf16)
            grad = jnp.where(lanes, (gc if part else gp)[inner:upto, :], 0.0).astype(bf16)
            if part:
                pieces = [(kp, vp, dkp, dvp, 0, PROMPT, None)]
                pieces.append((kc, vc, dkc, dvc, 0, upto, cont_bias[:upto, inner:upto]))
            else:
                pieces = [(kp, vp, dkp, dvp, 0, inner, None)] if inner else []
                pieces.append((kp, vp, dkp, dvp, inner, upto, tri_bias[...]))
            scores = []
            for key, _, _, _, at, end, bias in pieces:
                score = nt_dot(key[at:end, :], query)
                scores.append(score if bias is None else score + bias)
            top = functools.reduce(
                jnp.maximum, [jnp.max(score, axis=0, keepdims=True) for score in scores]
            )
            scores = [jnp.exp(score - top) for score in scores]
            total = sum(jnp.sum(score, axis=0, keepdims=True) for score in scores)
            scores = [score * (1.0 / total) for score in scores]
            grads = [
                nt_dot(value[at:end, :], grad) for _, value, _, _, at, end, _ in pieces
            ]
            row_dot = sum(
                jnp.sum(score * up, axis=0, keepdims=True)
                for score, up in zip(scores, grads, strict=True)
            )
            for score, up, (key, _, dk, dv, at, end, _) in zip(
                scores, grads, pieces, strict=True
            ):
                grad_scores = (score * (up - row_dot)).astype(bf16)
                dv[at:end, :] += nn_dot(score.astype(bf16), grad)
                dk[at:end, :] += nn_dot(grad_scores, query)
                masked = jnp.where(lanes, key[at:end, :] * scale, 0.0).astype(bf16)
                dq = dq + tn_dot(grad_scores, masked)
        which = (1 - turn) if part else turn
        d_ref[0, which, inner:upto, :] = dq.astype(bf16)


def attend_back_phases(pair, step, col_ref, row_ref, *refs):
    qp, qc, kp, kc, vp, vc, gp, gc, d_ref, cont_bias, tri_bias, *accs = refs

    def prompt():
        @pl.when(step == 0)
        def _():
            fill_bias(col_ref, row_ref, cont_bias, tri_bias, True)

        for acc in accs:
            acc[...] = jnp.zeros_like(acc)
        attend_back_part(0, pair, *refs)

    def continuations():
        attend_back_part(1, pair, *refs)
        turn = turned(pair)
        for number, acc in enumerate(accs):
            which = (1 - turn) if number % 2 else turn
            d_ref[1 + number // 2, which] = acc[...].astype(bf16)

    return [prompt, continuations]


def attend_back_kernel(pair, *refs):
    for phase in attend_back_phases(pair, pl.program_id(0), *refs):
        phase()


def half_specs(size, lead, pair):
    blank = (pl.Squeezed(),) * (1 if lead is None else 2)

    def spec(cont):
        def index(i):
            half = 1 - turned(pair) if cont else turned(pair)
            return (half, 0, i) if lead is None else (lead, half, 0, i)

        return pl.BlockSpec((*blank, size, LANES), index)

    return [spec(False), spec(True)]


def attend_call(kernel, name, labels, projected, grad_heads, dots, accs, ride=None):
    rows, cols = projected.shape[1:]
    cont = rows - PROMPT
    pair = paired()
    kernel = functools.partial(kernel, pair)
    halves = projected.reshape(3, 2, PROMPT, cols)
    work = 2 * rows * rows * cols * dots
    back = grad_heads is not None
    lead = (3,) if back else ()
    specs = [s for c in range(3) for s in half_specs(PROMPT, c, pair)]
    args = [halves] * 6
    if back:
        specs += half_specs(PROMPT, None, pair)
        args += [grad_heads.reshape(2, PROMPT, cols)] * 2
    specs = [
        pl.BlockSpec((cont, 1), lambda i: (0, 0)),
        pl.BlockSpec((1, cont), lambda i: (0, 0)),
        *specs,
    ]
    out_spec = pl.BlockSpec(
        (*lead, 2, PROMPT, LANES), lambda i: (*(0 for _ in lead), 0, 0, i)
    )
    out_shape = jax.ShapeDtypeStruct((*lead, 2, PROMPT, cols), bf16)
    scratch = [
        pltpu.VMEM((cont, cont), f32),
        pltpu.VMEM((BLOCK, BLOCK), f32),
        *[pltpu.VMEM((PROMPT, LANES), f32)] * accs,
    ]
    args = [labels[:, None], labels[None, :], *args]
    steps = cols // LANES
    if ride is not None:
        out, state = carry(
            kernel,
            steps,
            specs,
            [out_spec],
            [out_shape],
            scratch,
            args,
            [ride],
            [None],
            name,
            work,
            3,
        )
        return out.reshape(*lead, rows, cols), state
    out = pl.pallas_call(
        kernel,
        grid=(steps,),
        in_specs=specs,
        out_specs=out_spec,
        scratch_shapes=scratch,
        out_shape=out_shape,
        cost_estimate=pl.CostEstimate(
            flops=work, bytes_accessed=14 * rows * cols, transcendentals=rows * rows * 4
        ),
        name=name,
    )(*args)
    return out.reshape(*lead, rows, cols)


def attend(labels, projected):
    return attend_call(attend_kernel, "attend", labels, projected, None, 2, 0)


def attend_back(labels, projected, grad_heads, ride=None):
    kernel = attend_back_kernel if ride is None else attend_back_phases
    return attend_call(
        kernel, "attend_back", labels, projected, grad_heads, 5, 4, ride
    )


HIDDEN = 512
ROWS = 512
CUT = 256


def gelu_both(pre_act):
    slope = 0.7978845608028654
    square = pre_act * pre_act
    bend = jnp.tanh(slope * (pre_act + 0.044715 * (square * pre_act)))
    share = 0.5 * (1.0 + bend)
    steep = 0.5 * slope * (1.0 + (3 * 0.044715) * square)
    return pre_act * share, share + pre_act * (1.0 - bend * bend) * steep


def feed_rows(first, at, x_ref, dy_ref, wu_ref, wd_ref, act, dact, y_acc, dx_acc):
    pre_act = nn_dot(x_ref[at, :], wu_ref[...])
    up = nt_dot(dy_ref[at, :], wd_ref[...])
    value, slope = gelu_both(pre_act)
    value = value.astype(bf16)
    back = (up * slope).astype(bf16)
    act[at, :] = value
    dact[at, :] = back
    out = nn_dot(value, wd_ref[...])
    grad = nt_dot(back, wu_ref[...])

    @pl.when(first)
    def _():
        y_acc[at, :] = out
        dx_acc[at, :] = grad

    @pl.when(jnp.logical_not(first))
    def _():
        y_acc[at, :] += out
        dx_acc[at, :] += grad


def feed_down(x_ref, dy_ref, act, dact, gu_ref, gd_ref):
    for at in range(0, gd_ref.shape[0], CUT):
        gd_ref[at : at + CUT, :] = tn_dot(act[:, at : at + CUT], dy_ref[...]).astype(gd_ref.dtype)


def feed_up(x_ref, dy_ref, act, dact, gu_ref, gd_ref):
    for at in range(0, gu_ref.shape[0], CUT):
        gu_ref[at : at + CUT, :] = tn_dot(x_ref[:, at : at + CUT], dact[...]).astype(gu_ref.dtype)


def feed_kernel(x_ref, dy_ref, wu_ref, wd_ref, *refs):
    yk, ya, dxk, dxa, gu_ref, gd_ref, act, dact, y_acc, dx_acc = refs
    step = pl.program_id(0)
    for at in range(0, x_ref.shape[0], ROWS):
        rows = slice(at, at + ROWS)
        feed_rows(step == 0, rows, x_ref, dy_ref, wu_ref, wd_ref, act, dact, y_acc, dx_acc)
    feed_down(x_ref, dy_ref, act, dact, gu_ref, gd_ref)
    feed_up(x_ref, dy_ref, act, dact, gu_ref, gd_ref)

    @pl.when(step == pl.num_programs(0) - 1)
    def _():
        half = yk.shape[0]
        yk[...] = y_acc[:half, :]
        dxk[...] = dx_acc[:half, :]
        ya[...] = y_acc[half:, :].astype(bf16)
        dxa[...] = dx_acc[half:, :].astype(bf16)


def one_buffer(shape):
    return pl.BlockSpec(shape, lambda *_: (0,) * len(shape), pipeline_mode=pl.Buffered(1))


def feed_forward(x, dy, w_up, w_down):
    rows, width = x.shape
    hidden = w_up.shape[1]
    tile = min(HIDDEN, hidden)
    half = rows // 2
    block = jax.ShapeDtypeStruct((half, width), f32)
    sent = jax.ShapeDtypeStruct((half, width), bf16)
    return pl.pallas_call(
        feed_kernel,
        grid=(hidden // tile,),
        in_specs=[
            one_buffer((rows, width)),
            one_buffer((rows, width)),
            pl.BlockSpec((width, tile), lambda i: (0, i)),
            pl.BlockSpec((tile, width), lambda i: (i, 0)),
        ],
        out_specs=[
            *[one_buffer((half, width))] * 4,
            pl.BlockSpec((width, tile), lambda i: (0, i)),
            pl.BlockSpec((tile, width), lambda i: (i, 0)),
        ],
        out_shape=[
            block,
            sent,
            block,
            sent,
            jax.ShapeDtypeStruct((width, hidden), bf16),
            jax.ShapeDtypeStruct((hidden, width), bf16),
        ],
        scratch_shapes=[
            pltpu.VMEM((rows, tile), bf16),
            pltpu.VMEM((rows, tile), bf16),
            pltpu.VMEM((rows, width), f32),
            pltpu.VMEM((rows, width), f32),
        ],
        compiler_params=pltpu.CompilerParams(vmem_limit_bytes=56 * 1024 * 1024),
        cost_estimate=pl.CostEstimate(
            flops=12 * rows * width * hidden,
            bytes_accessed=8 * width * hidden + 12 * rows * width,
            transcendentals=rows * hidden,
        ),
        name="feed_forward",
    )(x, dy, w_up, w_down)


ORDERS = ((1, 2, 4, 8), (2, 4, 1, 8), (4, 1, 2, 8))
DEPTH = 4
MESH = pl.DeviceIdType.MESH


def partner_of(bit):
    me = lax.axis_index("expert")
    side = lax.rem(me // bit, 2)
    return me + bit * (1 - 2 * side), side


def greet(core):
    barrier = pltpu.get_barrier_semaphore()
    for bit in sorted(ORDERS[0]):
        pl.semaphore_signal(
            barrier, 1, device_id={"expert": partner_of(bit)[0]}, device_id_type=MESH
        )
    if core:
        other = 1 - lax.axis_index("tensor")
        pl.semaphore_signal(barrier, 1, device_id={"tensor": other}, device_id_type=MESH)
    pl.semaphore_wait(barrier, DEPTH + core)


class Ride:
    def __init__(self, level_in, level_out, values, layout, width, counts):
        self.first, self.last = level_in, level_out
        self.values, self.layout, self.width, self.counts = list(values), layout, width, counts
        self.pieces = sum(map(len, layout))
        self.where = [(a, piece) for a, pieces in enumerate(layout) for piece in pieces]
        self.ticks = max(counts) + level_out - level_in

    def rows_at(self, level):
        return PIECE >> (level if level <= DEPTH else 2 * DEPTH - level)

    def out_shape(self, shapes):
        if self.last < 2 * DEPTH:
            shapes = [(self.pieces, self.rows_at(self.last), self.width)]
        return [jax.ShapeDtypeStruct(shape, bf16) for shape in shapes]

    def scratch(self):
        shapes = []
        if self.first < DEPTH:
            shapes.append(self.rows_at(self.first))
            shapes += [self.rows_at(n + 1) for n in range(self.first, min(self.last, DEPTH))]
        if self.last > DEPTH:
            shapes.append(self.rows_at(self.last))
        hops = self.last - self.first
        return [
            *[pltpu.VMEM((self.pieces, rows, self.width), bf16) for rows in shapes],
            pltpu.SemaphoreType.DMA((hops, self.pieces)),
            pltpu.SemaphoreType.DMA((hops, self.pieces)),
            pltpu.SemaphoreType.DMA((self.pieces,)),
            pltpu.SemaphoreType.DMA((self.pieces,)),
        ]

    def bind(self, ins, outs, scratch):
        self.ins, self.outs = ins, outs
        *buffers, self.send_sem, self.recv_sem, self.load_sem, self.store_sem = scratch
        self.held = buffers[0] if self.first < DEPTH else None
        self.got = buffers[1 : 1 + max(0, min(self.last, DEPTH) - self.first)]
        self.full = buffers[-1] if self.last > DEPTH else None
        self.sides = {bit: partner_of(bit) for bit in ORDERS[0]}

    def held_at(self, order, level):
        total = 0
        for n in range(self.first, level):
            total = total + self.sides[order[n]][1] * self.rows_at(n + 1)
        return pl.multiple_of(total, 16)

    def full_at(self, order, level):
        total = 0
        for n in range(2 * DEPTH - self.last, 2 * DEPTH - level):
            total = total + self.sides[order[n]][1] * self.rows_at(n + 1)
        return pl.multiple_of(total, 16)

    def color_of(self, piece):
        color = 0
        while piece >= sum(self.counts[: color + 1]):
            color += 1
        return color

    def load(self, piece):
        sem = self.load_sem.at[piece]
        if self.first == 0:
            a, parts = self.where[piece]
            return [
                pltpu.make_async_copy(self.ins[a].at[src], self.held.at[(piece, *dst)], sem)
                for src, dst in parts
            ]
        if self.first < DEPTH:
            return [pltpu.make_async_copy(self.ins[0].at[piece], self.held.at[piece], sem)]
        order = ORDERS[self.color_of(piece)]
        at = pl.ds(self.full_at(order, self.first), self.rows_at(self.first))
        return [pltpu.make_async_copy(self.ins[0].at[piece], self.full.at[piece, at], sem)]

    def await_load(self, order, piece):
        sem = self.load_sem.at[piece]
        if self.first < DEPTH:
            whole = self.held.at[piece]
        else:
            at = pl.ds(self.full_at(order, self.first), self.rows_at(self.first))
            whole = self.full.at[piece, at]
        pltpu.make_async_copy(whole, whole, sem).wait()

    def stores(self, piece):
        sem = self.store_sem.at[piece]
        if self.last == 2 * DEPTH:
            a, parts = self.where[piece]
            return [
                pltpu.make_async_copy(self.full.at[(piece, *dst)], self.outs[a].at[src], sem)
                for src, dst in parts
            ]
        if self.last > DEPTH:
            return [pltpu.make_async_copy(self.full.at[piece], self.outs[0].at[piece], sem)]
        order = ORDERS[self.color_of(piece)]
        at = pl.ds(self.held_at(order, self.last), self.rows_at(self.last))
        return [pltpu.make_async_copy(self.held.at[piece, at], self.outs[0].at[piece], sem)]

    def start_store(self, order, piece):
        if self.last == 2 * DEPTH:
            for number in range(self.pieces):

                @pl.when(piece == number)
                def _(number=number):
                    for copy in self.stores(number):
                        copy.start()

            return
        sem = self.store_sem.at[piece]
        if self.last > DEPTH:
            source = self.full.at[piece]
        else:
            at = pl.ds(self.held_at(order, self.last), self.rows_at(self.last))
            source = self.held.at[piece, at]
        pltpu.make_async_copy(source, self.outs[0].at[piece], sem).start()

    def exchange(self, order, hop, piece):
        sems = (self.send_sem.at[hop - self.first, piece], self.recv_sem.at[hop - self.first, piece])
        if hop < DEPTH:
            target, side = self.sides[order[hop]]
            size = self.rows_at(hop + 1)
            away = pl.multiple_of(self.held_at(order, hop) + (1 - side) * size, 16)
            source = self.held.at[piece, pl.ds(away, size)]
            dest = self.got[hop - self.first].at[piece]
        else:
            target, _ = self.sides[order[2 * DEPTH - 1 - hop]]
            at = pl.ds(self.full_at(order, hop), self.rows_at(hop))
            source = dest = self.full.at[piece, at]
        return pltpu.make_async_remote_copy(
            source, dest, *sems, device_id={"expert": target}, device_id_type=MESH
        )

    def run(self, color, stage, piece):
        order = ORDERS[color]
        if stage == 0:
            self.await_load(order, piece)
        else:
            hop = self.first + stage - 1
            self.exchange(order, hop, piece).wait()
            if hop < DEPTH:
                size = self.rows_at(hop + 1)
                at = pl.ds(self.held_at(order, hop + 1), size)
                total = self.held[piece, at, :].astype(f32)
                total = (total + self.got[hop - self.first][piece].astype(f32)).astype(bf16)
                if hop + 1 == DEPTH and self.last > DEPTH:
                    self.full[piece, pl.ds(self.full_at(order, DEPTH), size), :] = total
                else:
                    self.held[piece, at, :] = total
        if self.first + stage < self.last:
            self.exchange(order, self.first + stage, piece).start()
        else:
            self.start_store(order, piece)

    def begin(self):
        for piece in range(self.pieces):
            for copy in self.load(piece):
                copy.start()

    def tick(self, t):
        for stage in range(self.last - self.first + 1):
            for color, count in enumerate(self.counts):

                @pl.when((t >= stage) & (t - stage < count))
                def _(color=color, stage=stage):
                    self.run(color, stage, sum(self.counts[:color]) + t - stage)

    def end(self):
        for piece in range(self.pieces):
            for copy in self.stores(piece):
                copy.wait()


def carry(
    phases, steps, specs, out_specs, out_shape, scratch, args, rides, out_shapes, name, flops, collective
):
    n_ticks = max(ride.ticks for ride in rides)
    ride_outs = [ride.out_shape(shapes) for ride, shapes in zip(rides, out_shapes, strict=True)]
    parts = 2
    grid = max(steps, -(-n_ticks // parts))

    def clamp(spec):
        if spec.index_map is None:
            return spec
        return pl.BlockSpec(
            spec.block_shape,
            lambda i: spec.index_map(jnp.minimum(i, steps - 1)),
            pipeline_mode=spec.pipeline_mode,
        )

    any_spec = pl.BlockSpec(memory_space=pl.ANY)
    n_in, n_out = len(args), len(out_shape)

    def kernel(*refs):
        refs = list(refs)
        take = lambda count: [refs.pop(0) for _ in range(count)]
        main_in = take(n_in)
        ins = [take(len(ride.values)) for ride in rides]
        main_out = take(n_out)
        outs = [take(len(shapes)) for shapes in ride_outs]
        main_scratch = take(len(scratch))
        for ride, got, out in zip(rides, ins, outs, strict=True):
            ride.bind(got, out, take(len(ride.scratch())))
        step = pl.program_id(0)

        @pl.when(step == 0)
        def _():
            for ride in rides:
                ride.begin()
            greet(False)

        for number, phase in enumerate(phases(step, *main_in, *main_out, *main_scratch)):
            for ride in rides:
                ride.tick(step * parts + number)
            pl.when(step < steps)(phase)

        @pl.when(step == grid - 1)
        def _():
            for ride in rides:
                ride.end()

    moved = sum(v.size for ride in rides for v in ride.values)
    return pl.pallas_call(
        kernel,
        grid_spec=pltpu.PrefetchScalarGridSpec(
            num_scalar_prefetch=0,
            grid=(grid,),
            in_specs=[*map(clamp, specs), *[any_spec] * sum(len(ride.values) for ride in rides)],
            out_specs=[*map(clamp, out_specs), *[any_spec] * sum(map(len, ride_outs))],
            scratch_shapes=[*scratch, *[m for ride in rides for m in ride.scratch()]],
        ),
        out_shape=[*out_shape, *[shape for shapes in ride_outs for shape in shapes]],
        compiler_params=pltpu.CompilerParams(
            collective_id=collective, has_side_effects=True, vmem_limit_bytes=62 * 1024 * 1024
        ),
        cost_estimate=pl.CostEstimate(flops=flops, bytes_accessed=4 * moved, transcendentals=0),
        name=name,
    )(*args, *[v for ride in rides for v in ride.values])


def split_layout(shapes, width):
    layout = []
    for shape in shapes:
        pieces = []
        leads = [(c,) for c in range(shape[0])] if len(shape) == 3 else [()]
        for lead in leads:
            for c in range(0, shape[-1], width):
                for r in range(0, shape[-2], PIECE):
                    pieces.append([((*lead, slice(r, r + PIECE), slice(c, c + width)), ())])
        layout.append(pieces)
    return layout


def last_kernel(rides, small_in, *refs):
    refs = list(refs)
    take = lambda count: [refs.pop(0) for _ in range(count)]
    ins = [take(len(ride.values)) for ride in rides]
    (small_out,) = take(1)
    outs = [take(count) for count in [2] * len(rides)]
    small, small_got, small_sem = take(3)
    for ride, got, out in zip(rides, ins, outs, strict=True):
        ride.bind(got, out, take(len(ride.scratch())))
    bits = sorted(ORDERS[0])

    def small_copy(step):
        if step < DEPTH:
            target = {"expert": partner_of(bits[step])[0]}
        else:
            target = {"tensor": 1 - lax.axis_index("tensor")}
        return pltpu.make_async_remote_copy(
            small.at[step],
            small_got.at[step],
            small_sem.at[0, step],
            small_sem.at[1, step],
            device_id=target,
            device_id_type=MESH,
        )

    for ride in rides:
        ride.begin()
    first = pltpu.make_async_copy(small_in, small.at[0], small_sem.at[2, 0])
    first.start()
    greet(True)

    def step(t, _):
        for ride in rides:
            ride.tick(t)
        for number in range(DEPTH + 2):

            @pl.when(t == number)
            def _(number=number):
                if number == 0:
                    first.wait()
                else:
                    small_copy(number - 1).wait()
                    small[number] = small[number - 1] + small_got[number - 1]
                if number < DEPTH + 1:
                    small_copy(number).start()

        return 0

    lax.fori_loop(0, max(ride.ticks for ride in rides), step, 0)
    out = pltpu.make_async_copy(small.at[DEPTH + 1], small_out, small_sem.at[2, 1])
    out.start()
    for ride in rides:
        ride.end()
    out.wait()


def alone_kernel(ride, *refs):
    count = len(ride.values)
    ride.bind(refs[:count], refs[count : count + 1], refs[count + 1 :])
    ride.begin()
    greet(False)

    def step(t, _):
        ride.tick(t)
        return 0

    lax.fori_loop(0, ride.ticks, step, 0)
    ride.end()


def ride_alone(ride, collective):
    any_spec = pl.BlockSpec(memory_space=pl.ANY)
    return pl.pallas_call(
        functools.partial(alone_kernel, ride),
        in_specs=[any_spec] * len(ride.values),
        out_specs=[any_spec],
        out_shape=ride.out_shape(None),
        scratch_shapes=ride.scratch(),
        compiler_params=pltpu.CompilerParams(
            collective_id=collective, has_side_effects=True, vmem_limit_bytes=62 * 1024 * 1024
        ),
        name="ride_alone",
    )(*ride.values)


def last_sums(rides, out_shapes, small):
    any_spec = pl.BlockSpec(memory_space=pl.ANY)
    ride_outs = [ride.out_shape(shapes) for ride, shapes in zip(rides, out_shapes, strict=True)]
    values = [v for ride in rides for v in ride.values]
    shapes = [shape for shapes in ride_outs for shape in shapes]
    return pl.pallas_call(
        functools.partial(last_kernel, rides),
        in_specs=[any_spec] * (1 + len(values)),
        out_specs=[any_spec] * (1 + len(shapes)),
        out_shape=[jax.ShapeDtypeStruct(small.shape, f32), *shapes],
        scratch_shapes=[
            pltpu.VMEM((DEPTH + 2, *small.shape), f32),
            pltpu.VMEM((DEPTH + 1, *small.shape), f32),
            pltpu.SemaphoreType.DMA((3, DEPTH + 1)),
            *[m for ride in rides for m in ride.scratch()],
        ],
        compiler_params=pltpu.CompilerParams(
            collective_id=4, has_side_effects=True, vmem_limit_bytes=62 * 1024 * 1024
        ),
        name="last_sums",
    )(small, *values)


def expert_data_phases(steps, step, x_ref, dy_ref, wu_ref, wd_ref, *refs):
    keep, away, act, dact, y_acc, dx_acc = refs
    halves = x_ref.shape[0] // 2
    width = x_ref.shape[1]

    def rows(number):
        at = slice(number * halves, (number + 1) * halves)
        feed_rows(step == 0, at, x_ref, dy_ref, wu_ref, wd_ref, act, dact, y_acc, dx_acc)

    def finish():
        rows(1)
        half = width // 2
        for side in range(2):

            @pl.when((step == steps - 1) & (lax.axis_index("tensor") == side))
            def _(side=side):
                own = slice(side * half, (side + 1) * half)
                other = slice((1 - side) * half, (2 - side) * half)
                keep[:, :half] = y_acc[:, own]
                keep[:, half:] = dx_acc[:, own]
                away[:, :half] = y_acc[:, other].astype(bf16)
                away[:, half:] = dx_acc[:, other].astype(bf16)

    return [functools.partial(rows, 0), finish]


def expert_data(x, dy, w_up, w_down, ride):
    rows, width = x.shape
    hidden = w_up.shape[1]
    tile = min(HIDDEN, hidden)
    steps = hidden // tile
    inner = jax.ShapeDtypeStruct((rows, hidden), bf16)
    return carry(
        functools.partial(expert_data_phases, steps),
        steps,
        [
            one_buffer((rows, width)),
            one_buffer((rows, width)),
            pl.BlockSpec((width, tile), lambda i: (0, i)),
            pl.BlockSpec((tile, width), lambda i: (i, 0)),
        ],
        [
            *[one_buffer((rows, width))] * 2,
            *[pl.BlockSpec((rows, tile), lambda i: (0, i))] * 2,
        ],
        [
            jax.ShapeDtypeStruct((rows, width), f32),
            jax.ShapeDtypeStruct((rows, width), bf16),
            inner,
            inner,
        ],
        [pltpu.VMEM((rows, width), f32)] * 2,
        [x, dy, w_up, w_down],
        [ride],
        [None],
        "expert_data",
        8 * rows * width * hidden,
        1,
    )


def expert_weights_kernel(*refs):
    feed_down(*refs)
    feed_up(*refs)


def expert_weights(x, dy, act, dact):
    rows, width = x.shape
    hidden = act.shape[1]
    tile = min(HIDDEN, hidden)
    return pl.pallas_call(
        expert_weights_kernel,
        grid=(hidden // tile,),
        in_specs=[
            one_buffer((rows, width)),
            one_buffer((rows, width)),
            *[pl.BlockSpec((rows, tile), lambda i: (0, i))] * 2,
        ],
        out_specs=[
            pl.BlockSpec((width, tile), lambda i: (0, i)),
            pl.BlockSpec((tile, width), lambda i: (i, 0)),
        ],
        out_shape=[
            jax.ShapeDtypeStruct((width, hidden), f32),
            jax.ShapeDtypeStruct((hidden, width), f32),
        ],
        compiler_params=pltpu.CompilerParams(vmem_limit_bytes=56 * 1024 * 1024),
        cost_estimate=pl.CostEstimate(
            flops=4 * rows * width * hidden,
            bytes_accessed=8 * width * hidden + 4 * rows * width + 4 * rows * hidden,
            transcendentals=0,
        ),
        name="expert_weights",
    )(x, dy, act, dact)


def paired():
    return lax.axis_size("tensor") == 2


def swap(values):
    return lax.ppermute(values, "tensor", [(0, 1), (1, 0)])


def gather_rows(own):
    if paired():
        return jnp.concatenate([own, swap(own)], axis=0)
    return lax.all_gather(own, "tensor", axis=0, tiled=True)


def scatter_rows(partial, kind=bf16):
    if paired():
        size = partial.shape[0] // 2
        return partial[:size] + swap(partial[size:].astype(kind)).astype(f32)
    return lax.psum_scatter(
        partial.astype(kind), "tensor", scatter_dimension=0, tiled=True
    ).astype(f32)


def own_rows_of(values):
    size = values.shape[0] // lax.axis_size("tensor")
    if paired():
        return values[:size]
    return lax.dynamic_slice_in_dim(values, lax.axis_index("tensor") * size, size, 0)


def local_order(values):
    if paired():
        size = values.shape[0] // 2
        turned = jnp.concatenate([values[size:], values[:size]], axis=0)
        return jnp.where(lax.axis_index("tensor") == 0, values, turned)
    return values


def scatter_cols(partial):
    size = partial.shape[1] // lax.axis_size("tensor")
    rank = lax.axis_index("tensor")
    if paired():
        keep = lax.dynamic_slice_in_dim(partial, rank * size, size, 1)
        away = lax.dynamic_slice_in_dim(partial, (1 - rank) * size, size, 1).astype(bf16)
        return (keep + swap(away).astype(f32)).astype(bf16)
    return lax.psum_scatter(partial.astype(bf16), "tensor", scatter_dimension=1, tiled=True)


def turn_pair(cols_mine, count):
    width = cols_mine.shape[1] // count
    if not paired():
        return [
            lax.all_to_all(cols_mine[:, at : at + width], "tensor", 0, 1, tiled=True)
            for at in range(0, count * width, width)
        ]
    size = cols_mine.shape[0] // 2
    own, other = cols_mine[:size], swap(cols_mine[size:])
    first = lax.axis_index("tensor") == 0
    left, right = jnp.where(first, own, other), jnp.where(first, other, own)
    return [
        jnp.concatenate([left[:, at : at + width], right[:, at : at + width]], axis=1)
        for at in range(0, count * width, width)
    ]


def join_kernel(own_ref, other_ref, *outs):
    size = own_ref.shape[1] // len(outs)
    rank = lax.axis_index("tensor")
    for side in range(2):

        @pl.when(rank == side)
        def _(side=side):
            for number, out in enumerate(outs):
                cols = slice(number * size, (number + 1) * size)
                out[:, side * size : (side + 1) * size] = own_ref[:, cols]
                out[:, (1 - side) * size : (2 - side) * size] = other_ref[:, cols]


def join_cols(own, count):
    rows, width = own.shape
    if not paired():
        whole = lax.all_gather(own.reshape(rows, count, -1), "tensor", axis=2, tiled=True)
        return [whole[:, number] for number in range(count)]
    step = min(rows, 256)
    outs = [jax.ShapeDtypeStruct((rows, 2 * width // count), own.dtype)] * count
    return pl.pallas_call(
        join_kernel,
        grid=(rows // step,),
        in_specs=[pl.BlockSpec((step, width), lambda i: (i, 0))] * 2,
        out_specs=[pl.BlockSpec((step, 2 * width // count), lambda i: (i, 0))] * count,
        out_shape=outs,
        cost_estimate=pl.CostEstimate(
            flops=0, bytes_accessed=8 * rows * width, transcendentals=0
        ),
        name="join_cols",
    )(own, swap(own))


def body(
    tokens,
    norm1_gain,
    w_qkv,
    w_out,
    norm2_gain,
    w_up,
    w_down,
    w_router,
    w_mix,
    w_exp_up,
    w_exp_down,
    routes,
    segments,
    cotangent,
):
    own_rows = tokens.shape[0]
    model_width = tokens.shape[1]
    tensor_size = lax.axis_size("tensor")
    tensor_rank = lax.axis_index("tensor")
    owner_count = lax.axis_size("expert")
    group_rows = own_rows * tensor_size
    own_cols = model_width // tensor_size
    experts_all = w_router.shape[1]
    local_experts = w_exp_up.shape[0]
    capacity = group_rows // experts_all
    slots = experts_all * capacity
    barrier = lax.optimization_barrier
    special = owner_count == 16 and tensor_size == 2 and local_experts == 1

    def my_cols(values):
        return lax.dynamic_slice_in_dim(values, tensor_rank * own_cols, own_cols, 1)

    route_ids = local_order(routes[:, 0])
    route_hot = route_ids[:, None] == jnp.arange(experts_all, dtype=jnp.int32)[None, :]
    hot_float = route_hot.astype(f32)
    positions = local_order(jnp.arange(group_rows, dtype=jnp.int32))
    before = (positions[None, :] < positions[:, None]).astype(bf16)
    earlier = jnp.dot(before, route_hot.astype(bf16), preferred_element_type=f32)
    slot_index = jnp.sum(earlier * hot_float, axis=1).astype(jnp.int32)
    slot_of = jnp.where(slot_index < capacity, route_ids * capacity + slot_index, slots)
    slot_ids = jnp.arange(slots, dtype=jnp.int32)
    pick_rows = barrier((slot_ids[:, None] == slot_of[None, :]).astype(bf16))
    pick_slots = barrier((slot_of[:, None] == slot_ids[None, :]).astype(bf16))

    def by_expert(values):
        return values.transpose(1, 0, 2, 3).reshape(slots, values.shape[-1])

    def send_slots(cols_mine):
        picked = jnp.dot(pick_rows, cols_mine, preferred_element_type=f32).astype(bf16)
        picked = picked.reshape(owner_count, local_experts * capacity, -1)
        arrived = lax.all_to_all(picked, "expert", split_axis=0, concat_axis=0, tiled=True)
        return by_expert(arrived.reshape(owner_count, local_experts, capacity, -1))

    def return_slots(mine):
        mine = by_expert(mine.reshape(local_experts, owner_count, capacity, -1))
        mine = mine.reshape(owner_count, local_experts * capacity, -1)
        back = lax.all_to_all(mine, "expert", split_axis=0, concat_axis=0, tiled=True)
        return back.reshape(slots, -1)

    def unslot(back):
        rows = jnp.dot(pick_slots, back, preferred_element_type=f32).astype(bf16)
        return [
            whole.astype(f32) for whole in turn_pair(rows, back.shape[1] // own_cols)
        ]

    cot_all = gather_rows(cotangent)
    cot_arrived = send_slots(my_cols(cot_all))
    token_f32 = tokens.astype(f32)
    normed_one = layer_norm(token_f32, norm1_gain).astype(bf16)
    normed_all = gather_rows(normed_one)
    projected = jnp.einsum("gd,cdk->cgk", normed_all, w_qkv, preferred_element_type=f32).astype(
        bf16
    )
    labels = segments[0]
    attn_heads = attend(labels, projected)
    attn_part = jnp.dot(attn_heads, w_out, preferred_element_type=f32)
    attn_part, cot_arrived = barrier((attn_part, cot_arrived))
    attn_own = scatter_rows(attn_part, f32)
    middle = token_f32 + attn_own
    normed_two = layer_norm(middle, norm2_gain).astype(bf16)
    hidden_all = gather_rows(normed_two)

    gate_w = jnp.concatenate([w_router, w_mix], axis=1)

    def gates(logits, hot):
        router_soft = jax.nn.softmax(logits[:, :experts_all], axis=-1)
        return jax.nn.softmax(logits[:, experts_all:], axis=-1), jnp.sum(
            router_soft * hot, axis=-1
        )

    logits = jnp.dot(hidden_all, gate_w, preferred_element_type=f32)
    mix_all, gate_all = gates(logits, hot_float)

    arrived = send_slots(my_cols(hidden_all))
    (cot_slots,) = join_cols(cot_arrived, 1)

    dense_grad_rows = barrier((cot_all * mix_all[:, 0:1]).astype(bf16))
    if special:
        dense_grad_rows, cot_slots = barrier((dense_grad_rows, cot_slots))
        y_keep, y_away, dx_keep, dx_away, grad_w_up, grad_w_down = feed_forward(
            hidden_all, dense_grad_rows, w_up, w_down
        )
        dense_own = y_keep + swap(y_away).astype(f32)
        dense_back_own = dx_keep + swap(dx_away).astype(f32)
    else:
        pre_up = jnp.dot(hidden_all, w_up, preferred_element_type=f32)
        act_up = jax.nn.gelu(pre_up).astype(bf16)
        dense_own = scatter_rows(jnp.dot(act_up, w_down, preferred_element_type=f32))
        grad_act_up = jnp.einsum("gd,fd->gf", dense_grad_rows, w_down, preferred_element_type=f32)
        grad_pre_up = gelu_grad(pre_up, grad_act_up).astype(bf16)
        grad_w_down = jnp.einsum("gf,gd->fd", act_up, dense_grad_rows, preferred_element_type=f32)
        grad_w_up = jnp.einsum("gd,gf->df", hidden_all, grad_pre_up, preferred_element_type=f32)
        dense_back_own = scatter_rows(
            jnp.einsum("gf,df->gd", grad_pre_up, w_up, preferred_element_type=f32)
        )

    arrived, grad_w_up = barrier((arrived, grad_w_up))
    (slots_in,) = join_cols(arrived, 1)
    slot_logits = jnp.dot(slots_in, gate_w, preferred_element_type=f32)
    slot_expert = lax.axis_index("expert") * local_experts + (
        jnp.arange(slots, dtype=jnp.int32) // (owner_count * capacity)
    )
    slot_hot = slot_expert[:, None] == jnp.arange(experts_all, dtype=jnp.int32)[None, :]
    slot_mix, slot_gate = gates(slot_logits, slot_hot.astype(f32))
    grad_slots_in = barrier(
        (cot_slots.astype(f32) * (slot_mix[:, 1] * slot_gate)[:, None]).astype(bf16)
    )

    if special:
        layout = split_layout([grad_w_up.shape, grad_w_down.shape], 1024)
        share = (6, 6, 4)
        keep, away, act_exp, dact_exp, state = expert_data(
            slots_in,
            grad_slots_in,
            w_exp_up[0],
            w_exp_down[0],
            Ride(0, 1, [grad_w_up, grad_w_down], layout, 1024, share),
        )
        mine = (keep + swap(away).astype(f32)).astype(bf16)
        mine, act_exp = barrier((mine, act_exp))
        back = return_slots(mine)
        grad_w_exp_up, grad_w_exp_down = expert_weights(
            slots_in, grad_slots_in, act_exp, dact_exp
        )
        state, grad_w_exp_up = barrier((state, grad_w_exp_up))
        (state,) = ride_alone(Ride(1, 4, [state], layout, 1024, share), 2)
        back, state = barrier((back, state))
        grad_w_exp_up, grad_w_exp_down = grad_w_exp_up[None], grad_w_exp_down[None]
        expert_own, grad_expert_own = unslot(back)
    else:
        slots_in, grad_slots_in = (
            v.reshape(local_experts, owner_count * capacity, model_width)
            for v in (slots_in, grad_slots_in)
        )
        pre_exp = jnp.einsum("lsd,ldf->lsf", slots_in, w_exp_up, preferred_element_type=f32)
        act_exp = jax.nn.gelu(pre_exp).astype(bf16)
        out_exp = jnp.einsum("lsf,lfd->lsd", act_exp, w_exp_down, preferred_element_type=f32)
        (expert_own,) = unslot(return_slots(scatter_cols(out_exp.reshape(slots, model_width))))
        grad_act_exp = jnp.einsum(
            "lsd,lfd->lsf", grad_slots_in, w_exp_down, preferred_element_type=f32
        )
        grad_pre_exp = gelu_grad(pre_exp, grad_act_exp).astype(bf16)
        grad_slots_out = jnp.einsum(
            "lsf,ldf->lsd", grad_pre_exp, w_exp_up, preferred_element_type=f32
        )
        back = return_slots(scatter_cols(grad_slots_out.reshape(slots, model_width)))
        (grad_expert_own,) = unslot(back)
        grad_w_exp_down = jnp.einsum(
            "lsf,lsd->lfd", act_exp, grad_slots_in, preferred_element_type=f32
        )
        grad_w_exp_up = jnp.einsum(
            "lsd,lsf->ldf", slots_in, grad_pre_exp, preferred_element_type=f32
        )

    logits_own, hot_own = own_rows_of(logits), own_rows_of(hot_float)
    (mix_own, gate_own), gates_pull = jax.vjp(lambda z: gates(z, hot_own), logits_own)
    output = (
        middle + mix_own[:, 0:1] * dense_own + (mix_own[:, 1] * gate_own)[:, None] * expert_own
    ).astype(bf16)
    grad_out = cotangent.astype(f32)
    dense_dot = jnp.sum(grad_out * dense_own, axis=1)
    expert_dot = jnp.sum(grad_out * expert_own, axis=1)
    grad_mix_coef = jnp.stack([dense_dot, gate_own * expert_dot], axis=1)
    (grad_logits,) = gates_pull((grad_mix_coef, mix_own[:, 1] * expert_dot))
    grad_gate_w = lax.dot_general(
        grad_logits,
        normed_two.astype(f32),
        (((0,), (0,)), ((), ())),
        precision=highest,
        preferred_element_type=f32,
    )
    grad_hidden_gate = lax.dot_general(
        grad_logits,
        gate_w.astype(f32),
        (((1,), (1,)), ((), ())),
        precision=highest,
        preferred_element_type=f32,
    )
    grad_hidden_own = dense_back_own + grad_expert_own + grad_hidden_gate
    _, norm_two_pull = jax.vjp(layer_norm, middle, norm2_gain)
    grad_middle_norm, grad_gain2 = norm_two_pull(grad_hidden_own)
    grad_middle = grad_out + grad_middle_norm

    grad_attn_all = gather_rows(grad_middle.astype(bf16))
    grad_w_out = jnp.einsum("gk,gd->kd", attn_heads, grad_attn_all, preferred_element_type=f32)
    grad_heads = jnp.einsum("gd,kd->gk", grad_attn_all, w_out, preferred_element_type=f32).astype(
        bf16
    )
    if special:
        ride = Ride(4, 7, [state], layout, 1024, share)
        grad_qkv, state = attend_back(labels, projected, grad_heads, ride)
    else:
        grad_qkv = attend_back(labels, projected, grad_heads)
    grad_w_qkv = jnp.einsum("gd,cgk->cdk", normed_all, grad_qkv, preferred_element_type=f32)
    grad_normed_one = scatter_rows(
        jnp.einsum("cgk,cdk->gd", grad_qkv, w_qkv, preferred_element_type=f32)
    )
    _, norm_one_pull = jax.vjp(layer_norm, token_f32, norm1_gain)
    grad_token_norm, grad_gain1 = norm_one_pull(grad_normed_one)
    grad_tokens = grad_middle + grad_token_norm

    wide = [g.astype(bf16) for g in (grad_w_qkv, grad_w_out)]
    small = jnp.concatenate([grad_gain1[None], grad_gain2[None], grad_gate_w], axis=0)
    if special:
        padding = -small.shape[0] % 8
        shapes = [[grad_w_up.shape, grad_w_down.shape], [g.shape for g in wide]]
        rides = [
            Ride(7, 8, [state], layout, 1024, share),
            Ride(0, 8, wide, split_layout(shapes[1], 512), 512, share),
        ]
        small = jnp.pad(small, ((0, padding), (0, 0)))
        small, grad_w_up, grad_w_down, *wide = last_sums(rides, shapes, small)
    else:
        grad_w_up, grad_w_down = lax.psum(
            [g.astype(bf16) for g in (grad_w_up, grad_w_down)], "expert"
        )
        wide = lax.psum(wide, "expert")
        small = lax.psum(small, ("expert", "tensor"))
    grad_w_qkv, grad_w_out, grad_w_up, grad_w_down = (
        g.astype(f32) for g in (*wide, grad_w_up, grad_w_down)
    )
    return (
        output,
        grad_tokens,
        small[0],
        grad_w_qkv,
        grad_w_out,
        small[1],
        grad_w_up,
        grad_w_down,
        small[2 : 2 + experts_all].T,
        small[2 + experts_all : 4 + experts_all].T,
        grad_w_exp_up,
        grad_w_exp_down,
    )


def solution(mesh):
    return jax.shard_map(
        body,
        mesh=mesh,
        in_specs=(
            P(("expert", "tensor"), None),
            P(),
            P(None, None, "tensor"),
            P("tensor", None),
            P(),
            P(None, "tensor"),
            P("tensor", None),
            P(),
            P(),
            P("expert", None, "tensor"),
            P("expert", "tensor", None),
            P("expert", None),
            P("expert", None),
            P(("expert", "tensor"), None),
        ),
        out_specs=(
            P(("expert", "tensor"), None),
            P(("expert", "tensor"), None),
            P(),
            P(None, None, "tensor"),
            P("tensor", None),
            P(),
            P(None, "tensor"),
            P("tensor", None),
            P(),
            P(),
            P("expert", None, "tensor"),
            P("expert", "tensor", None),
        ),
        check_vma=False,
    )
```

```python
import functools

import jax
import jax.numpy as jnp
from jax import lax
from jax.experimental import pallas as pl
from jax.experimental.pallas import tpu as pltpu
from jax.sharding import PartitionSpec as P

HEAD = 64
PROMPT = 512
BLOCK = 256
LANES = 128
PIECE = 256
MASKED = -1e30

epsilon = 1e-05
highest = lax.Precision.HIGHEST
f32 = jnp.float32
bf16 = jnp.bfloat16


def layer_norm(values, norm_gain):
    centred = values - jnp.mean(values, axis=-1, keepdims=True)
    variance = jnp.mean(centred * centred, axis=-1, keepdims=True)
    return centred * lax.rsqrt(variance + epsilon) * norm_gain


def gelu_grad(pre_act, upstream):
    return jax.vjp(jax.nn.gelu, pre_act)[1](upstream)[0]


def nt_dot(left, right):
    return lax.dot_general(left, right, (((1,), (1,)), ((), ())), preferred_element_type=f32)


def nn_dot(left, right):
    return lax.dot_general(left, right, (((1,), (0,)), ((), ())), preferred_element_type=f32)


def tn_dot(left, right):
    return lax.dot_general(left, right, (((0,), (0,)), ((), ())), preferred_element_type=f32)


def fill_bias(row_labels_ref, col_labels_ref, cont_bias, tri_bias, transposed):
    size = cont_bias.shape[0]
    down = lax.broadcasted_iota(jnp.int32, (size, size), 0)
    across = lax.broadcasted_iota(jnp.int32, (size, size), 1)
    ordered = (down <= across) if transposed else (across <= down)
    same = row_labels_ref[...] == col_labels_ref[...]
    cont_bias[...] = jnp.where(ordered & same, 0.0, MASKED)
    down = lax.broadcasted_iota(jnp.int32, (BLOCK, BLOCK), 0)
    across = lax.broadcasted_iota(jnp.int32, (BLOCK, BLOCK), 1)
    ordered = (down <= across) if transposed else (across <= down)
    tri_bias[...] = jnp.where(ordered, 0.0, MASKED)


def head_lanes(half):
    lane = lax.broadcasted_iota(jnp.int32, (1, LANES), 1)
    return (lane < HEAD) if half == 0 else (lane >= HEAD)


def turned(pair):
    return lax.axis_index("tensor") if pair else 0


def attend_kernel(pair, col_ref, row_ref, qp, qc, kp, kc, vp, vc, o_ref, cont_bias, tri_bias):
    @pl.when(pl.program_id(0) == 0)
    def _():
        fill_bias(col_ref, row_ref, cont_bias, tri_bias, False)

    turn = turned(pair)
    scale = HEAD**-0.5
    for part in range(2):
        for inner in range(0, PROMPT, BLOCK):
            upto = inner + BLOCK
            mixed = []
            for half in range(2):
                source = (qc if part else qp)[inner:upto, :]
                query = jnp.where(head_lanes(half), source * scale, 0.0).astype(bf16)
                pieces = []
                if part:
                    pieces.append((kp[...], vp[...], None))
                    pieces.append((kc[:upto, :], vc[:upto, :], cont_bias[inner:upto, :upto]))
                else:
                    if inner:
                        pieces.append((kp[:inner, :], vp[:inner, :], None))
                    pieces.append((kp[inner:upto, :], vp[inner:upto, :], tri_bias[...]))
                scores = []
                for key, _, bias in pieces:
                    score = nt_dot(query, key)
                    scores.append(score if bias is None else score + bias)
                top = functools.reduce(
                    jnp.maximum, [jnp.max(score, axis=1, keepdims=True) for score in scores]
                )
                total, out = 0.0, 0.0
                for score, (_, value, _) in zip(scores, pieces, strict=True):
                    weights = jnp.exp(score - top)
                    total = total + jnp.sum(weights, axis=1, keepdims=True)
                    out = out + nn_dot(weights.astype(bf16), value)
                mixed.append(out / total)
            which = (1 - turn) if part else turn
            o_ref[which, inner:upto, :] = jnp.where(head_lanes(0), mixed[0], mixed[1]).astype(bf16)


def attend_back_part(
    part, pair, qp, qc, kp, kc, vp, vc, gp, gc, d_ref, cont_bias, tri_bias, *accs
):
    turn = turned(pair)
    scale = HEAD**-0.5
    dkp, dkc, dvp, dvc = accs
    for inner in range(0, PROMPT, BLOCK):
        upto = inner + BLOCK
        dq = 0.0
        for half in range(2):
            lanes = head_lanes(half)
            query = jnp.where(lanes, (qc if part else qp)[inner:upto, :] * scale, 0.0)
            query = query.astype(bf16)
            grad = jnp.where(lanes, (gc if part else gp)[inner:upto, :], 0.0).astype(bf16)
            if part:
                pieces = [(kp, vp, dkp, dvp, 0, PROMPT, None)]
                pieces.append((kc, vc, dkc, dvc, 0, upto, cont_bias[:upto, inner:upto]))
            else:
                pieces = [(kp, vp, dkp, dvp, 0, inner, None)] if inner else []
                pieces.append((kp, vp, dkp, dvp, inner, upto, tri_bias[...]))
            scores = []
            for key, _, _, _, at, end, bias in pieces:
                score = nt_dot(key[at:end, :], query)
                scores.append(score if bias is None else score + bias)
            top = functools.reduce(
                jnp.maximum, [jnp.max(score, axis=0, keepdims=True) for score in scores]
            )
            scores = [jnp.exp(score - top) for score in scores]
            total = sum(jnp.sum(score, axis=0, keepdims=True) for score in scores)
            scores = [score * (1.0 / total) for score in scores]
            grads = [
                nt_dot(value[at:end, :], grad) for _, value, _, _, at, end, _ in pieces
            ]
            row_dot = sum(
                jnp.sum(score * up, axis=0, keepdims=True)
                for score, up in zip(scores, grads, strict=True)
            )
            for score, up, (key, _, dk, dv, at, end, _) in zip(
                scores, grads, pieces, strict=True
            ):
                grad_scores = (score * (up - row_dot)).astype(bf16)
                dv[at:end, :] += nn_dot(score.astype(bf16), grad)
                dk[at:end, :] += nn_dot(grad_scores, query)
                masked = jnp.where(lanes, key[at:end, :] * scale, 0.0).astype(bf16)
                dq = dq + tn_dot(grad_scores, masked)
        which = (1 - turn) if part else turn
        d_ref[0, which, inner:upto, :] = dq.astype(bf16)


def attend_back_phases(pair, step, col_ref, row_ref, *refs):
    qp, qc, kp, kc, vp, vc, gp, gc, d_ref, cont_bias, tri_bias, *accs = refs

    def prompt():
        @pl.when(step == 0)
        def _():
            fill_bias(col_ref, row_ref, cont_bias, tri_bias, True)

        for acc in accs:
            acc[...] = jnp.zeros_like(acc)
        attend_back_part(0, pair, *refs)

    def continuations():
        attend_back_part(1, pair, *refs)
        turn = turned(pair)
        for number, acc in enumerate(accs):
            which = (1 - turn) if number % 2 else turn
            d_ref[1 + number // 2, which] = acc[...].astype(bf16)

    return [prompt, continuations]


def attend_back_kernel(pair, *refs):
    for phase in attend_back_phases(pair, pl.program_id(0), *refs):
        phase()


def half_specs(size, lead, pair, steps=None):
    blank = (pl.Squeezed(),) * (1 if lead is None else 2)

    def spec(cont):
        def index(i):
            i = i if steps is None else jnp.minimum(i, steps - 1)
            half = 1 - turned(pair) if cont else turned(pair)
            return (half, 0, i) if lead is None else (lead, half, 0, i)

        return pl.BlockSpec((*blank, size, LANES), index)

    return [spec(False), spec(True)]


def attend_call(kernel, name, labels, projected, grad_heads, dots, accs):
    rows, cols = projected.shape[1:]
    cont = rows - PROMPT
    pair = paired()
    kernel = functools.partial(kernel, pair)
    halves = projected.reshape(3, 2, PROMPT, cols)
    work = 2 * rows * rows * cols * dots
    back = grad_heads is not None
    lead = (3,) if back else ()
    specs = [s for c in range(3) for s in half_specs(PROMPT, c, pair)]
    args = [halves] * 6
    if back:
        specs += half_specs(PROMPT, None, pair)
        args += [grad_heads.reshape(2, PROMPT, cols)] * 2
    specs = [
        pl.BlockSpec((cont, 1), lambda i: (0, 0)),
        pl.BlockSpec((1, cont), lambda i: (0, 0)),
        *specs,
    ]
    out_spec = pl.BlockSpec(
        (*lead, 2, PROMPT, LANES), lambda i: (*(0 for _ in lead), 0, 0, i)
    )
    out_shape = jax.ShapeDtypeStruct((*lead, 2, PROMPT, cols), bf16)
    scratch = [
        pltpu.VMEM((cont, cont), f32),
        pltpu.VMEM((BLOCK, BLOCK), f32),
        *[pltpu.VMEM((PROMPT, LANES), f32)] * accs,
    ]
    args = [labels[:, None], labels[None, :], *args]
    steps = cols // LANES
    out = pl.pallas_call(
        kernel,
        grid=(steps,),
        in_specs=specs,
        out_specs=out_spec,
        scratch_shapes=scratch,
        out_shape=out_shape,
        cost_estimate=pl.CostEstimate(
            flops=work, bytes_accessed=14 * rows * cols, transcendentals=rows * rows * 4
        ),
        name=name,
    )(*args)
    return out.reshape(*lead, rows, cols)


def attend(labels, projected):
    return attend_call(attend_kernel, "attend", labels, projected, None, 2, 0)


def attend_back(labels, projected, grad_heads):
    return attend_call(
        attend_back_kernel, "attend_back", labels, projected, grad_heads, 5, 4
    )


HIDDEN = 512
ROWS = 512
CUT = 256
MIDDLE = 4
RIDE_GAP = 2


def gelu_both(pre_act):
    slope = 0.7978845608028654
    square = pre_act * pre_act
    bend = jnp.tanh(slope * (pre_act + 0.044715 * (square * pre_act)))
    share = 0.5 * (1.0 + bend)
    steep = 0.5 * slope * (1.0 + (3 * 0.044715) * square)
    return pre_act * share, share + pre_act * (1.0 - bend * bend) * steep


def feed_rows(first, at, x_ref, dy_ref, wu_ref, wd_ref, act, dact, y_acc, dx_acc):
    pre_act = nn_dot(x_ref[at, :], wu_ref[...])
    up = nt_dot(dy_ref[at, :], wd_ref[...])
    value, slope = gelu_both(pre_act)
    value = value.astype(bf16)
    back = (up * slope).astype(bf16)
    act[at, :] = value
    dact[at, :] = back
    out = nn_dot(value, wd_ref[...])
    grad = nt_dot(back, wu_ref[...])

    @pl.when(first)
    def _():
        y_acc[at, :] = out
        dx_acc[at, :] = grad

    @pl.when(jnp.logical_not(first))
    def _():
        y_acc[at, :] += out
        dx_acc[at, :] += grad


def feed_down(x_ref, dy_ref, act, dact, gu_ref, gd_ref):
    for at in range(0, gd_ref.shape[0], CUT):
        gd_ref[at : at + CUT, :] = tn_dot(act[:, at : at + CUT], dy_ref[...]).astype(gd_ref.dtype)


def feed_up(x_ref, dy_ref, act, dact, gu_ref, gd_ref):
    for at in range(0, gu_ref.shape[0], CUT):
        gu_ref[at : at + CUT, :] = tn_dot(x_ref[:, at : at + CUT], dact[...]).astype(gu_ref.dtype)


def feed_kernel(x_ref, dy_ref, wu_ref, wd_ref, *refs):
    yk, ya, dxk, dxa, gu_ref, gd_ref, act, dact, y_acc, dx_acc = refs
    step = pl.program_id(0)
    for at in range(0, x_ref.shape[0], ROWS):
        rows = slice(at, at + ROWS)
        feed_rows(step == 0, rows, x_ref, dy_ref, wu_ref, wd_ref, act, dact, y_acc, dx_acc)
    feed_down(x_ref, dy_ref, act, dact, gu_ref, gd_ref)
    feed_up(x_ref, dy_ref, act, dact, gu_ref, gd_ref)

    @pl.when(step == pl.num_programs(0) - 1)
    def _():
        half = yk.shape[0]
        yk[...] = y_acc[:half, :]
        dxk[...] = dx_acc[:half, :]
        ya[...] = y_acc[half:, :].astype(bf16)
        dxa[...] = dx_acc[half:, :].astype(bf16)


def one_buffer(shape):
    return pl.BlockSpec(shape, lambda *_: (0,) * len(shape), pipeline_mode=pl.Buffered(1))


def feed_forward(x, dy, w_up, w_down):
    rows, width = x.shape
    hidden = w_up.shape[1]
    tile = min(HIDDEN, hidden)
    half = rows // 2
    block = jax.ShapeDtypeStruct((half, width), f32)
    sent = jax.ShapeDtypeStruct((half, width), bf16)
    return pl.pallas_call(
        feed_kernel,
        grid=(hidden // tile,),
        in_specs=[
            one_buffer((rows, width)),
            one_buffer((rows, width)),
            pl.BlockSpec((width, tile), lambda i: (0, i)),
            pl.BlockSpec((tile, width), lambda i: (i, 0)),
        ],
        out_specs=[
            *[one_buffer((half, width))] * 4,
            pl.BlockSpec((width, tile), lambda i: (0, i)),
            pl.BlockSpec((tile, width), lambda i: (i, 0)),
        ],
        out_shape=[
            block,
            sent,
            block,
            sent,
            jax.ShapeDtypeStruct((width, hidden), bf16),
            jax.ShapeDtypeStruct((hidden, width), bf16),
        ],
        scratch_shapes=[
            pltpu.VMEM((rows, tile), bf16),
            pltpu.VMEM((rows, tile), bf16),
            pltpu.VMEM((rows, width), f32),
            pltpu.VMEM((rows, width), f32),
        ],
        compiler_params=pltpu.CompilerParams(vmem_limit_bytes=56 * 1024 * 1024),
        cost_estimate=pl.CostEstimate(
            flops=12 * rows * width * hidden,
            bytes_accessed=8 * width * hidden + 12 * rows * width,
            transcendentals=rows * hidden,
        ),
        name="feed_forward",
    )(x, dy, w_up, w_down)


ORDERS = ((1, 2, 4, 8), (2, 4, 1, 8), (4, 1, 2, 8))
DEPTH = 4
MESH = pl.DeviceIdType.MESH


def partner_of(bit):
    me = lax.axis_index("expert")
    side = lax.rem(me // bit, 2)
    return me + bit * (1 - 2 * side), side


def greet(core):
    barrier = pltpu.get_barrier_semaphore()
    for bit in sorted(ORDERS[0]):
        pl.semaphore_signal(
            barrier, 1, device_id={"expert": partner_of(bit)[0]}, device_id_type=MESH
        )
    if core:
        other = 1 - lax.axis_index("tensor")
        pl.semaphore_signal(barrier, 1, device_id={"tensor": other}, device_id_type=MESH)
    pl.semaphore_wait(barrier, DEPTH + core)


class Ride:
    def __init__(self, level_in, level_out, values, shapes, width, counts, gap=1):
        self.first, self.last = level_in, level_out
        self.values, self.shapes, self.width, self.counts = list(values), shapes, width, counts
        layout = split_layout(shapes, width)
        self.pieces = sum(map(len, layout))
        self.where = [(a, piece) for a, pieces in enumerate(layout) for piece in pieces]
        stages = range(level_out - level_in + 1)
        self.delays = [gap * stage for stage in stages] if isinstance(gap, int) else gap
        self.ticks = max(counts) + self.delays[-1]

    def rows_at(self, level):
        return PIECE >> (level if level <= DEPTH else 2 * DEPTH - level)

    def out_shape(self):
        shapes = self.shapes
        if self.last < 2 * DEPTH:
            shapes = [(self.pieces, self.rows_at(self.last), self.width)]
        return [jax.ShapeDtypeStruct(shape, bf16) for shape in shapes]

    def scratch(self):
        shapes = []
        if self.first < DEPTH:
            shapes.append(self.rows_at(self.first))
            shapes += [self.rows_at(n + 1) for n in range(self.first, min(self.last, DEPTH))]
        if self.last > DEPTH:
            shapes.append(self.rows_at(self.last))
        hops = self.last - self.first
        return [
            *[pltpu.VMEM((self.pieces, rows, self.width), bf16) for rows in shapes],
            pltpu.SemaphoreType.DMA((hops, self.pieces)),
            pltpu.SemaphoreType.DMA((hops, self.pieces)),
            pltpu.SemaphoreType.DMA((self.pieces,)),
            pltpu.SemaphoreType.DMA((self.pieces,)),
        ]

    def bind(self, ins, outs, scratch):
        self.ins, self.outs = ins, outs
        *buffers, self.send_sem, self.recv_sem, self.load_sem, self.store_sem = scratch
        self.held = buffers[0] if self.first < DEPTH else None
        self.got = buffers[1 : 1 + max(0, min(self.last, DEPTH) - self.first)]
        self.full = buffers[-1] if self.last > DEPTH else None
        self.sides = {bit: partner_of(bit) for bit in ORDERS[0]}

    def held_at(self, order, level):
        total = 0
        for n in range(self.first, level):
            total = total + self.sides[order[n]][1] * self.rows_at(n + 1)
        return pl.multiple_of(total, 16)

    def full_at(self, order, level):
        total = 0
        for n in range(2 * DEPTH - self.last, 2 * DEPTH - level):
            total = total + self.sides[order[n]][1] * self.rows_at(n + 1)
        return pl.multiple_of(total, 16)

    def color_of(self, piece):
        color = 0
        while piece >= sum(self.counts[: color + 1]):
            color += 1
        return color

    def load(self, piece):
        sem = self.load_sem.at[piece]
        if self.first == 0:
            a, parts = self.where[piece]
            return [
                pltpu.make_async_copy(self.ins[a].at[src], self.held.at[(piece, *dst)], sem)
                for src, dst in parts
            ]
        if self.first < DEPTH:
            return [pltpu.make_async_copy(self.ins[0].at[piece], self.held.at[piece], sem)]
        order = ORDERS[self.color_of(piece)]
        at = pl.ds(self.full_at(order, self.first), self.rows_at(self.first))
        return [pltpu.make_async_copy(self.ins[0].at[piece], self.full.at[piece, at], sem)]

    def await_load(self, order, piece):
        sem = self.load_sem.at[piece]
        if self.first < DEPTH:
            whole = self.held.at[piece]
        else:
            at = pl.ds(self.full_at(order, self.first), self.rows_at(self.first))
            whole = self.full.at[piece, at]
        pltpu.make_async_copy(whole, whole, sem).wait()

    def stores(self, piece):
        sem = self.store_sem.at[piece]
        if self.last == 2 * DEPTH:
            a, parts = self.where[piece]
            return [
                pltpu.make_async_copy(self.full.at[(piece, *dst)], self.outs[a].at[src], sem)
                for src, dst in parts
            ]
        if self.last > DEPTH:
            return [pltpu.make_async_copy(self.full.at[piece], self.outs[0].at[piece], sem)]
        order = ORDERS[self.color_of(piece)]
        at = pl.ds(self.held_at(order, self.last), self.rows_at(self.last))
        return [pltpu.make_async_copy(self.held.at[piece, at], self.outs[0].at[piece], sem)]

    def start_store(self, order, piece):
        if self.last == 2 * DEPTH:
            for number in range(self.pieces):

                @pl.when(piece == number)
                def _(number=number):
                    for copy in self.stores(number):
                        copy.start()

            return
        sem = self.store_sem.at[piece]
        if self.last > DEPTH:
            source = self.full.at[piece]
        else:
            at = pl.ds(self.held_at(order, self.last), self.rows_at(self.last))
            source = self.held.at[piece, at]
        pltpu.make_async_copy(source, self.outs[0].at[piece], sem).start()

    def exchange(self, order, hop, piece):
        sems = (self.send_sem.at[hop - self.first, piece], self.recv_sem.at[hop - self.first, piece])
        if hop < DEPTH:
            target, side = self.sides[order[hop]]
            size = self.rows_at(hop + 1)
            away = pl.multiple_of(self.held_at(order, hop) + (1 - side) * size, 16)
            source = self.held.at[piece, pl.ds(away, size)]
            dest = self.got[hop - self.first].at[piece]
        else:
            target, _ = self.sides[order[2 * DEPTH - 1 - hop]]
            at = pl.ds(self.full_at(order, hop), self.rows_at(hop))
            source = dest = self.full.at[piece, at]
        return pltpu.make_async_remote_copy(
            source, dest, *sems, device_id={"expert": target}, device_id_type=MESH
        )

    def run(self, color, stage, piece):
        order = ORDERS[color]
        if stage == 0:
            self.await_load(order, piece)
        else:
            hop = self.first + stage - 1
            self.exchange(order, hop, piece).wait()
            if hop < DEPTH:
                size = self.rows_at(hop + 1)
                at = pl.ds(self.held_at(order, hop + 1), size)
                total = self.held[piece, at, :].astype(f32)
                total = (total + self.got[hop - self.first][piece].astype(f32)).astype(bf16)
                if hop + 1 == DEPTH and self.last > DEPTH:
                    self.full[piece, pl.ds(self.full_at(order, DEPTH), size), :] = total
                else:
                    self.held[piece, at, :] = total
        if self.first + stage < self.last:
            self.exchange(order, self.first + stage, piece).start()
        else:
            self.start_store(order, piece)

    def begin(self):
        for piece in range(self.pieces):
            for copy in self.load(piece):
                copy.start()

    def tick(self, t):
        for stage in range(self.last - self.first + 1):
            for color, count in enumerate(self.counts):

                at = t - self.delays[stage]

                @pl.when((at >= 0) & (at < count))
                def _(color=color, stage=stage, at=at):
                    self.run(color, stage, sum(self.counts[:color]) + at)

    def end(self):
        for piece in range(self.pieces):
            for copy in self.stores(piece):
                copy.wait()


any_spec = pl.BlockSpec(memory_space=pl.ANY)


def carry(
    phases, steps, specs, out_specs, out_shape, scratch, args, rides, name, flops, collective
):
    n_ticks = max(ride.ticks for ride in rides)
    ride_outs = [ride.out_shape() for ride in rides]
    parts = 2
    grid = max(steps, -(-n_ticks // parts))

    def clamp(spec):
        if spec.index_map is None:
            return spec
        return pl.BlockSpec(
            spec.block_shape,
            lambda i: spec.index_map(jnp.minimum(i, steps - 1)),
            pipeline_mode=spec.pipeline_mode,
        )

    n_in, n_out = len(args), len(out_shape)

    def kernel(*refs):
        refs = list(refs)
        take = lambda count: [refs.pop(0) for _ in range(count)]
        main_in = take(n_in)
        ins = [take(len(ride.values)) for ride in rides]
        main_out = take(n_out)
        outs = [take(len(shapes)) for shapes in ride_outs]
        main_scratch = take(len(scratch))
        for ride, got, out in zip(rides, ins, outs, strict=True):
            ride.bind(got, out, take(len(ride.scratch())))
        step = pl.program_id(0)

        @pl.when(step == 0)
        def _():
            for ride in rides:
                ride.begin()
            greet(False)

        for number, phase in enumerate(phases(step, *main_in, *main_out, *main_scratch)):
            for ride in rides:
                ride.tick(step * parts + number)
            pl.when(step < steps)(phase)

        @pl.when(step == grid - 1)
        def _():
            for ride in rides:
                ride.end()

    moved = sum(v.size for ride in rides for v in ride.values)
    return pl.pallas_call(
        kernel,
        grid_spec=pltpu.PrefetchScalarGridSpec(
            num_scalar_prefetch=0,
            grid=(grid,),
            in_specs=[*map(clamp, specs), *[any_spec] * sum(len(ride.values) for ride in rides)],
            out_specs=[*map(clamp, out_specs), *[any_spec] * sum(map(len, ride_outs))],
            scratch_shapes=[*scratch, *[m for ride in rides for m in ride.scratch()]],
        ),
        out_shape=[*out_shape, *[shape for shapes in ride_outs for shape in shapes]],
        compiler_params=pltpu.CompilerParams(
            collective_id=collective, has_side_effects=True, vmem_limit_bytes=62 * 1024 * 1024
        ),
        cost_estimate=pl.CostEstimate(flops=flops, bytes_accessed=4 * moved, transcendentals=0),
        name=name,
    )(*args, *[v for ride in rides for v in ride.values])


def split_layout(shapes, width):
    layout = []
    for shape in shapes:
        pieces = []
        leads = [(c,) for c in range(shape[0])] if len(shape) == 3 else [()]
        for lead in leads:
            for c in range(0, shape[-1], width):
                for r in range(0, shape[-2], PIECE):
                    pieces.append([((*lead, slice(r, r + PIECE), slice(c, c + width)), ())])
        layout.append(pieces)
    return layout


def last_kernel(rides, small_in, *refs):
    refs = list(refs)
    take = lambda count: [refs.pop(0) for _ in range(count)]
    ins = [take(len(ride.values)) for ride in rides]
    (small_out,) = take(1)
    outs = [take(len(ride.out_shape())) for ride in rides]
    small, small_got, small_sem = take(3)
    for ride, got, out in zip(rides, ins, outs, strict=True):
        ride.bind(got, out, take(len(ride.scratch())))
    bits = sorted(ORDERS[0])

    def small_copy(step):
        if step < DEPTH:
            target = {"expert": partner_of(bits[step])[0]}
        else:
            target = {"tensor": 1 - lax.axis_index("tensor")}
        return pltpu.make_async_remote_copy(
            small.at[step],
            small_got.at[step],
            small_sem.at[0, step],
            small_sem.at[1, step],
            device_id=target,
            device_id_type=MESH,
        )

    for ride in rides:
        ride.begin()
    first = pltpu.make_async_copy(small_in, small.at[0], small_sem.at[2, 0])
    first.start()
    greet(True)

    def step(t, _):
        for ride in rides:
            ride.tick(t)
        for number in range(DEPTH + 2):

            @pl.when(t == number)
            def _(number=number):
                if number == 0:
                    first.wait()
                else:
                    small_copy(number - 1).wait()
                    small[number] = small[number - 1] + small_got[number - 1]
                if number < DEPTH + 1:
                    small_copy(number).start()

        return 0

    lax.fori_loop(0, max(ride.ticks for ride in rides), step, 0)
    out = pltpu.make_async_copy(small.at[DEPTH + 1], small_out, small_sem.at[2, 1])
    out.start()
    for ride in rides:
        ride.end()
    out.wait()


def alone_kernel(ride, *refs):
    count = len(ride.values)
    ride.bind(refs[:count], refs[count : count + 1], refs[count + 1 :])
    ride.begin()
    greet(False)

    def step(t, _):
        ride.tick(t)
        return 0

    lax.fori_loop(0, ride.ticks, step, 0)
    ride.end()


def ride_alone(ride, collective):
    return pl.pallas_call(
        functools.partial(alone_kernel, ride),
        in_specs=[any_spec] * len(ride.values),
        out_specs=[any_spec],
        out_shape=ride.out_shape(),
        scratch_shapes=ride.scratch(),
        compiler_params=pltpu.CompilerParams(
            collective_id=collective, has_side_effects=True, vmem_limit_bytes=62 * 1024 * 1024
        ),
        name="ride_alone",
    )(*ride.values)


def last_sums(rides, small):
    ride_outs = [ride.out_shape() for ride in rides]
    values = [v for ride in rides for v in ride.values]
    shapes = [shape for shapes in ride_outs for shape in shapes]
    return pl.pallas_call(
        functools.partial(last_kernel, rides),
        in_specs=[any_spec] * (1 + len(values)),
        out_specs=[any_spec] * (1 + len(shapes)),
        out_shape=[jax.ShapeDtypeStruct(small.shape, f32), *shapes],
        scratch_shapes=[
            pltpu.VMEM((DEPTH + 2, *small.shape), f32),
            pltpu.VMEM((DEPTH + 1, *small.shape), f32),
            pltpu.SemaphoreType.DMA((3, DEPTH + 1)),
            *[m for ride in rides for m in ride.scratch()],
        ],
        compiler_params=pltpu.CompilerParams(
            collective_id=4, has_side_effects=True, vmem_limit_bytes=62 * 1024 * 1024
        ),
        name="last_sums",
    )(small, *values)


def expert_data_phases(steps, step, x_ref, dy_ref, wu_ref, wd_ref, *refs):
    keep, away, act, dact, y_acc, dx_acc = refs
    halves = x_ref.shape[0] // 2
    width = x_ref.shape[1]

    def rows(number):
        at = slice(number * halves, (number + 1) * halves)
        feed_rows(step == 0, at, x_ref, dy_ref, wu_ref, wd_ref, act, dact, y_acc, dx_acc)

    def finish():
        rows(1)
        half = width // 2
        for side in range(2):

            @pl.when((step == steps - 1) & (lax.axis_index("tensor") == side))
            def _(side=side):
                own = slice(side * half, (side + 1) * half)
                other = slice((1 - side) * half, (2 - side) * half)
                keep[:, :half] = y_acc[:, own]
                keep[:, half:] = dx_acc[:, own]
                away[:, :half] = y_acc[:, other].astype(bf16)
                away[:, half:] = dx_acc[:, other].astype(bf16)

    return [functools.partial(rows, 0), finish]


def expert_data(x, dy, w_up, w_down, ride):
    rows, width = x.shape
    hidden = w_up.shape[1]
    tile = min(HIDDEN, hidden)
    steps = hidden // tile
    inner = jax.ShapeDtypeStruct((rows, hidden), bf16)
    return carry(
        functools.partial(expert_data_phases, steps),
        steps,
        [
            one_buffer((rows, width)),
            one_buffer((rows, width)),
            pl.BlockSpec((width, tile), lambda i: (0, i)),
            pl.BlockSpec((tile, width), lambda i: (i, 0)),
        ],
        [
            *[one_buffer((rows, width))] * 2,
            *[pl.BlockSpec((rows, tile), lambda i: (0, i))] * 2,
        ],
        [
            jax.ShapeDtypeStruct((rows, width), f32),
            jax.ShapeDtypeStruct((rows, width), bf16),
            inner,
            inner,
        ],
        [pltpu.VMEM((rows, width), f32)] * 2,
        [x, dy, w_up, w_down],
        [ride],
        "expert_data",
        8 * rows * width * hidden,
        1,
    )


def expert_weights_kernel(*refs):
    feed_down(*refs)
    feed_up(*refs)


def expert_weights(x, dy, act, dact):
    rows, width = x.shape
    hidden = act.shape[1]
    tile = min(HIDDEN, hidden)
    return pl.pallas_call(
        expert_weights_kernel,
        grid=(hidden // tile,),
        in_specs=[
            one_buffer((rows, width)),
            one_buffer((rows, width)),
            *[pl.BlockSpec((rows, tile), lambda i: (0, i))] * 2,
        ],
        out_specs=[
            pl.BlockSpec((width, tile), lambda i: (0, i)),
            pl.BlockSpec((tile, width), lambda i: (i, 0)),
        ],
        out_shape=[
            jax.ShapeDtypeStruct((width, hidden), f32),
            jax.ShapeDtypeStruct((hidden, width), f32),
        ],
        compiler_params=pltpu.CompilerParams(vmem_limit_bytes=56 * 1024 * 1024),
        cost_estimate=pl.CostEstimate(
            flops=4 * rows * width * hidden,
            bytes_accessed=8 * width * hidden + 4 * rows * width + 4 * rows * hidden,
            transcendentals=0,
        ),
        name="expert_weights",
    )(x, dy, act, dact)


def attention_back_phases(pairs, step, col_ref, row_ref, da_ref, wo_ref, *refs):
    halves, refs = refs[:6], refs[6:]
    wq_any, normed_any, gq_ref, keep, away, *refs = refs
    cont_bias, tri_bias, do_s, d_s, dh_acc, wq, normed, sems, *accs = refs
    rows = da_ref.shape[0]
    half = rows // 2
    copies = [
        pltpu.make_async_copy(source, dest, sems.at[number])
        for number, (source, dest) in enumerate(
            ((wq_any, wq), (normed_any, normed))
        )
    ]
    turn = turned(True)
    lanes = pl.ds(pl.multiple_of(jnp.minimum(step, pairs - 1) * LANES, LANES), LANES)

    def attend_part(part):
        grads = [do_s.at[which, :, lanes] for which in (turn, 1 - turn)]
        out = d_s.at[:, :, :, lanes]
        attend_back_part(part, True, *halves, *grads, out, cont_bias, tri_bias, *accs)

    which = jnp.clip(step - pairs, 0, 2)

    def first():
        @pl.when(step == 0)
        def _():
            for copy in copies:
                copy.start()
            for number in range(2):
                at = slice(number * half, (number + 1) * half)
                do_s[number] = nt_dot(da_ref[at, :], wo_ref[...]).astype(bf16)
            fill_bias(col_ref, row_ref, cont_bias, tri_bias, True)

        @pl.when(step < pairs)
        def _():
            for acc in accs:
                acc[...] = jnp.zeros_like(acc)
            attend_part(0)

        @pl.when(step == pairs)
        def _():
            for copy in copies:
                copy.wait()
            dh_acc[...] = jnp.zeros_like(dh_acc)

        @pl.when((step >= pairs) & (step < pairs + 3))
        def _():
            for number in range(2):
                dh_acc[number] += nt_dot(d_s[which, number], wq[which])

    def second():
        @pl.when(step < pairs)
        def _():
            attend_part(1)
            for number, acc in enumerate(accs):
                place = (1 - turn) if number % 2 else turn
                d_s[1 + number // 2, place, :, lanes] = acc[...].astype(bf16)

        @pl.when((step >= pairs) & (step < pairs + 3))
        def _():
            grads = d_s[which].reshape(rows, d_s.shape[-1])
            for at in range(0, normed.shape[1], CUT):
                gq_ref[which, at : at + CUT, :] = tn_dot(normed[:, at : at + CUT], grads).astype(
                    bf16
                )

        @pl.when(step == pairs + 2)
        def _():
            keep[...] = dh_acc[0]
            away[...] = dh_acc[1].astype(bf16)

    return [first, second]


def attention_back(labels, projected, grad_attn, w_out, w_qkv, normed, rides):
    rows, cols = projected.shape[1:]
    width = normed.shape[1]
    cont = rows - PROMPT
    pairs = cols // LANES
    inputs = projected.reshape(3, 2, PROMPT, cols)
    return carry(
        functools.partial(attention_back_phases, pairs),
        pairs + 3,
        [
            one_buffer((cont, 1)),
            one_buffer((1, cont)),
            one_buffer((rows, width)),
            one_buffer((cols, width)),
            *[s for c in range(3) for s in half_specs(PROMPT, c, True, pairs)],
            *[any_spec] * 2,
        ],
        [
            one_buffer((3, width, cols)),
            one_buffer((rows // 2, width)),
            one_buffer((rows // 2, width)),
        ],
        [
            jax.ShapeDtypeStruct((3, width, cols), bf16),
            jax.ShapeDtypeStruct((rows // 2, width), f32),
            jax.ShapeDtypeStruct((rows // 2, width), bf16),
        ],
        [
            pltpu.VMEM((cont, cont), f32),
            pltpu.VMEM((BLOCK, BLOCK), f32),
            pltpu.VMEM((2, rows // 2, cols), bf16),
            pltpu.VMEM((3, 2, rows // 2, cols), bf16),
            pltpu.VMEM((2, rows // 2, width), f32),
            pltpu.VMEM(w_qkv.shape, bf16),
            pltpu.VMEM(normed.shape, bf16),
            pltpu.SemaphoreType.DMA((2,)),
            *[pltpu.VMEM((PROMPT, LANES), f32)] * 4,
        ],
        [labels[:, None], labels[None, :], grad_attn, w_out, *[inputs] * 6, w_qkv, normed],
        rides,
        "attention_back",
        2 * rows * rows * cols * 5,
        3,
    )


def paired():
    return lax.axis_size("tensor") == 2


def swap(values):
    return lax.ppermute(values, "tensor", [(0, 1), (1, 0)])


def gather_rows(own):
    if paired():
        return jnp.concatenate([own, swap(own)], axis=0)
    return lax.all_gather(own, "tensor", axis=0, tiled=True)


def scatter_rows(partial, kind=bf16):
    if paired():
        size = partial.shape[0] // 2
        return partial[:size] + swap(partial[size:].astype(kind)).astype(f32)
    return lax.psum_scatter(
        partial.astype(kind), "tensor", scatter_dimension=0, tiled=True
    ).astype(f32)


def own_rows_of(values):
    size = values.shape[0] // lax.axis_size("tensor")
    if paired():
        return values[:size]
    return lax.dynamic_slice_in_dim(values, lax.axis_index("tensor") * size, size, 0)


def local_order(values):
    if paired():
        size = values.shape[0] // 2
        turned = jnp.concatenate([values[size:], values[:size]], axis=0)
        return jnp.where(lax.axis_index("tensor") == 0, values, turned)
    return values


def scatter_cols(partial):
    size = partial.shape[1] // lax.axis_size("tensor")
    rank = lax.axis_index("tensor")
    if paired():
        keep = lax.dynamic_slice_in_dim(partial, rank * size, size, 1)
        away = lax.dynamic_slice_in_dim(partial, (1 - rank) * size, size, 1).astype(bf16)
        return (keep + swap(away).astype(f32)).astype(bf16)
    return lax.psum_scatter(partial.astype(bf16), "tensor", scatter_dimension=1, tiled=True)


def turn_pair(cols_mine, count):
    width = cols_mine.shape[1] // count
    if not paired():
        return [
            lax.all_to_all(cols_mine[:, at : at + width], "tensor", 0, 1, tiled=True)
            for at in range(0, count * width, width)
        ]
    size = cols_mine.shape[0] // 2
    own, other = cols_mine[:size], swap(cols_mine[size:])
    first = lax.axis_index("tensor") == 0
    left, right = jnp.where(first, own, other), jnp.where(first, other, own)
    return [
        jnp.concatenate([left[:, at : at + width], right[:, at : at + width]], axis=1)
        for at in range(0, count * width, width)
    ]


def join_kernel(own_ref, other_ref, *outs):
    size = own_ref.shape[1] // len(outs)
    rank = lax.axis_index("tensor")
    for side in range(2):

        @pl.when(rank == side)
        def _(side=side):
            for number, out in enumerate(outs):
                cols = slice(number * size, (number + 1) * size)
                out[:, side * size : (side + 1) * size] = own_ref[:, cols]
                out[:, (1 - side) * size : (2 - side) * size] = other_ref[:, cols]


def join_cols(own, count):
    rows, width = own.shape
    if not paired():
        whole = lax.all_gather(own.reshape(rows, count, -1), "tensor", axis=2, tiled=True)
        return [whole[:, number] for number in range(count)]
    step = min(rows, 256)
    outs = [jax.ShapeDtypeStruct((rows, 2 * width // count), own.dtype)] * count
    return pl.pallas_call(
        join_kernel,
        grid=(rows // step,),
        in_specs=[pl.BlockSpec((step, width), lambda i: (i, 0))] * 2,
        out_specs=[pl.BlockSpec((step, 2 * width // count), lambda i: (i, 0))] * count,
        out_shape=outs,
        cost_estimate=pl.CostEstimate(
            flops=0, bytes_accessed=8 * rows * width, transcendentals=0
        ),
        name="join_cols",
    )(own, swap(own))


def body(
    tokens,
    norm1_gain,
    w_qkv,
    w_out,
    norm2_gain,
    w_up,
    w_down,
    w_router,
    w_mix,
    w_exp_up,
    w_exp_down,
    routes,
    segments,
    cotangent,
):
    own_rows = tokens.shape[0]
    model_width = tokens.shape[1]
    tensor_size = lax.axis_size("tensor")
    tensor_rank = lax.axis_index("tensor")
    owner_count = lax.axis_size("expert")
    group_rows = own_rows * tensor_size
    own_cols = model_width // tensor_size
    experts_all = w_router.shape[1]
    local_experts = w_exp_up.shape[0]
    capacity = group_rows // experts_all
    slots = experts_all * capacity
    barrier = lax.optimization_barrier
    special = owner_count == 16 and tensor_size == 2 and local_experts == 1

    def my_cols(values):
        return lax.dynamic_slice_in_dim(values, tensor_rank * own_cols, own_cols, 1)

    route_ids = local_order(routes[:, 0])
    route_hot = route_ids[:, None] == jnp.arange(experts_all, dtype=jnp.int32)[None, :]
    hot_float = route_hot.astype(f32)
    positions = local_order(jnp.arange(group_rows, dtype=jnp.int32))
    before = (positions[None, :] < positions[:, None]).astype(bf16)
    earlier = jnp.dot(before, route_hot.astype(bf16), preferred_element_type=f32)
    slot_index = jnp.sum(earlier * hot_float, axis=1).astype(jnp.int32)
    slot_of = jnp.where(slot_index < capacity, route_ids * capacity + slot_index, slots)
    slot_ids = jnp.arange(slots, dtype=jnp.int32)
    pick_rows = barrier((slot_ids[:, None] == slot_of[None, :]).astype(bf16))
    pick_slots = barrier((slot_of[:, None] == slot_ids[None, :]).astype(bf16))

    def by_expert(values):
        return values.transpose(1, 0, 2, 3).reshape(slots, values.shape[-1])

    def send_slots(cols_mine):
        picked = jnp.dot(pick_rows, cols_mine, preferred_element_type=f32).astype(bf16)
        picked = picked.reshape(owner_count, local_experts * capacity, -1)
        arrived = lax.all_to_all(picked, "expert", split_axis=0, concat_axis=0, tiled=True)
        return by_expert(arrived.reshape(owner_count, local_experts, capacity, -1))

    def return_slots(mine):
        mine = by_expert(mine.reshape(local_experts, owner_count, capacity, -1))
        mine = mine.reshape(owner_count, local_experts * capacity, -1)
        back = lax.all_to_all(mine, "expert", split_axis=0, concat_axis=0, tiled=True)
        return back.reshape(slots, -1)

    def unslot(back):
        rows = jnp.dot(pick_slots, back, preferred_element_type=f32).astype(bf16)
        return [
            whole.astype(f32) for whole in turn_pair(rows, back.shape[1] // own_cols)
        ]

    cot_all = gather_rows(cotangent)
    token_f32 = tokens.astype(f32)
    normed_one = layer_norm(token_f32, norm1_gain).astype(bf16)
    normed_all = gather_rows(normed_one)
    projected = jnp.einsum("gd,cdk->cgk", normed_all, w_qkv, preferred_element_type=f32).astype(
        bf16
    )
    labels = segments[0]
    attn_heads = attend(labels, projected)
    attn_part = jnp.dot(attn_heads, w_out, preferred_element_type=f32)
    attn_own = scatter_rows(attn_part, f32)
    middle = token_f32 + attn_own
    normed_two = layer_norm(middle, norm2_gain).astype(bf16)
    hidden_all = gather_rows(normed_two)

    gate_w = jnp.concatenate([w_router, w_mix], axis=1)

    def gates(logits, hot):
        router_soft = jax.nn.softmax(logits[:, :experts_all], axis=-1)
        return jax.nn.softmax(logits[:, experts_all:], axis=-1), jnp.sum(
            router_soft * hot, axis=-1
        )

    logits = jnp.dot(hidden_all, gate_w, preferred_element_type=f32)
    mix_all, gate_all = gates(logits, hot_float)

    expert_grad_rows = (my_cols(cot_all) * (mix_all[:, 1] * gate_all)[:, None]).astype(bf16)
    arrived = send_slots(jnp.concatenate([my_cols(hidden_all), expert_grad_rows], axis=1))

    dense_grad_rows = barrier((cot_all * mix_all[:, 0:1]).astype(bf16))
    if special:
        y_keep, y_away, dx_keep, dx_away, grad_w_up, grad_w_down = feed_forward(
            hidden_all, dense_grad_rows, w_up, w_down
        )
        dense_own = y_keep + swap(y_away).astype(f32)
        dense_back_own = dx_keep + swap(dx_away).astype(f32)
    else:
        pre_up = jnp.dot(hidden_all, w_up, preferred_element_type=f32)
        act_up = jax.nn.gelu(pre_up).astype(bf16)
        dense_own = scatter_rows(jnp.dot(act_up, w_down, preferred_element_type=f32))
        grad_act_up = jnp.einsum("gd,fd->gf", dense_grad_rows, w_down, preferred_element_type=f32)
        grad_pre_up = gelu_grad(pre_up, grad_act_up).astype(bf16)
        grad_w_down = jnp.einsum("gf,gd->fd", act_up, dense_grad_rows, preferred_element_type=f32)
        grad_w_up = jnp.einsum("gd,gf->df", hidden_all, grad_pre_up, preferred_element_type=f32)
        dense_back_own = scatter_rows(
            jnp.einsum("gf,df->gd", grad_pre_up, w_up, preferred_element_type=f32)
        )

    arrived, grad_w_up = barrier((arrived, grad_w_up))
    slots_in, grad_slots_in = join_cols(arrived, 2)
    if special:
        dense_shapes = [grad_w_up.shape, grad_w_down.shape]
        share = (6, 6, 4)
        keep, away, act_exp, dact_exp, state = expert_data(
            slots_in,
            grad_slots_in,
            w_exp_up[0],
            w_exp_down[0],
            Ride(0, 1, [grad_w_up, grad_w_down], dense_shapes, 1024, share, 2),
        )
        mine = (keep + swap(away).astype(f32)).astype(bf16)
        mine, act_exp = barrier((mine, act_exp))
        back = return_slots(mine)
        grad_w_exp_up, grad_w_exp_down = expert_weights(
            slots_in, grad_slots_in, act_exp, dact_exp
        )
        state, grad_w_exp_up = barrier((state, grad_w_exp_up))
        (state,) = ride_alone(Ride(1, MIDDLE, [state], dense_shapes, 1024, share), 2)
        back, state = barrier((back, state))
        grad_w_exp_up, grad_w_exp_down = grad_w_exp_up[None], grad_w_exp_down[None]
        expert_own, grad_expert_own = unslot(back)
    else:
        slots_in, grad_slots_in = (
            v.reshape(local_experts, owner_count * capacity, model_width)
            for v in (slots_in, grad_slots_in)
        )
        pre_exp = jnp.einsum("lsd,ldf->lsf", slots_in, w_exp_up, preferred_element_type=f32)
        act_exp = jax.nn.gelu(pre_exp).astype(bf16)
        out_exp = jnp.einsum("lsf,lfd->lsd", act_exp, w_exp_down, preferred_element_type=f32)
        (expert_own,) = unslot(return_slots(scatter_cols(out_exp.reshape(slots, model_width))))
        grad_act_exp = jnp.einsum(
            "lsd,lfd->lsf", grad_slots_in, w_exp_down, preferred_element_type=f32
        )
        grad_pre_exp = gelu_grad(pre_exp, grad_act_exp).astype(bf16)
        grad_slots_out = jnp.einsum(
            "lsf,ldf->lsd", grad_pre_exp, w_exp_up, preferred_element_type=f32
        )
        back = return_slots(scatter_cols(grad_slots_out.reshape(slots, model_width)))
        (grad_expert_own,) = unslot(back)
        grad_w_exp_down = jnp.einsum(
            "lsf,lsd->lfd", act_exp, grad_slots_in, preferred_element_type=f32
        )
        grad_w_exp_up = jnp.einsum(
            "lsd,lsf->ldf", slots_in, grad_pre_exp, preferred_element_type=f32
        )

    logits_own, hot_own = own_rows_of(logits), own_rows_of(hot_float)
    (mix_own, gate_own), gates_pull = jax.vjp(lambda z: gates(z, hot_own), logits_own)
    output = (
        middle + mix_own[:, 0:1] * dense_own + (mix_own[:, 1] * gate_own)[:, None] * expert_own
    ).astype(bf16)
    grad_out = cotangent.astype(f32)
    dense_dot = jnp.sum(grad_out * dense_own, axis=1)
    expert_dot = jnp.sum(grad_out * expert_own, axis=1)
    grad_mix_coef = jnp.stack([dense_dot, gate_own * expert_dot], axis=1)
    (grad_logits,) = gates_pull((grad_mix_coef, mix_own[:, 1] * expert_dot))
    grad_gate_w = lax.dot_general(
        grad_logits,
        normed_two.astype(f32),
        (((0,), (0,)), ((), ())),
        precision=highest,
        preferred_element_type=f32,
    )
    grad_hidden_gate = lax.dot_general(
        grad_logits,
        gate_w.astype(f32),
        (((1,), (1,)), ((), ())),
        precision=highest,
        preferred_element_type=f32,
    )
    grad_hidden_own = dense_back_own + grad_expert_own + grad_hidden_gate
    _, norm_two_pull = jax.vjp(layer_norm, middle, norm2_gain)
    grad_middle_norm, grad_gain2 = norm_two_pull(grad_hidden_own)
    grad_middle = grad_out + grad_middle_norm

    grad_attn_all = gather_rows(grad_middle.astype(bf16))
    if special:
        grad_w_out = jnp.einsum(
            "gk,gd->kd", attn_heads, grad_attn_all, preferred_element_type=f32
        ).astype(bf16)
        rides = [
            Ride(MIDDLE, 8, [state], dense_shapes, 1024, share, RIDE_GAP),
            Ride(0, 4, [grad_w_out], [grad_w_out.shape], 512, (2, 1, 1), 2),
        ]
        grad_w_qkv, keep, away, grad_w_up, grad_w_down, state = attention_back(
            labels, projected, grad_attn_all, w_out, w_qkv, normed_all, rides
        )
        grad_normed_one = keep + swap(away).astype(f32)
    else:
        grad_w_out = jnp.einsum("gk,gd->kd", attn_heads, grad_attn_all, preferred_element_type=f32)
        grad_heads = jnp.einsum(
            "gd,kd->gk", grad_attn_all, w_out, preferred_element_type=f32
        ).astype(bf16)
        grad_qkv = attend_back(labels, projected, grad_heads)
        grad_w_qkv = jnp.einsum("gd,cgk->cdk", normed_all, grad_qkv, preferred_element_type=f32)
        grad_normed_one = scatter_rows(
            jnp.einsum("cgk,cdk->gd", grad_qkv, w_qkv, preferred_element_type=f32)
        )
    _, norm_one_pull = jax.vjp(layer_norm, token_f32, norm1_gain)
    grad_token_norm, grad_gain1 = norm_one_pull(grad_normed_one)
    grad_tokens = grad_middle + grad_token_norm

    small = jnp.concatenate([grad_gain1[None], grad_gain2[None], grad_gate_w], axis=0)
    if special:
        padding = -small.shape[0] % 8
        rides = [
            Ride(0, 8, [grad_w_qkv], [grad_w_qkv.shape], 512, (4, 4, 4)),
            Ride(4, 8, [state], [grad_w_out.shape], 512, (2, 1, 1)),
        ]
        small = jnp.pad(small, ((0, padding), (0, 0)))
        small, grad_w_qkv, grad_w_out = last_sums(rides, small)
    else:
        grad_w_up, grad_w_down, grad_w_qkv, grad_w_out = lax.psum(
            [g.astype(bf16) for g in (grad_w_up, grad_w_down, grad_w_qkv, grad_w_out)], "expert"
        )
        small = lax.psum(small, ("expert", "tensor"))
    grad_w_qkv, grad_w_out, grad_w_up, grad_w_down = (
        g.astype(f32) for g in (grad_w_qkv, grad_w_out, grad_w_up, grad_w_down)
    )
    return (
        output,
        grad_tokens,
        small[0],
        grad_w_qkv,
        grad_w_out,
        small[1],
        grad_w_up,
        grad_w_down,
        small[2 : 2 + experts_all].T,
        small[2 + experts_all : 4 + experts_all].T,
        grad_w_exp_up,
        grad_w_exp_down,
    )


def solution(mesh):
    return jax.shard_map(
        body,
        mesh=mesh,
        in_specs=(
            P(("expert", "tensor"), None),
            P(),
            P(None, None, "tensor"),
            P("tensor", None),
            P(),
            P(None, "tensor"),
            P("tensor", None),
            P(),
            P(),
            P("expert", None, "tensor"),
            P("expert", "tensor", None),
            P("expert", None),
            P("expert", None),
            P(("expert", "tensor"), None),
        ),
        out_specs=(
            P(("expert", "tensor"), None),
            P(("expert", "tensor"), None),
            P(),
            P(None, None, "tensor"),
            P("tensor", None),
            P(),
            P(None, "tensor"),
            P("tensor", None),
            P(),
            P(),
            P("expert", None, "tensor"),
            P("expert", "tensor", None),
        ),
        check_vma=False,
    )
```

```python
import functools

import jax
import jax.numpy as jnp
from jax import lax
from jax.experimental import pallas as pl
from jax.experimental.pallas import tpu as pltpu
from jax.sharding import PartitionSpec as P

HEAD = 64
PROMPT = 512
BLOCK = 256
LANES = 128
PIECE = 256
MASKED = -1e30

epsilon = 1e-05
highest = lax.Precision.HIGHEST
f32 = jnp.float32
bf16 = jnp.bfloat16


def layer_norm(values, norm_gain):
    centred = values - jnp.mean(values, axis=-1, keepdims=True)
    variance = jnp.mean(centred * centred, axis=-1, keepdims=True)
    return centred * lax.rsqrt(variance + epsilon) * norm_gain


def gelu_grad(pre_act, upstream):
    return jax.vjp(jax.nn.gelu, pre_act)[1](upstream)[0]


def nt_dot(left, right):
    return lax.dot_general(left, right, (((1,), (1,)), ((), ())), preferred_element_type=f32)


def nn_dot(left, right):
    return lax.dot_general(left, right, (((1,), (0,)), ((), ())), preferred_element_type=f32)


def tn_dot(left, right):
    return lax.dot_general(left, right, (((0,), (0,)), ((), ())), preferred_element_type=f32)


def fill_bias(row_labels_ref, col_labels_ref, cont_bias, tri_bias, transposed):
    size = cont_bias.shape[0]
    down = lax.broadcasted_iota(jnp.int32, (size, size), 0)
    across = lax.broadcasted_iota(jnp.int32, (size, size), 1)
    ordered = (down <= across) if transposed else (across <= down)
    same = row_labels_ref[...] == col_labels_ref[...]
    cont_bias[...] = jnp.where(ordered & same, 0.0, MASKED)
    down = lax.broadcasted_iota(jnp.int32, (BLOCK, BLOCK), 0)
    across = lax.broadcasted_iota(jnp.int32, (BLOCK, BLOCK), 1)
    ordered = (down <= across) if transposed else (across <= down)
    tri_bias[...] = jnp.where(ordered, 0.0, MASKED)


def head_lanes(half):
    lane = lax.broadcasted_iota(jnp.int32, (1, LANES), 1)
    return (lane < HEAD) if half == 0 else (lane >= HEAD)


def turned(pair):
    return lax.axis_index("tensor") if pair else 0


def attend_kernel(pair, col_ref, row_ref, qp, qc, kp, kc, vp, vc, o_ref, cont_bias, tri_bias):
    @pl.when(pl.program_id(0) == 0)
    def _():
        fill_bias(col_ref, row_ref, cont_bias, tri_bias, False)

    turn = turned(pair)
    scale = HEAD**-0.5
    for part in range(2):
        for inner in range(0, PROMPT, BLOCK):
            upto = inner + BLOCK
            mixed = []
            for half in range(2):
                source = (qc if part else qp)[inner:upto, :]
                query = jnp.where(head_lanes(half), source * scale, 0.0).astype(bf16)
                pieces = []
                if part:
                    pieces.append((kp[...], vp[...], None))
                    pieces.append((kc[:upto, :], vc[:upto, :], cont_bias[inner:upto, :upto]))
                else:
                    if inner:
                        pieces.append((kp[:inner, :], vp[:inner, :], None))
                    pieces.append((kp[inner:upto, :], vp[inner:upto, :], tri_bias[...]))
                scores = []
                for key, _, bias in pieces:
                    score = nt_dot(query, key)
                    scores.append(score if bias is None else score + bias)
                top = functools.reduce(
                    jnp.maximum, [jnp.max(score, axis=1, keepdims=True) for score in scores]
                )
                total, out = 0.0, 0.0
                for score, (_, value, _) in zip(scores, pieces, strict=True):
                    weights = jnp.exp(score - top)
                    total = total + jnp.sum(weights, axis=1, keepdims=True)
                    out = out + nn_dot(weights.astype(bf16), value)
                mixed.append(out / total)
            which = (1 - turn) if part else turn
            o_ref[which, inner:upto, :] = jnp.where(head_lanes(0), mixed[0], mixed[1]).astype(bf16)


def attend_back_part(
    part, pair, qp, qc, kp, kc, vp, vc, gp, gc, d_ref, cont_bias, tri_bias, *accs
):
    turn = turned(pair)
    scale = HEAD**-0.5
    dkp, dkc, dvp, dvc = accs
    for inner in range(0, PROMPT, BLOCK):
        upto = inner + BLOCK
        dq = 0.0
        for half in range(2):
            lanes = head_lanes(half)
            query = jnp.where(lanes, (qc if part else qp)[inner:upto, :] * scale, 0.0)
            query = query.astype(bf16)
            grad = jnp.where(lanes, (gc if part else gp)[inner:upto, :], 0.0).astype(bf16)
            if part:
                pieces = [(kp, vp, dkp, dvp, 0, PROMPT, None)]
                pieces.append((kc, vc, dkc, dvc, 0, upto, cont_bias[:upto, inner:upto]))
            else:
                pieces = [(kp, vp, dkp, dvp, 0, inner, None)] if inner else []
                pieces.append((kp, vp, dkp, dvp, inner, upto, tri_bias[...]))
            scores = []
            for key, _, _, _, at, end, bias in pieces:
                score = nt_dot(key[at:end, :], query)
                scores.append(score if bias is None else score + bias)
            top = functools.reduce(
                jnp.maximum, [jnp.max(score, axis=0, keepdims=True) for score in scores]
            )
            scores = [jnp.exp(score - top) for score in scores]
            total = sum(jnp.sum(score, axis=0, keepdims=True) for score in scores)
            scores = [score * (1.0 / total) for score in scores]
            grads = [
                nt_dot(value[at:end, :], grad) for _, value, _, _, at, end, _ in pieces
            ]
            row_dot = sum(
                jnp.sum(score * up, axis=0, keepdims=True)
                for score, up in zip(scores, grads, strict=True)
            )
            for score, up, (key, _, dk, dv, at, end, _) in zip(
                scores, grads, pieces, strict=True
            ):
                grad_scores = (score * (up - row_dot)).astype(bf16)
                dv[at:end, :] += nn_dot(score.astype(bf16), grad)
                dk[at:end, :] += nn_dot(grad_scores, query)
                masked = jnp.where(lanes, key[at:end, :] * scale, 0.0).astype(bf16)
                dq = dq + tn_dot(grad_scores, masked)
        which = (1 - turn) if part else turn
        d_ref[0, which, inner:upto, :] = dq.astype(bf16)


def attend_back_phases(pair, step, col_ref, row_ref, *refs):
    qp, qc, kp, kc, vp, vc, gp, gc, d_ref, cont_bias, tri_bias, *accs = refs

    def prompt():
        @pl.when(step == 0)
        def _():
            fill_bias(col_ref, row_ref, cont_bias, tri_bias, True)

        for acc in accs:
            acc[...] = jnp.zeros_like(acc)
        attend_back_part(0, pair, *refs)

    def continuations():
        attend_back_part(1, pair, *refs)
        turn = turned(pair)
        for number, acc in enumerate(accs):
            which = (1 - turn) if number % 2 else turn
            d_ref[1 + number // 2, which] = acc[...].astype(bf16)

    return [prompt, continuations]


def attend_back_kernel(pair, *refs):
    for phase in attend_back_phases(pair, pl.program_id(0), *refs):
        phase()


def half_specs(size, lead, pair, steps=None):
    blank = (pl.Squeezed(),) * (1 if lead is None else 2)

    def spec(cont):
        def index(i):
            i = i if steps is None else jnp.minimum(i, steps - 1)
            half = 1 - turned(pair) if cont else turned(pair)
            return (half, 0, i) if lead is None else (lead, half, 0, i)

        return pl.BlockSpec((*blank, size, LANES), index)

    return [spec(False), spec(True)]


def attend_call(kernel, name, labels, projected, grad_heads, dots, accs):
    rows, cols = projected.shape[1:]
    cont = rows - PROMPT
    pair = paired()
    kernel = functools.partial(kernel, pair)
    halves = projected.reshape(3, 2, PROMPT, cols)
    work = 2 * rows * rows * cols * dots
    back = grad_heads is not None
    lead = (3,) if back else ()
    specs = [s for c in range(3) for s in half_specs(PROMPT, c, pair)]
    args = [halves] * 6
    if back:
        specs += half_specs(PROMPT, None, pair)
        args += [grad_heads.reshape(2, PROMPT, cols)] * 2
    specs = [
        pl.BlockSpec((cont, 1), lambda i: (0, 0)),
        pl.BlockSpec((1, cont), lambda i: (0, 0)),
        *specs,
    ]
    out_spec = pl.BlockSpec(
        (*lead, 2, PROMPT, LANES), lambda i: (*(0 for _ in lead), 0, 0, i)
    )
    out_shape = jax.ShapeDtypeStruct((*lead, 2, PROMPT, cols), bf16)
    scratch = [
        pltpu.VMEM((cont, cont), f32),
        pltpu.VMEM((BLOCK, BLOCK), f32),
        *[pltpu.VMEM((PROMPT, LANES), f32)] * accs,
    ]
    args = [labels[:, None], labels[None, :], *args]
    steps = cols // LANES
    out = pl.pallas_call(
        kernel,
        grid=(steps,),
        in_specs=specs,
        out_specs=out_spec,
        scratch_shapes=scratch,
        out_shape=out_shape,
        cost_estimate=pl.CostEstimate(
            flops=work, bytes_accessed=14 * rows * cols, transcendentals=rows * rows * 4
        ),
        name=name,
    )(*args)
    return out.reshape(*lead, rows, cols)


def attend(labels, projected):
    return attend_call(attend_kernel, "attend", labels, projected, None, 2, 0)


def attend_back(labels, projected, grad_heads):
    return attend_call(
        attend_back_kernel, "attend_back", labels, projected, grad_heads, 5, 4
    )


HIDDEN = 512
ROWS = 512
CUT = 256
MIDDLE = 4
RIDE_GAP = 2


def gelu_both(pre_act):
    slope = 0.7978845608028654
    square = pre_act * pre_act
    bend = jnp.tanh(slope * (pre_act + 0.044715 * (square * pre_act)))
    share = 0.5 * (1.0 + bend)
    steep = 0.5 * slope * (1.0 + (3 * 0.044715) * square)
    return pre_act * share, share + pre_act * (1.0 - bend * bend) * steep


def feed_rows(first, at, x_ref, dy_ref, wu_ref, wd_ref, act, dact, y_acc, dx_acc):
    pre_act = nn_dot(x_ref[at, :], wu_ref[...])
    up = nt_dot(dy_ref[at, :], wd_ref[...])
    value, slope = gelu_both(pre_act)
    value = value.astype(bf16)
    back = (up * slope).astype(bf16)
    act[at, :] = value
    dact[at, :] = back
    out = nn_dot(value, wd_ref[...])
    grad = nt_dot(back, wu_ref[...])

    @pl.when(first)
    def _():
        y_acc[at, :] = out
        dx_acc[at, :] = grad

    @pl.when(jnp.logical_not(first))
    def _():
        y_acc[at, :] += out
        dx_acc[at, :] += grad


def feed_down(x_ref, dy_ref, act, dact, gu_ref, gd_ref):
    for at in range(0, gd_ref.shape[0], CUT):
        gd_ref[at : at + CUT, :] = tn_dot(act[:, at : at + CUT], dy_ref[...]).astype(gd_ref.dtype)


def feed_up(x_ref, dy_ref, act, dact, gu_ref, gd_ref):
    for at in range(0, gu_ref.shape[0], CUT):
        gu_ref[at : at + CUT, :] = tn_dot(x_ref[:, at : at + CUT], dact[...]).astype(gu_ref.dtype)


def feed_kernel(x_ref, dy_ref, wu_ref, wd_ref, *refs):
    yk, ya, dxk, dxa, gu_ref, gd_ref, act, dact, y_acc, dx_acc = refs
    step = pl.program_id(0)
    for at in range(0, x_ref.shape[0], ROWS):
        rows = slice(at, at + ROWS)
        feed_rows(step == 0, rows, x_ref, dy_ref, wu_ref, wd_ref, act, dact, y_acc, dx_acc)
    feed_down(x_ref, dy_ref, act, dact, gu_ref, gd_ref)
    feed_up(x_ref, dy_ref, act, dact, gu_ref, gd_ref)

    @pl.when(step == pl.num_programs(0) - 1)
    def _():
        half = yk.shape[0]
        yk[...] = y_acc[:half, :]
        dxk[...] = dx_acc[:half, :]
        ya[...] = y_acc[half:, :].astype(bf16)
        dxa[...] = dx_acc[half:, :].astype(bf16)


def one_buffer(shape):
    return pl.BlockSpec(shape, lambda *_: (0,) * len(shape), pipeline_mode=pl.Buffered(1))


def feed_forward(x, dy, w_up, w_down):
    rows, width = x.shape
    hidden = w_up.shape[1]
    tile = min(HIDDEN, hidden)
    half = rows // 2
    block = jax.ShapeDtypeStruct((half, width), f32)
    sent = jax.ShapeDtypeStruct((half, width), bf16)
    return pl.pallas_call(
        feed_kernel,
        grid=(hidden // tile,),
        in_specs=[
            one_buffer((rows, width)),
            one_buffer((rows, width)),
            pl.BlockSpec((width, tile), lambda i: (0, i)),
            pl.BlockSpec((tile, width), lambda i: (i, 0)),
        ],
        out_specs=[
            *[one_buffer((half, width))] * 4,
            pl.BlockSpec((width, tile), lambda i: (0, i)),
            pl.BlockSpec((tile, width), lambda i: (i, 0)),
        ],
        out_shape=[
            block,
            sent,
            block,
            sent,
            jax.ShapeDtypeStruct((width, hidden), bf16),
            jax.ShapeDtypeStruct((hidden, width), bf16),
        ],
        scratch_shapes=[
            pltpu.VMEM((rows, tile), bf16),
            pltpu.VMEM((rows, tile), bf16),
            pltpu.VMEM((rows, width), f32),
            pltpu.VMEM((rows, width), f32),
        ],
        compiler_params=pltpu.CompilerParams(vmem_limit_bytes=56 * 1024 * 1024),
        cost_estimate=pl.CostEstimate(
            flops=12 * rows * width * hidden,
            bytes_accessed=8 * width * hidden + 12 * rows * width,
            transcendentals=rows * hidden,
        ),
        name="feed_forward",
    )(x, dy, w_up, w_down)


ORDERS = ((1, 2, 4, 8), (2, 4, 1, 8), (4, 1, 2, 8))
DEPTH = 4
MESH = pl.DeviceIdType.MESH


def partner_of(bit):
    me = lax.axis_index("expert")
    side = lax.rem(me // bit, 2)
    return me + bit * (1 - 2 * side), side


def greet(core):
    barrier = pltpu.get_barrier_semaphore()
    for bit in sorted(ORDERS[0]):
        pl.semaphore_signal(
            barrier, 1, device_id={"expert": partner_of(bit)[0]}, device_id_type=MESH
        )
    if core:
        other = 1 - lax.axis_index("tensor")
        pl.semaphore_signal(barrier, 1, device_id={"tensor": other}, device_id_type=MESH)
    pl.semaphore_wait(barrier, DEPTH + core)


class Ride:
    def __init__(self, level_in, level_out, values, shapes, width, counts, gap=1):
        self.first, self.last = level_in, level_out
        self.values, self.shapes, self.width, self.counts = list(values), shapes, width, counts
        layout = split_layout(shapes, width)
        self.pieces = sum(map(len, layout))
        self.where = [(a, piece) for a, pieces in enumerate(layout) for piece in pieces]
        stages = range(level_out - level_in + 1)
        self.delays = [gap * stage for stage in stages] if isinstance(gap, int) else gap
        self.ticks = max(counts) + self.delays[-1]

    def rows_at(self, level):
        return PIECE >> (level if level <= DEPTH else 2 * DEPTH - level)

    def out_shape(self):
        shapes = self.shapes
        if self.last < 2 * DEPTH:
            shapes = [(self.pieces, self.rows_at(self.last), self.width)]
        return [jax.ShapeDtypeStruct(shape, bf16) for shape in shapes]

    def scratch(self):
        shapes = []
        if self.first < DEPTH:
            shapes.append(self.rows_at(self.first))
            shapes += [self.rows_at(n + 1) for n in range(self.first, min(self.last, DEPTH))]
        if self.last > DEPTH:
            shapes.append(self.rows_at(self.last))
        hops = self.last - self.first
        return [
            *[pltpu.VMEM((self.pieces, rows, self.width), bf16) for rows in shapes],
            pltpu.SemaphoreType.DMA((hops, self.pieces)),
            pltpu.SemaphoreType.DMA((hops, self.pieces)),
            pltpu.SemaphoreType.DMA((self.pieces,)),
            pltpu.SemaphoreType.DMA((self.pieces,)),
        ]

    def bind(self, ins, outs, scratch):
        self.ins, self.outs = ins, outs
        *buffers, self.send_sem, self.recv_sem, self.load_sem, self.store_sem = scratch
        self.held = buffers[0] if self.first < DEPTH else None
        self.got = buffers[1 : 1 + max(0, min(self.last, DEPTH) - self.first)]
        self.full = buffers[-1] if self.last > DEPTH else None
        self.sides = {bit: partner_of(bit) for bit in ORDERS[0]}

    def held_at(self, order, level):
        total = 0
        for n in range(self.first, level):
            total = total + self.sides[order[n]][1] * self.rows_at(n + 1)
        return pl.multiple_of(total, 16)

    def full_at(self, order, level):
        total = 0
        for n in range(2 * DEPTH - self.last, 2 * DEPTH - level):
            total = total + self.sides[order[n]][1] * self.rows_at(n + 1)
        return pl.multiple_of(total, 16)

    def color_of(self, piece):
        color = 0
        while piece >= sum(self.counts[: color + 1]):
            color += 1
        return color

    def load(self, piece):
        sem = self.load_sem.at[piece]
        if self.first == 0:
            a, parts = self.where[piece]
            return [
                pltpu.make_async_copy(self.ins[a].at[src], self.held.at[(piece, *dst)], sem)
                for src, dst in parts
            ]
        if self.first < DEPTH:
            return [pltpu.make_async_copy(self.ins[0].at[piece], self.held.at[piece], sem)]
        order = ORDERS[self.color_of(piece)]
        at = pl.ds(self.full_at(order, self.first), self.rows_at(self.first))
        return [pltpu.make_async_copy(self.ins[0].at[piece], self.full.at[piece, at], sem)]

    def await_load(self, order, piece):
        sem = self.load_sem.at[piece]
        if self.first < DEPTH:
            whole = self.held.at[piece]
        else:
            at = pl.ds(self.full_at(order, self.first), self.rows_at(self.first))
            whole = self.full.at[piece, at]
        pltpu.make_async_copy(whole, whole, sem).wait()

    def stores(self, piece):
        sem = self.store_sem.at[piece]
        if self.last == 2 * DEPTH:
            a, parts = self.where[piece]
            return [
                pltpu.make_async_copy(self.full.at[(piece, *dst)], self.outs[a].at[src], sem)
                for src, dst in parts
            ]
        if self.last > DEPTH:
            return [pltpu.make_async_copy(self.full.at[piece], self.outs[0].at[piece], sem)]
        order = ORDERS[self.color_of(piece)]
        at = pl.ds(self.held_at(order, self.last), self.rows_at(self.last))
        return [pltpu.make_async_copy(self.held.at[piece, at], self.outs[0].at[piece], sem)]

    def start_store(self, order, piece):
        if self.last == 2 * DEPTH:
            for number in range(self.pieces):

                @pl.when(piece == number)
                def _(number=number):
                    for copy in self.stores(number):
                        copy.start()

            return
        sem = self.store_sem.at[piece]
        if self.last > DEPTH:
            source = self.full.at[piece]
        else:
            at = pl.ds(self.held_at(order, self.last), self.rows_at(self.last))
            source = self.held.at[piece, at]
        pltpu.make_async_copy(source, self.outs[0].at[piece], sem).start()

    def exchange(self, order, hop, piece):
        sems = (self.send_sem.at[hop - self.first, piece], self.recv_sem.at[hop - self.first, piece])
        if hop < DEPTH:
            target, side = self.sides[order[hop]]
            size = self.rows_at(hop + 1)
            away = pl.multiple_of(self.held_at(order, hop) + (1 - side) * size, 16)
            source = self.held.at[piece, pl.ds(away, size)]
            dest = self.got[hop - self.first].at[piece]
        else:
            target, _ = self.sides[order[2 * DEPTH - 1 - hop]]
            at = pl.ds(self.full_at(order, hop), self.rows_at(hop))
            source = dest = self.full.at[piece, at]
        return pltpu.make_async_remote_copy(
            source, dest, *sems, device_id={"expert": target}, device_id_type=MESH
        )

    def run(self, color, stage, piece):
        order = ORDERS[color]
        if stage == 0:
            self.await_load(order, piece)
        else:
            hop = self.first + stage - 1
            self.exchange(order, hop, piece).wait()
            if hop < DEPTH:
                size = self.rows_at(hop + 1)
                at = pl.ds(self.held_at(order, hop + 1), size)
                total = self.held[piece, at, :].astype(f32)
                total = (total + self.got[hop - self.first][piece].astype(f32)).astype(bf16)
                if hop + 1 == DEPTH and self.last > DEPTH:
                    self.full[piece, pl.ds(self.full_at(order, DEPTH), size), :] = total
                else:
                    self.held[piece, at, :] = total
        if self.first + stage < self.last:
            self.exchange(order, self.first + stage, piece).start()
        else:
            self.start_store(order, piece)

    def begin(self):
        for piece in range(self.pieces):
            for copy in self.load(piece):
                copy.start()

    def tick(self, t):
        for stage in range(self.last - self.first + 1):
            for color, count in enumerate(self.counts):

                at = t - self.delays[stage]

                @pl.when((at >= 0) & (at < count))
                def _(color=color, stage=stage, at=at):
                    self.run(color, stage, sum(self.counts[:color]) + at)

    def end(self):
        for piece in range(self.pieces):
            for copy in self.stores(piece):
                copy.wait()


any_spec = pl.BlockSpec(memory_space=pl.ANY)


def carry(
    phases, steps, specs, out_specs, out_shape, scratch, args, rides, name, flops, collective, core=False
):
    n_ticks = max(ride.ticks for ride in rides)
    ride_outs = [ride.out_shape() for ride in rides]
    parts = 2
    grid = max(steps, -(-n_ticks // parts))

    def clamp(spec):
        if spec.index_map is None:
            return spec
        return pl.BlockSpec(
            spec.block_shape,
            lambda i: spec.index_map(jnp.minimum(i, steps - 1)),
            pipeline_mode=spec.pipeline_mode,
        )

    n_in, n_out = len(args), len(out_shape)

    def kernel(*refs):
        refs = list(refs)
        take = lambda count: [refs.pop(0) for _ in range(count)]
        main_in = take(n_in)
        ins = [take(len(ride.values)) for ride in rides]
        main_out = take(n_out)
        outs = [take(len(shapes)) for shapes in ride_outs]
        main_scratch = take(len(scratch))
        for ride, got, out in zip(rides, ins, outs, strict=True):
            ride.bind(got, out, take(len(ride.scratch())))
        step = pl.program_id(0)

        @pl.when(step == 0)
        def _():
            for ride in rides:
                ride.begin()
            greet(core)

        for number, phase in enumerate(phases(step, *main_in, *main_out, *main_scratch)):
            for ride in rides:
                ride.tick(step * parts + number)
            pl.when(step < steps)(phase)

        @pl.when(step == grid - 1)
        def _():
            for ride in rides:
                ride.end()

    moved = sum(v.size for ride in rides for v in ride.values)
    return pl.pallas_call(
        kernel,
        grid_spec=pltpu.PrefetchScalarGridSpec(
            num_scalar_prefetch=0,
            grid=(grid,),
            in_specs=[*map(clamp, specs), *[any_spec] * sum(len(ride.values) for ride in rides)],
            out_specs=[*map(clamp, out_specs), *[any_spec] * sum(map(len, ride_outs))],
            scratch_shapes=[*scratch, *[m for ride in rides for m in ride.scratch()]],
        ),
        out_shape=[*out_shape, *[shape for shapes in ride_outs for shape in shapes]],
        compiler_params=pltpu.CompilerParams(
            collective_id=collective, has_side_effects=True, vmem_limit_bytes=62 * 1024 * 1024
        ),
        cost_estimate=pl.CostEstimate(flops=flops, bytes_accessed=4 * moved, transcendentals=0),
        name=name,
    )(*args, *[v for ride in rides for v in ride.values])


def split_layout(shapes, width):
    layout = []
    for shape in shapes:
        pieces = []
        leads = [(c,) for c in range(shape[0])] if len(shape) == 3 else [()]
        for lead in leads:
            for c in range(0, shape[-1], width):
                for r in range(0, shape[-2], PIECE):
                    pieces.append([((*lead, slice(r, r + PIECE), slice(c, c + width)), ())])
        layout.append(pieces)
    return layout


def last_kernel(rides, small_in, *refs):
    refs = list(refs)
    take = lambda count: [refs.pop(0) for _ in range(count)]
    ins = [take(len(ride.values)) for ride in rides]
    (small_out,) = take(1)
    outs = [take(len(ride.out_shape())) for ride in rides]
    small, small_got, small_sem = take(3)
    for ride, got, out in zip(rides, ins, outs, strict=True):
        ride.bind(got, out, take(len(ride.scratch())))
    bits = sorted(ORDERS[0])

    def small_copy(step):
        if step < DEPTH:
            target = {"expert": partner_of(bits[step])[0]}
        else:
            target = {"tensor": 1 - lax.axis_index("tensor")}
        return pltpu.make_async_remote_copy(
            small.at[step],
            small_got.at[step],
            small_sem.at[0, step],
            small_sem.at[1, step],
            device_id=target,
            device_id_type=MESH,
        )

    for ride in rides:
        ride.begin()
    first = pltpu.make_async_copy(small_in, small.at[0], small_sem.at[2, 0])
    first.start()
    greet(True)

    def step(t, _):
        for ride in rides:
            ride.tick(t)
        for number in range(DEPTH + 2):

            @pl.when(t == number)
            def _(number=number):
                if number == 0:
                    first.wait()
                else:
                    small_copy(number - 1).wait()
                    small[number] = small[number - 1] + small_got[number - 1]
                if number < DEPTH + 1:
                    small_copy(number).start()

        return 0

    lax.fori_loop(0, max(ride.ticks for ride in rides), step, 0)
    out = pltpu.make_async_copy(small.at[DEPTH + 1], small_out, small_sem.at[2, 1])
    out.start()
    for ride in rides:
        ride.end()
    out.wait()


def alone_kernel(ride, *refs):
    count = len(ride.values)
    ride.bind(refs[:count], refs[count : count + 1], refs[count + 1 :])
    ride.begin()
    greet(False)

    def step(t, _):
        ride.tick(t)
        return 0

    lax.fori_loop(0, ride.ticks, step, 0)
    ride.end()


def ride_alone(ride, collective):
    return pl.pallas_call(
        functools.partial(alone_kernel, ride),
        in_specs=[any_spec] * len(ride.values),
        out_specs=[any_spec],
        out_shape=ride.out_shape(),
        scratch_shapes=ride.scratch(),
        compiler_params=pltpu.CompilerParams(
            collective_id=collective, has_side_effects=True, vmem_limit_bytes=62 * 1024 * 1024
        ),
        name="ride_alone",
    )(*ride.values)


def last_sums(rides, small):
    ride_outs = [ride.out_shape() for ride in rides]
    values = [v for ride in rides for v in ride.values]
    shapes = [shape for shapes in ride_outs for shape in shapes]
    return pl.pallas_call(
        functools.partial(last_kernel, rides),
        in_specs=[any_spec] * (1 + len(values)),
        out_specs=[any_spec] * (1 + len(shapes)),
        out_shape=[jax.ShapeDtypeStruct(small.shape, f32), *shapes],
        scratch_shapes=[
            pltpu.VMEM((DEPTH + 2, *small.shape), f32),
            pltpu.VMEM((DEPTH + 1, *small.shape), f32),
            pltpu.SemaphoreType.DMA((3, DEPTH + 1)),
            *[m for ride in rides for m in ride.scratch()],
        ],
        compiler_params=pltpu.CompilerParams(
            collective_id=4, has_side_effects=True, vmem_limit_bytes=62 * 1024 * 1024
        ),
        name="last_sums",
    )(small, *values)


def expert_data_phases(steps, step, x_ref, dy_ref, wu_ref, wd_ref, *refs):
    mine, act, dact, y_acc, dx_acc, sent, came, sems = refs
    rows = x_ref.shape[0] // 2
    half = x_ref.shape[1] // 2
    rank = lax.axis_index("tensor")

    def block(number):
        return slice(number * rows, (number + 1) * rows)

    def swap_copy(number):
        return pltpu.make_async_remote_copy(
            sent.at[block(number)],
            came.at[block(number)],
            sems.at[0, number],
            sems.at[1, number],
            device_id={"tensor": 1 - rank},
            device_id_type=MESH,
        )

    def cols(side):
        return slice(side * half, (side + 1) * half)

    def part(number):
        at = block(number)
        feed_rows(step == 0, at, x_ref, dy_ref, wu_ref, wd_ref, act, dact, y_acc, dx_acc)
        for side in range(2):

            @pl.when((step == steps - 1) & (rank == side))
            def _(side=side):
                sent[at, :half] = y_acc[at, cols(1 - side)].astype(bf16)
                sent[at, half:] = dx_acc[at, cols(1 - side)].astype(bf16)

        @pl.when(step == steps - 1)
        def _():
            swap_copy(number).start()

    def finish():
        part(1)

        @pl.when(step == steps - 1)
        def _():
            for number in range(2):
                swap_copy(number).wait()
                at = block(number)
                for side in range(2):

                    @pl.when(rank == side)
                    def _(side=side, at=at):
                        for cut, acc in ((slice(0, half), y_acc), (slice(half, 2 * half), dx_acc)):
                            total = acc[at, cols(side)] + came[at, cut].astype(f32)
                            mine[at, cut] = total.astype(bf16)

    return [functools.partial(part, 0), finish]


def expert_data(x, dy, w_up, w_down, ride):
    rows, width = x.shape
    hidden = w_up.shape[1]
    tile = min(HIDDEN, hidden)
    steps = hidden // tile
    inner = jax.ShapeDtypeStruct((rows, hidden), bf16)
    return carry(
        functools.partial(expert_data_phases, steps),
        steps,
        [
            one_buffer((rows, width)),
            one_buffer((rows, width)),
            pl.BlockSpec((width, tile), lambda i: (0, i)),
            pl.BlockSpec((tile, width), lambda i: (i, 0)),
        ],
        [
            one_buffer((rows, width)),
            *[pl.BlockSpec((rows, tile), lambda i: (0, i))] * 2,
        ],
        [jax.ShapeDtypeStruct((rows, width), bf16), inner, inner],
        [
            pltpu.VMEM((rows, width), f32),
            pltpu.VMEM((rows, width), f32),
            pltpu.VMEM((rows, width), bf16),
            pltpu.VMEM((rows, width), bf16),
            pltpu.SemaphoreType.DMA((2, 2)),
        ],
        [x, dy, w_up, w_down],
        [ride],
        "expert_data",
        8 * rows * width * hidden,
        1,
        True,
    )


def expert_weights_kernel(*refs):
    feed_down(*refs)
    feed_up(*refs)


def expert_weights(x, dy, act, dact):
    rows, width = x.shape
    hidden = act.shape[1]
    tile = min(HIDDEN, hidden)
    return pl.pallas_call(
        expert_weights_kernel,
        grid=(hidden // tile,),
        in_specs=[
            one_buffer((rows, width)),
            one_buffer((rows, width)),
            *[pl.BlockSpec((rows, tile), lambda i: (0, i))] * 2,
        ],
        out_specs=[
            pl.BlockSpec((width, tile), lambda i: (0, i)),
            pl.BlockSpec((tile, width), lambda i: (i, 0)),
        ],
        out_shape=[
            jax.ShapeDtypeStruct((width, hidden), f32),
            jax.ShapeDtypeStruct((hidden, width), f32),
        ],
        compiler_params=pltpu.CompilerParams(vmem_limit_bytes=56 * 1024 * 1024),
        cost_estimate=pl.CostEstimate(
            flops=4 * rows * width * hidden,
            bytes_accessed=8 * width * hidden + 4 * rows * width + 4 * rows * hidden,
            transcendentals=0,
        ),
        name="expert_weights",
    )(x, dy, act, dact)


def attention_back_phases(pairs, step, col_ref, row_ref, da_ref, wo_ref, *refs):
    halves, refs = refs[:6], refs[6:]
    wq_any, normed_any, gq_ref, dh_ref, *refs = refs
    cont_bias, tri_bias, do_s, d_s, dh_acc, wq, normed, sems, sent, came, *accs = refs
    rows = da_ref.shape[0]
    half = rows // 2
    copies = [
        pltpu.make_async_copy(source, dest, sems.at[number])
        for number, (source, dest) in enumerate(
            ((wq_any, wq), (normed_any, normed))
        )
    ]
    swap_copy = pltpu.make_async_remote_copy(
        sent,
        came,
        sems.at[2],
        sems.at[3],
        device_id={"tensor": 1 - lax.axis_index("tensor")},
        device_id_type=MESH,
    )
    turn = turned(True)
    lanes = pl.ds(pl.multiple_of(jnp.minimum(step, pairs - 1) * LANES, LANES), LANES)

    def attend_part(part):
        grads = [do_s.at[which, :, lanes] for which in (turn, 1 - turn)]
        out = d_s.at[:, :, :, lanes]
        attend_back_part(part, True, *halves, *grads, out, cont_bias, tri_bias, *accs)

    which = jnp.clip(step - pairs, 0, 2)

    def first():
        @pl.when(step == 0)
        def _():
            for copy in copies:
                copy.start()
            for number in range(2):
                at = slice(number * half, (number + 1) * half)
                do_s[number] = nt_dot(da_ref[at, :], wo_ref[...]).astype(bf16)
            fill_bias(col_ref, row_ref, cont_bias, tri_bias, True)

        @pl.when(step < pairs)
        def _():
            for acc in accs:
                acc[...] = jnp.zeros_like(acc)
            attend_part(0)

        @pl.when(step == pairs)
        def _():
            for copy in copies:
                copy.wait()
            dh_acc[...] = jnp.zeros_like(dh_acc)

        @pl.when((step >= pairs) & (step < pairs + 3))
        def _():
            for number in range(2):
                dh_acc[number] += nt_dot(d_s[which, number], wq[which])

    def second():
        @pl.when(step < pairs)
        def _():
            attend_part(1)
            for number, acc in enumerate(accs):
                place = (1 - turn) if number % 2 else turn
                d_s[1 + number // 2, place, :, lanes] = acc[...].astype(bf16)

        @pl.when(step == pairs + 2)
        def _():
            sent[...] = dh_acc[1].astype(bf16)
            swap_copy.start()

        @pl.when((step >= pairs) & (step < pairs + 3))
        def _():
            grads = d_s[which].reshape(rows, d_s.shape[-1])
            for at in range(0, normed.shape[1], CUT):
                gq_ref[which, at : at + CUT, :] = tn_dot(normed[:, at : at + CUT], grads).astype(
                    bf16
                )

        @pl.when(step == pairs + 2)
        def _():
            swap_copy.wait()
            dh_ref[...] = dh_acc[0] + came[...].astype(f32)

    return [first, second]


def attention_back(labels, projected, grad_attn, w_out, w_qkv, normed, rides):
    rows, cols = projected.shape[1:]
    width = normed.shape[1]
    cont = rows - PROMPT
    pairs = cols // LANES
    inputs = projected.reshape(3, 2, PROMPT, cols)
    return carry(
        functools.partial(attention_back_phases, pairs),
        pairs + 3,
        [
            one_buffer((cont, 1)),
            one_buffer((1, cont)),
            one_buffer((rows, width)),
            one_buffer((cols, width)),
            *[s for c in range(3) for s in half_specs(PROMPT, c, True, pairs)],
            *[any_spec] * 2,
        ],
        [
            one_buffer((3, width, cols)),
            one_buffer((rows // 2, width)),
        ],
        [
            jax.ShapeDtypeStruct((3, width, cols), bf16),
            jax.ShapeDtypeStruct((rows // 2, width), f32),
        ],
        [
            pltpu.VMEM((cont, cont), f32),
            pltpu.VMEM((BLOCK, BLOCK), f32),
            pltpu.VMEM((2, rows // 2, cols), bf16),
            pltpu.VMEM((3, 2, rows // 2, cols), bf16),
            pltpu.VMEM((2, rows // 2, width), f32),
            pltpu.VMEM(w_qkv.shape, bf16),
            pltpu.VMEM(normed.shape, bf16),
            pltpu.SemaphoreType.DMA((4,)),
            pltpu.VMEM((rows // 2, width), bf16),
            pltpu.VMEM((rows // 2, width), bf16),
            *[pltpu.VMEM((PROMPT, LANES), f32)] * 4,
        ],
        [labels[:, None], labels[None, :], grad_attn, w_out, *[inputs] * 6, w_qkv, normed],
        rides,
        "attention_back",
        2 * rows * rows * cols * 5,
        3,
        True,
    )


def paired():
    return lax.axis_size("tensor") == 2


def swap(values):
    return lax.ppermute(values, "tensor", [(0, 1), (1, 0)])


def gather_rows(own):
    if paired():
        return jnp.concatenate([own, swap(own)], axis=0)
    return lax.all_gather(own, "tensor", axis=0, tiled=True)


def scatter_rows(partial, kind=bf16):
    if paired():
        size = partial.shape[0] // 2
        return partial[:size] + swap(partial[size:].astype(kind)).astype(f32)
    return lax.psum_scatter(
        partial.astype(kind), "tensor", scatter_dimension=0, tiled=True
    ).astype(f32)


def own_rows_of(values):
    size = values.shape[0] // lax.axis_size("tensor")
    if paired():
        return values[:size]
    return lax.dynamic_slice_in_dim(values, lax.axis_index("tensor") * size, size, 0)


def local_order(values):
    if paired():
        size = values.shape[0] // 2
        turned = jnp.concatenate([values[size:], values[:size]], axis=0)
        return jnp.where(lax.axis_index("tensor") == 0, values, turned)
    return values


def scatter_cols(partial):
    size = partial.shape[1] // lax.axis_size("tensor")
    rank = lax.axis_index("tensor")
    if paired():
        keep = lax.dynamic_slice_in_dim(partial, rank * size, size, 1)
        away = lax.dynamic_slice_in_dim(partial, (1 - rank) * size, size, 1).astype(bf16)
        return (keep + swap(away).astype(f32)).astype(bf16)
    return lax.psum_scatter(partial.astype(bf16), "tensor", scatter_dimension=1, tiled=True)


def turn_pair(cols_mine, count):
    width = cols_mine.shape[1] // count
    if not paired():
        return [
            lax.all_to_all(cols_mine[:, at : at + width], "tensor", 0, 1, tiled=True)
            for at in range(0, count * width, width)
        ]
    size = cols_mine.shape[0] // 2
    own, other = cols_mine[:size], swap(cols_mine[size:])
    first = lax.axis_index("tensor") == 0
    left, right = jnp.where(first, own, other), jnp.where(first, other, own)
    return [
        jnp.concatenate([left[:, at : at + width], right[:, at : at + width]], axis=1)
        for at in range(0, count * width, width)
    ]


def join_kernel(own_ref, other_ref, *outs):
    size = own_ref.shape[1] // len(outs)
    rank = lax.axis_index("tensor")
    for side in range(2):

        @pl.when(rank == side)
        def _(side=side):
            for number, out in enumerate(outs):
                cols = slice(number * size, (number + 1) * size)
                out[:, side * size : (side + 1) * size] = own_ref[:, cols]
                out[:, (1 - side) * size : (2 - side) * size] = other_ref[:, cols]


def join_cols(own, count):
    rows, width = own.shape
    if not paired():
        whole = lax.all_gather(own.reshape(rows, count, -1), "tensor", axis=2, tiled=True)
        return [whole[:, number] for number in range(count)]
    step = min(rows, 256)
    outs = [jax.ShapeDtypeStruct((rows, 2 * width // count), own.dtype)] * count
    return pl.pallas_call(
        join_kernel,
        grid=(rows // step,),
        in_specs=[pl.BlockSpec((step, width), lambda i: (i, 0))] * 2,
        out_specs=[pl.BlockSpec((step, 2 * width // count), lambda i: (i, 0))] * count,
        out_shape=outs,
        cost_estimate=pl.CostEstimate(
            flops=0, bytes_accessed=8 * rows * width, transcendentals=0
        ),
        name="join_cols",
    )(own, swap(own))


def body(
    tokens,
    norm1_gain,
    w_qkv,
    w_out,
    norm2_gain,
    w_up,
    w_down,
    w_router,
    w_mix,
    w_exp_up,
    w_exp_down,
    routes,
    segments,
    cotangent,
):
    own_rows = tokens.shape[0]
    model_width = tokens.shape[1]
    tensor_size = lax.axis_size("tensor")
    tensor_rank = lax.axis_index("tensor")
    owner_count = lax.axis_size("expert")
    group_rows = own_rows * tensor_size
    own_cols = model_width // tensor_size
    experts_all = w_router.shape[1]
    local_experts = w_exp_up.shape[0]
    capacity = group_rows // experts_all
    slots = experts_all * capacity
    barrier = lax.optimization_barrier
    special = owner_count == 16 and tensor_size == 2 and local_experts == 1

    def my_cols(values):
        return lax.dynamic_slice_in_dim(values, tensor_rank * own_cols, own_cols, 1)

    route_ids = local_order(routes[:, 0])
    route_hot = route_ids[:, None] == jnp.arange(experts_all, dtype=jnp.int32)[None, :]
    hot_float = route_hot.astype(f32)
    positions = local_order(jnp.arange(group_rows, dtype=jnp.int32))
    before = (positions[None, :] < positions[:, None]).astype(bf16)
    earlier = jnp.dot(before, route_hot.astype(bf16), preferred_element_type=f32)
    slot_index = jnp.sum(earlier * hot_float, axis=1).astype(jnp.int32)
    slot_of = jnp.where(slot_index < capacity, route_ids * capacity + slot_index, slots)
    slot_ids = jnp.arange(slots, dtype=jnp.int32)
    pick_rows = barrier((slot_ids[:, None] == slot_of[None, :]).astype(bf16))
    pick_slots = barrier((slot_of[:, None] == slot_ids[None, :]).astype(bf16))

    def by_expert(values):
        return values.transpose(1, 0, 2, 3).reshape(slots, values.shape[-1])

    def send_slots(cols_mine):
        picked = jnp.dot(pick_rows, cols_mine, preferred_element_type=f32).astype(bf16)
        picked = picked.reshape(owner_count, local_experts * capacity, -1)
        arrived = lax.all_to_all(picked, "expert", split_axis=0, concat_axis=0, tiled=True)
        return by_expert(arrived.reshape(owner_count, local_experts, capacity, -1))

    def return_slots(mine):
        mine = by_expert(mine.reshape(local_experts, owner_count, capacity, -1))
        mine = mine.reshape(owner_count, local_experts * capacity, -1)
        back = lax.all_to_all(mine, "expert", split_axis=0, concat_axis=0, tiled=True)
        return back.reshape(slots, -1)

    def unslot(back):
        rows = jnp.dot(pick_slots, back, preferred_element_type=f32).astype(bf16)
        return [
            whole.astype(f32) for whole in turn_pair(rows, back.shape[1] // own_cols)
        ]

    cot_all = gather_rows(cotangent)
    token_f32 = tokens.astype(f32)
    normed_one = layer_norm(token_f32, norm1_gain).astype(bf16)
    normed_all = barrier(gather_rows(normed_one))
    projected = jnp.einsum("gd,cdk->cgk", normed_all, w_qkv, preferred_element_type=f32).astype(
        bf16
    )
    labels = segments[0]
    attn_heads = attend(labels, projected)
    attn_part = jnp.dot(attn_heads, w_out, preferred_element_type=f32)
    attn_own = scatter_rows(attn_part)
    middle = token_f32 + attn_own
    normed_two = layer_norm(middle, norm2_gain).astype(bf16)
    hidden_all = gather_rows(normed_two)

    gate_w = jnp.concatenate([w_router, w_mix], axis=1)

    def gates(logits, hot):
        router_soft = jax.nn.softmax(logits[:, :experts_all], axis=-1)
        return jax.nn.softmax(logits[:, experts_all:], axis=-1), jnp.sum(
            router_soft * hot, axis=-1
        )

    logits = jnp.dot(hidden_all, gate_w, preferred_element_type=f32)
    mix_all, gate_all = gates(logits, hot_float)

    expert_grad_rows = (my_cols(cot_all) * (mix_all[:, 1] * gate_all)[:, None]).astype(bf16)
    arrived = send_slots(jnp.concatenate([my_cols(hidden_all), expert_grad_rows], axis=1))

    dense_grad_rows = barrier((cot_all * mix_all[:, 0:1]).astype(bf16))
    if special:
        y_keep, y_away, dx_keep, dx_away, grad_w_up, grad_w_down = feed_forward(
            hidden_all, dense_grad_rows, w_up, w_down
        )
        dense_own = y_keep + swap(y_away).astype(f32)
        dense_back_own = dx_keep + swap(dx_away).astype(f32)
    else:
        pre_up = jnp.dot(hidden_all, w_up, preferred_element_type=f32)
        act_up = jax.nn.gelu(pre_up).astype(bf16)
        dense_own = scatter_rows(jnp.dot(act_up, w_down, preferred_element_type=f32))
        grad_act_up = jnp.einsum("gd,fd->gf", dense_grad_rows, w_down, preferred_element_type=f32)
        grad_pre_up = gelu_grad(pre_up, grad_act_up).astype(bf16)
        grad_w_down = jnp.einsum("gf,gd->fd", act_up, dense_grad_rows, preferred_element_type=f32)
        grad_w_up = jnp.einsum("gd,gf->df", hidden_all, grad_pre_up, preferred_element_type=f32)
        dense_back_own = scatter_rows(
            jnp.einsum("gf,df->gd", grad_pre_up, w_up, preferred_element_type=f32)
        )

    arrived, grad_w_up = barrier((arrived, grad_w_up))
    slots_in, grad_slots_in = join_cols(arrived, 2)
    if special:
        dense_shapes = [grad_w_up.shape, grad_w_down.shape]
        share = (6, 6, 4)
        mine, act_exp, dact_exp, state = expert_data(
            slots_in,
            grad_slots_in,
            w_exp_up[0],
            w_exp_down[0],
            Ride(0, 1, [grad_w_up, grad_w_down], dense_shapes, 1024, share, 2),
        )
        mine, act_exp = barrier((mine, act_exp))
        back = return_slots(mine)
        grad_w_exp_up, grad_w_exp_down = expert_weights(
            slots_in, grad_slots_in, act_exp, dact_exp
        )
        state, grad_w_exp_up = barrier((state, grad_w_exp_up))
        (state,) = ride_alone(Ride(1, MIDDLE, [state], dense_shapes, 1024, share), 2)
        back, state = barrier((back, state))
        grad_w_exp_up, grad_w_exp_down = grad_w_exp_up[None], grad_w_exp_down[None]
        expert_own, grad_expert_own = unslot(back)
    else:
        slots_in, grad_slots_in = (
            v.reshape(local_experts, owner_count * capacity, model_width)
            for v in (slots_in, grad_slots_in)
        )
        pre_exp = jnp.einsum("lsd,ldf->lsf", slots_in, w_exp_up, preferred_element_type=f32)
        act_exp = jax.nn.gelu(pre_exp).astype(bf16)
        out_exp = jnp.einsum("lsf,lfd->lsd", act_exp, w_exp_down, preferred_element_type=f32)
        (expert_own,) = unslot(return_slots(scatter_cols(out_exp.reshape(slots, model_width))))
        grad_act_exp = jnp.einsum(
            "lsd,lfd->lsf", grad_slots_in, w_exp_down, preferred_element_type=f32
        )
        grad_pre_exp = gelu_grad(pre_exp, grad_act_exp).astype(bf16)
        grad_slots_out = jnp.einsum(
            "lsf,ldf->lsd", grad_pre_exp, w_exp_up, preferred_element_type=f32
        )
        back = return_slots(scatter_cols(grad_slots_out.reshape(slots, model_width)))
        (grad_expert_own,) = unslot(back)
        grad_w_exp_down = jnp.einsum(
            "lsf,lsd->lfd", act_exp, grad_slots_in, preferred_element_type=f32
        )
        grad_w_exp_up = jnp.einsum(
            "lsd,lsf->ldf", slots_in, grad_pre_exp, preferred_element_type=f32
        )

    logits_own, hot_own = own_rows_of(logits), own_rows_of(hot_float)
    (mix_own, gate_own), gates_pull = jax.vjp(lambda z: gates(z, hot_own), logits_own)
    output = (
        middle + mix_own[:, 0:1] * dense_own + (mix_own[:, 1] * gate_own)[:, None] * expert_own
    ).astype(bf16)
    grad_out = cotangent.astype(f32)
    dense_dot = jnp.sum(grad_out * dense_own, axis=1)
    expert_dot = jnp.sum(grad_out * expert_own, axis=1)
    grad_mix_coef = jnp.stack([dense_dot, gate_own * expert_dot], axis=1)
    (grad_logits,) = gates_pull((grad_mix_coef, mix_own[:, 1] * expert_dot))
    grad_gate_w = lax.dot_general(
        grad_logits,
        normed_two.astype(f32),
        (((0,), (0,)), ((), ())),
        precision=highest,
        preferred_element_type=f32,
    )
    grad_hidden_gate = lax.dot_general(
        grad_logits,
        gate_w.astype(f32),
        (((1,), (1,)), ((), ())),
        precision=highest,
        preferred_element_type=f32,
    )
    grad_hidden_own = dense_back_own + grad_expert_own + grad_hidden_gate
    _, norm_two_pull = jax.vjp(layer_norm, middle, norm2_gain)
    grad_middle_norm, grad_gain2 = norm_two_pull(grad_hidden_own)
    grad_middle = grad_out + grad_middle_norm

    grad_attn_all = gather_rows(grad_middle.astype(bf16))
    if special:
        grad_w_out = jnp.einsum(
            "gk,gd->kd", attn_heads, grad_attn_all, preferred_element_type=f32
        ).astype(bf16)
        rides = [
            Ride(MIDDLE, 8, [state], dense_shapes, 1024, share, RIDE_GAP),
            Ride(0, 4, [grad_w_out], [grad_w_out.shape], 512, (2, 1, 1), 2),
        ]
        grad_w_qkv, grad_normed_one, grad_w_up, grad_w_down, state = attention_back(
            labels, projected, grad_attn_all, w_out, w_qkv, normed_all, rides
        )
    else:
        grad_w_out = jnp.einsum("gk,gd->kd", attn_heads, grad_attn_all, preferred_element_type=f32)
        grad_heads = jnp.einsum(
            "gd,kd->gk", grad_attn_all, w_out, preferred_element_type=f32
        ).astype(bf16)
        grad_qkv = attend_back(labels, projected, grad_heads)
        grad_w_qkv = jnp.einsum("gd,cgk->cdk", normed_all, grad_qkv, preferred_element_type=f32)
        grad_normed_one = scatter_rows(
            jnp.einsum("cgk,cdk->gd", grad_qkv, w_qkv, preferred_element_type=f32)
        )
    _, norm_one_pull = jax.vjp(layer_norm, token_f32, norm1_gain)
    grad_token_norm, grad_gain1 = norm_one_pull(grad_normed_one)
    grad_tokens = grad_middle + grad_token_norm

    small = jnp.concatenate([grad_gain1[None], grad_gain2[None], grad_gate_w], axis=0)
    if special:
        padding = -small.shape[0] % 8
        rides = [
            Ride(0, 8, [grad_w_qkv], [grad_w_qkv.shape], 512, (4, 4, 4)),
            Ride(4, 8, [state], [grad_w_out.shape], 512, (2, 1, 1)),
        ]
        small = jnp.pad(small, ((0, padding), (0, 0)))
        small, grad_w_qkv, grad_w_out = last_sums(rides, small)
    else:
        grad_w_up, grad_w_down, grad_w_qkv, grad_w_out = lax.psum(
            [g.astype(bf16) for g in (grad_w_up, grad_w_down, grad_w_qkv, grad_w_out)], "expert"
        )
        small = lax.psum(small, ("expert", "tensor"))
    grad_w_qkv, grad_w_out, grad_w_up, grad_w_down = (
        g.astype(f32) for g in (grad_w_qkv, grad_w_out, grad_w_up, grad_w_down)
    )
    return (
        output,
        grad_tokens,
        small[0],
        grad_w_qkv,
        grad_w_out,
        small[1],
        grad_w_up,
        grad_w_down,
        small[2 : 2 + experts_all].T,
        small[2 + experts_all : 4 + experts_all].T,
        grad_w_exp_up,
        grad_w_exp_down,
    )


def solution(mesh):
    return jax.shard_map(
        body,
        mesh=mesh,
        in_specs=(
            P(("expert", "tensor"), None),
            P(),
            P(None, None, "tensor"),
            P("tensor", None),
            P(),
            P(None, "tensor"),
            P("tensor", None),
            P(),
            P(),
            P("expert", None, "tensor"),
            P("expert", "tensor", None),
            P("expert", None),
            P("expert", None),
            P(("expert", "tensor"), None),
        ),
        out_specs=(
            P(("expert", "tensor"), None),
            P(("expert", "tensor"), None),
            P(),
            P(None, None, "tensor"),
            P("tensor", None),
            P(),
            P(None, "tensor"),
            P("tensor", None),
            P(),
            P(),
            P("expert", None, "tensor"),
            P("expert", "tensor", None),
        ),
        check_vma=False,
    )
```

```python
import functools

import jax
import jax.numpy as jnp
from jax import lax
from jax.experimental import pallas as pl
from jax.experimental.pallas import tpu as pltpu
from jax.sharding import PartitionSpec as P

HEAD = 64
PROMPT = 512
BLOCK = 256
LANES = 128
PIECE = 256
MASKED = -1e30

epsilon = 1e-05
highest = lax.Precision.HIGHEST
f32 = jnp.float32
bf16 = jnp.bfloat16


def layer_norm(values, norm_gain):
    centred = values - jnp.mean(values, axis=-1, keepdims=True)
    variance = jnp.mean(centred * centred, axis=-1, keepdims=True)
    return centred * lax.rsqrt(variance + epsilon) * norm_gain


def gelu_grad(pre_act, upstream):
    return jax.vjp(jax.nn.gelu, pre_act)[1](upstream)[0]


def nt_dot(left, right):
    return lax.dot_general(left, right, (((1,), (1,)), ((), ())), preferred_element_type=f32)


def nn_dot(left, right):
    return lax.dot_general(left, right, (((1,), (0,)), ((), ())), preferred_element_type=f32)


def tn_dot(left, right):
    return lax.dot_general(left, right, (((0,), (0,)), ((), ())), preferred_element_type=f32)


def fill_bias(row_labels_ref, col_labels_ref, cont_bias, tri_bias, transposed):
    size = cont_bias.shape[0]
    down = lax.broadcasted_iota(jnp.int32, (size, size), 0)
    across = lax.broadcasted_iota(jnp.int32, (size, size), 1)
    ordered = (down <= across) if transposed else (across <= down)
    same = row_labels_ref[...] == col_labels_ref[...]
    cont_bias[...] = jnp.where(ordered & same, 0.0, MASKED)
    down = lax.broadcasted_iota(jnp.int32, (BLOCK, BLOCK), 0)
    across = lax.broadcasted_iota(jnp.int32, (BLOCK, BLOCK), 1)
    ordered = (down <= across) if transposed else (across <= down)
    tri_bias[...] = jnp.where(ordered, 0.0, MASKED)


def head_lanes(half):
    lane = lax.broadcasted_iota(jnp.int32, (1, LANES), 1)
    return (lane < HEAD) if half == 0 else (lane >= HEAD)


def turned(pair):
    return lax.axis_index("tensor") if pair else 0


def attend_kernel(pair, col_ref, row_ref, qp, qc, kp, kc, vp, vc, o_ref, cont_bias, tri_bias):
    @pl.when(pl.program_id(0) == 0)
    def _():
        fill_bias(col_ref, row_ref, cont_bias, tri_bias, False)

    turn = turned(pair)
    scale = HEAD**-0.5
    for part in range(2):
        for inner in range(0, PROMPT, BLOCK):
            upto = inner + BLOCK
            mixed = []
            for half in range(2):
                source = (qc if part else qp)[inner:upto, :]
                query = jnp.where(head_lanes(half), source * scale, 0.0).astype(bf16)
                pieces = []
                if part:
                    pieces.append((kp[...], vp[...], None))
                    pieces.append((kc[:upto, :], vc[:upto, :], cont_bias[inner:upto, :upto]))
                else:
                    if inner:
                        pieces.append((kp[:inner, :], vp[:inner, :], None))
                    pieces.append((kp[inner:upto, :], vp[inner:upto, :], tri_bias[...]))
                scores = []
                for key, _, bias in pieces:
                    score = nt_dot(query, key)
                    scores.append(score if bias is None else score + bias)
                top = functools.reduce(
                    jnp.maximum, [jnp.max(score, axis=1, keepdims=True) for score in scores]
                )
                total, out = 0.0, 0.0
                for score, (_, value, _) in zip(scores, pieces, strict=True):
                    weights = jnp.exp(score - top)
                    total = total + jnp.sum(weights, axis=1, keepdims=True)
                    out = out + nn_dot(weights.astype(bf16), value)
                mixed.append(out / total)
            which = (1 - turn) if part else turn
            o_ref[which, inner:upto, :] = jnp.where(head_lanes(0), mixed[0], mixed[1]).astype(bf16)


def attend_back_part(
    part, pair, qp, qc, kp, kc, vp, vc, gp, gc, d_ref, cont_bias, tri_bias, *accs
):
    turn = turned(pair)
    scale = HEAD**-0.5
    dkp, dkc, dvp, dvc = accs
    for inner in range(0, PROMPT, BLOCK):
        upto = inner + BLOCK
        dq = 0.0
        for half in range(2):
            lanes = head_lanes(half)
            query = jnp.where(lanes, (qc if part else qp)[inner:upto, :] * scale, 0.0)
            query = query.astype(bf16)
            grad = jnp.where(lanes, (gc if part else gp)[inner:upto, :], 0.0).astype(bf16)
            if part:
                pieces = [(kp, vp, dkp, dvp, 0, PROMPT, None)]
                pieces.append((kc, vc, dkc, dvc, 0, upto, cont_bias[:upto, inner:upto]))
            else:
                pieces = [(kp, vp, dkp, dvp, 0, inner, None)] if inner else []
                pieces.append((kp, vp, dkp, dvp, inner, upto, tri_bias[...]))
            scores = []
            for key, _, _, _, at, end, bias in pieces:
                score = nt_dot(key[at:end, :], query)
                scores.append(score if bias is None else score + bias)
            top = functools.reduce(
                jnp.maximum, [jnp.max(score, axis=0, keepdims=True) for score in scores]
            )
            scores = [jnp.exp(score - top) for score in scores]
            total = sum(jnp.sum(score, axis=0, keepdims=True) for score in scores)
            scores = [score * (1.0 / total) for score in scores]
            grads = [
                nt_dot(value[at:end, :], grad) for _, value, _, _, at, end, _ in pieces
            ]
            row_dot = sum(
                jnp.sum(score * up, axis=0, keepdims=True)
                for score, up in zip(scores, grads, strict=True)
            )
            for score, up, (key, _, dk, dv, at, end, _) in zip(
                scores, grads, pieces, strict=True
            ):
                grad_scores = (score * (up - row_dot)).astype(bf16)
                dv[at:end, :] += nn_dot(score.astype(bf16), grad)
                dk[at:end, :] += nn_dot(grad_scores, query)
                masked = jnp.where(lanes, key[at:end, :] * scale, 0.0).astype(bf16)
                dq = dq + tn_dot(grad_scores, masked)
        which = (1 - turn) if part else turn
        d_ref[0, which, inner:upto, :] = dq.astype(bf16)


def attend_back_phases(pair, step, col_ref, row_ref, *refs):
    qp, qc, kp, kc, vp, vc, gp, gc, d_ref, cont_bias, tri_bias, *accs = refs

    def prompt():
        @pl.when(step == 0)
        def _():
            fill_bias(col_ref, row_ref, cont_bias, tri_bias, True)

        for acc in accs:
            acc[...] = jnp.zeros_like(acc)
        attend_back_part(0, pair, *refs)

    def continuations():
        attend_back_part(1, pair, *refs)
        turn = turned(pair)
        for number, acc in enumerate(accs):
            which = (1 - turn) if number % 2 else turn
            d_ref[1 + number // 2, which] = acc[...].astype(bf16)

    return [prompt, continuations]


def attend_back_kernel(pair, *refs):
    for phase in attend_back_phases(pair, pl.program_id(0), *refs):
        phase()


def half_specs(size, lead, pair, steps=None):
    blank = (pl.Squeezed(),) * (1 if lead is None else 2)

    def spec(cont):
        def index(i):
            i = i if steps is None else jnp.minimum(i, steps - 1)
            half = 1 - turned(pair) if cont else turned(pair)
            return (half, 0, i) if lead is None else (lead, half, 0, i)

        return pl.BlockSpec((*blank, size, LANES), index)

    return [spec(False), spec(True)]


def attend_call(kernel, name, labels, projected, grad_heads, dots, accs):
    rows, cols = projected.shape[1:]
    cont = rows - PROMPT
    pair = paired()
    kernel = functools.partial(kernel, pair)
    halves = projected.reshape(3, 2, PROMPT, cols)
    work = 2 * rows * rows * cols * dots
    back = grad_heads is not None
    lead = (3,) if back else ()
    specs = [s for c in range(3) for s in half_specs(PROMPT, c, pair)]
    args = [halves] * 6
    if back:
        specs += half_specs(PROMPT, None, pair)
        args += [grad_heads.reshape(2, PROMPT, cols)] * 2
    specs = [
        pl.BlockSpec((cont, 1), lambda i: (0, 0)),
        pl.BlockSpec((1, cont), lambda i: (0, 0)),
        *specs,
    ]
    out_spec = pl.BlockSpec(
        (*lead, 2, PROMPT, LANES), lambda i: (*(0 for _ in lead), 0, 0, i)
    )
    out_shape = jax.ShapeDtypeStruct((*lead, 2, PROMPT, cols), bf16)
    scratch = [
        pltpu.VMEM((cont, cont), f32),
        pltpu.VMEM((BLOCK, BLOCK), f32),
        *[pltpu.VMEM((PROMPT, LANES), f32)] * accs,
    ]
    args = [labels[:, None], labels[None, :], *args]
    steps = cols // LANES
    out = pl.pallas_call(
        kernel,
        grid=(steps,),
        in_specs=specs,
        out_specs=out_spec,
        scratch_shapes=scratch,
        out_shape=out_shape,
        cost_estimate=pl.CostEstimate(
            flops=work, bytes_accessed=14 * rows * cols, transcendentals=rows * rows * 4
        ),
        name=name,
    )(*args)
    return out.reshape(*lead, rows, cols)


def attend(labels, projected):
    return attend_call(attend_kernel, "attend", labels, projected, None, 2, 0)


def attend_back(labels, projected, grad_heads):
    return attend_call(
        attend_back_kernel, "attend_back", labels, projected, grad_heads, 5, 4
    )


HIDDEN = 512
ROWS = 512
CUT = 256
MIDDLE = 4
RIDE_GAP = 2


def gelu_both(pre_act):
    slope = 0.7978845608028654
    square = pre_act * pre_act
    bend = jnp.tanh(slope * (pre_act + 0.044715 * (square * pre_act)))
    share = 0.5 * (1.0 + bend)
    steep = 0.5 * slope * (1.0 + (3 * 0.044715) * square)
    return pre_act * share, share + pre_act * (1.0 - bend * bend) * steep


def feed_rows(first, at, x_ref, dy_ref, wu_ref, wd_ref, act, dact, y_acc, dx_acc):
    pre_act = nn_dot(x_ref[at, :], wu_ref[...])
    up = nt_dot(dy_ref[at, :], wd_ref[...])
    value, slope = gelu_both(pre_act)
    value = value.astype(bf16)
    back = (up * slope).astype(bf16)
    act[at, :] = value
    dact[at, :] = back
    out = nn_dot(value, wd_ref[...])
    grad = nt_dot(back, wu_ref[...])

    @pl.when(first)
    def _():
        y_acc[at, :] = out
        dx_acc[at, :] = grad

    @pl.when(jnp.logical_not(first))
    def _():
        y_acc[at, :] += out
        dx_acc[at, :] += grad


def feed_down(x_ref, dy_ref, act, dact, gu_ref, gd_ref):
    for at in range(0, gd_ref.shape[0], CUT):
        gd_ref[at : at + CUT, :] = tn_dot(act[:, at : at + CUT], dy_ref[...]).astype(gd_ref.dtype)


def feed_up(x_ref, dy_ref, act, dact, gu_ref, gd_ref):
    for at in range(0, gu_ref.shape[0], CUT):
        gu_ref[at : at + CUT, :] = tn_dot(x_ref[:, at : at + CUT], dact[...]).astype(gu_ref.dtype)


def feed_kernel(x_ref, dy_ref, wu_ref, wd_ref, *refs):
    yk, ya, dxk, dxa, gu_ref, gd_ref, act, dact, y_acc, dx_acc = refs
    step = pl.program_id(0)
    for at in range(0, x_ref.shape[0], ROWS):
        rows = slice(at, at + ROWS)
        feed_rows(step == 0, rows, x_ref, dy_ref, wu_ref, wd_ref, act, dact, y_acc, dx_acc)
    feed_down(x_ref, dy_ref, act, dact, gu_ref, gd_ref)
    feed_up(x_ref, dy_ref, act, dact, gu_ref, gd_ref)

    @pl.when(step == pl.num_programs(0) - 1)
    def _():
        half = yk.shape[0]
        yk[...] = y_acc[:half, :]
        dxk[...] = dx_acc[:half, :]
        ya[...] = y_acc[half:, :].astype(bf16)
        dxa[...] = dx_acc[half:, :].astype(bf16)


def one_buffer(shape):
    return pl.BlockSpec(shape, lambda *_: (0,) * len(shape), pipeline_mode=pl.Buffered(1))


def feed_forward(x, dy, w_up, w_down):
    rows, width = x.shape
    hidden = w_up.shape[1]
    tile = min(HIDDEN, hidden)
    half = rows // 2
    block = jax.ShapeDtypeStruct((half, width), f32)
    sent = jax.ShapeDtypeStruct((half, width), bf16)
    return pl.pallas_call(
        feed_kernel,
        grid=(hidden // tile,),
        in_specs=[
            one_buffer((rows, width)),
            one_buffer((rows, width)),
            pl.BlockSpec((width, tile), lambda i: (0, i)),
            pl.BlockSpec((tile, width), lambda i: (i, 0)),
        ],
        out_specs=[
            *[one_buffer((half, width))] * 4,
            pl.BlockSpec((width, tile), lambda i: (0, i)),
            pl.BlockSpec((tile, width), lambda i: (i, 0)),
        ],
        out_shape=[
            block,
            sent,
            block,
            sent,
            jax.ShapeDtypeStruct((width, hidden), bf16),
            jax.ShapeDtypeStruct((hidden, width), bf16),
        ],
        scratch_shapes=[
            pltpu.VMEM((rows, tile), bf16),
            pltpu.VMEM((rows, tile), bf16),
            pltpu.VMEM((rows, width), f32),
            pltpu.VMEM((rows, width), f32),
        ],
        compiler_params=pltpu.CompilerParams(vmem_limit_bytes=56 * 1024 * 1024),
        cost_estimate=pl.CostEstimate(
            flops=12 * rows * width * hidden,
            bytes_accessed=8 * width * hidden + 12 * rows * width,
            transcendentals=rows * hidden,
        ),
        name="feed_forward",
    )(x, dy, w_up, w_down)


ORDERS = ((1, 2, 4, 8), (2, 4, 1, 8), (4, 1, 2, 8))
DEPTH = 4
MESH = pl.DeviceIdType.MESH


def partner_of(bit):
    me = lax.axis_index("expert")
    side = lax.rem(me // bit, 2)
    return me + bit * (1 - 2 * side), side


def greet(core):
    barrier = pltpu.get_barrier_semaphore()
    for bit in sorted(ORDERS[0]):
        pl.semaphore_signal(
            barrier, 1, device_id={"expert": partner_of(bit)[0]}, device_id_type=MESH
        )
    if core:
        other = 1 - lax.axis_index("tensor")
        pl.semaphore_signal(barrier, 1, device_id={"tensor": other}, device_id_type=MESH)
    pl.semaphore_wait(barrier, DEPTH + core)


class Ride:
    def __init__(self, level_in, level_out, values, shapes, width, counts, gap=1):
        self.first, self.last = level_in, level_out
        self.values, self.shapes, self.width, self.counts = list(values), shapes, width, counts
        layout = split_layout(shapes, width)
        self.pieces = sum(map(len, layout))
        self.where = [(a, piece) for a, pieces in enumerate(layout) for piece in pieces]
        stages = range(level_out - level_in + 1)
        self.delays = [gap * stage for stage in stages] if isinstance(gap, int) else gap
        self.ticks = max(counts) + self.delays[-1]

    def rows_at(self, level):
        return PIECE >> (level if level <= DEPTH else 2 * DEPTH - level)

    def out_shape(self):
        shapes = self.shapes
        if self.last < 2 * DEPTH:
            shapes = [(self.pieces, self.rows_at(self.last), self.width)]
        return [jax.ShapeDtypeStruct(shape, bf16) for shape in shapes]

    def scratch(self):
        shapes = []
        if self.first < DEPTH:
            shapes.append(self.rows_at(self.first))
            shapes += [self.rows_at(n + 1) for n in range(self.first, min(self.last, DEPTH))]
        if self.last > DEPTH:
            shapes.append(self.rows_at(self.last))
        hops = self.last - self.first
        return [
            *[pltpu.VMEM((self.pieces, rows, self.width), bf16) for rows in shapes],
            pltpu.SemaphoreType.DMA((hops, self.pieces)),
            pltpu.SemaphoreType.DMA((hops, self.pieces)),
            pltpu.SemaphoreType.DMA((self.pieces,)),
            pltpu.SemaphoreType.DMA((self.pieces,)),
        ]

    def bind(self, ins, outs, scratch):
        self.ins, self.outs = ins, outs
        *buffers, self.send_sem, self.recv_sem, self.load_sem, self.store_sem = scratch
        self.held = buffers[0] if self.first < DEPTH else None
        self.got = buffers[1 : 1 + max(0, min(self.last, DEPTH) - self.first)]
        self.full = buffers[-1] if self.last > DEPTH else None
        self.sides = {bit: partner_of(bit) for bit in ORDERS[0]}

    def held_at(self, order, level):
        total = 0
        for n in range(self.first, level):
            total = total + self.sides[order[n]][1] * self.rows_at(n + 1)
        return pl.multiple_of(total, 16)

    def full_at(self, order, level):
        total = 0
        for n in range(2 * DEPTH - self.last, 2 * DEPTH - level):
            total = total + self.sides[order[n]][1] * self.rows_at(n + 1)
        return pl.multiple_of(total, 16)

    def color_of(self, piece):
        color = 0
        while piece >= sum(self.counts[: color + 1]):
            color += 1
        return color

    def load(self, piece):
        sem = self.load_sem.at[piece]
        if self.first == 0:
            a, parts = self.where[piece]
            return [
                pltpu.make_async_copy(self.ins[a].at[src], self.held.at[(piece, *dst)], sem)
                for src, dst in parts
            ]
        if self.first < DEPTH:
            return [pltpu.make_async_copy(self.ins[0].at[piece], self.held.at[piece], sem)]
        order = ORDERS[self.color_of(piece)]
        at = pl.ds(self.full_at(order, self.first), self.rows_at(self.first))
        return [pltpu.make_async_copy(self.ins[0].at[piece], self.full.at[piece, at], sem)]

    def await_load(self, order, piece):
        sem = self.load_sem.at[piece]
        if self.first < DEPTH:
            whole = self.held.at[piece]
        else:
            at = pl.ds(self.full_at(order, self.first), self.rows_at(self.first))
            whole = self.full.at[piece, at]
        pltpu.make_async_copy(whole, whole, sem).wait()

    def stores(self, piece):
        sem = self.store_sem.at[piece]
        if self.last == 2 * DEPTH:
            a, parts = self.where[piece]
            return [
                pltpu.make_async_copy(self.full.at[(piece, *dst)], self.outs[a].at[src], sem)
                for src, dst in parts
            ]
        if self.last > DEPTH:
            return [pltpu.make_async_copy(self.full.at[piece], self.outs[0].at[piece], sem)]
        order = ORDERS[self.color_of(piece)]
        at = pl.ds(self.held_at(order, self.last), self.rows_at(self.last))
        return [pltpu.make_async_copy(self.held.at[piece, at], self.outs[0].at[piece], sem)]

    def start_store(self, order, piece):
        if self.last == 2 * DEPTH:
            for number in range(self.pieces):

                @pl.when(piece == number)
                def _(number=number):
                    for copy in self.stores(number):
                        copy.start()

            return
        sem = self.store_sem.at[piece]
        if self.last > DEPTH:
            source = self.full.at[piece]
        else:
            at = pl.ds(self.held_at(order, self.last), self.rows_at(self.last))
            source = self.held.at[piece, at]
        pltpu.make_async_copy(source, self.outs[0].at[piece], sem).start()

    def exchange(self, order, hop, piece):
        sems = (self.send_sem.at[hop - self.first, piece], self.recv_sem.at[hop - self.first, piece])
        if hop < DEPTH:
            target, side = self.sides[order[hop]]
            size = self.rows_at(hop + 1)
            away = pl.multiple_of(self.held_at(order, hop) + (1 - side) * size, 16)
            source = self.held.at[piece, pl.ds(away, size)]
            dest = self.got[hop - self.first].at[piece]
        else:
            target, _ = self.sides[order[2 * DEPTH - 1 - hop]]
            at = pl.ds(self.full_at(order, hop), self.rows_at(hop))
            source = dest = self.full.at[piece, at]
        return pltpu.make_async_remote_copy(
            source, dest, *sems, device_id={"expert": target}, device_id_type=MESH
        )

    def run(self, color, stage, piece):
        order = ORDERS[color]
        if stage == 0:
            self.await_load(order, piece)
        else:
            hop = self.first + stage - 1
            self.exchange(order, hop, piece).wait()
            if hop < DEPTH:
                size = self.rows_at(hop + 1)
                at = pl.ds(self.held_at(order, hop + 1), size)
                total = self.held[piece, at, :].astype(f32)
                total = (total + self.got[hop - self.first][piece].astype(f32)).astype(bf16)
                if hop + 1 == DEPTH and self.last > DEPTH:
                    self.full[piece, pl.ds(self.full_at(order, DEPTH), size), :] = total
                else:
                    self.held[piece, at, :] = total
        if self.first + stage < self.last:
            self.exchange(order, self.first + stage, piece).start()
        else:
            self.start_store(order, piece)

    def begin(self):
        for piece in range(self.pieces):
            for copy in self.load(piece):
                copy.start()

    def tick(self, t):
        for stage in range(self.last - self.first + 1):
            for color, count in enumerate(self.counts):

                at = t - self.delays[stage]

                @pl.when((at >= 0) & (at < count))
                def _(color=color, stage=stage, at=at):
                    self.run(color, stage, sum(self.counts[:color]) + at)

    def end(self):
        for piece in range(self.pieces):
            for copy in self.stores(piece):
                copy.wait()


any_spec = pl.BlockSpec(memory_space=pl.ANY)


def carry(
    phases, steps, specs, out_specs, out_shape, scratch, args, rides, name, flops, collective, core=False
):
    n_ticks = max(ride.ticks for ride in rides)
    ride_outs = [ride.out_shape() for ride in rides]
    parts = 2
    grid = max(steps, -(-n_ticks // parts))

    def clamp(spec):
        if spec.index_map is None:
            return spec
        return pl.BlockSpec(
            spec.block_shape,
            lambda i: spec.index_map(jnp.minimum(i, steps - 1)),
            pipeline_mode=spec.pipeline_mode,
        )

    n_in, n_out = len(args), len(out_shape)

    def kernel(*refs):
        refs = list(refs)
        take = lambda count: [refs.pop(0) for _ in range(count)]
        main_in = take(n_in)
        ins = [take(len(ride.values)) for ride in rides]
        main_out = take(n_out)
        outs = [take(len(shapes)) for shapes in ride_outs]
        main_scratch = take(len(scratch))
        for ride, got, out in zip(rides, ins, outs, strict=True):
            ride.bind(got, out, take(len(ride.scratch())))
        step = pl.program_id(0)

        @pl.when(step == 0)
        def _():
            for ride in rides:
                ride.begin()
            greet(core)

        for number, phase in enumerate(phases(step, *main_in, *main_out, *main_scratch)):
            for ride in rides:
                ride.tick(step * parts + number)
            pl.when(step < steps)(phase)

        @pl.when(step == grid - 1)
        def _():
            for ride in rides:
                ride.end()

    moved = sum(v.size for ride in rides for v in ride.values)
    return pl.pallas_call(
        kernel,
        grid_spec=pltpu.PrefetchScalarGridSpec(
            num_scalar_prefetch=0,
            grid=(grid,),
            in_specs=[*map(clamp, specs), *[any_spec] * sum(len(ride.values) for ride in rides)],
            out_specs=[*map(clamp, out_specs), *[any_spec] * sum(map(len, ride_outs))],
            scratch_shapes=[*scratch, *[m for ride in rides for m in ride.scratch()]],
        ),
        out_shape=[*out_shape, *[shape for shapes in ride_outs for shape in shapes]],
        compiler_params=pltpu.CompilerParams(
            collective_id=collective, has_side_effects=True, vmem_limit_bytes=62 * 1024 * 1024
        ),
        cost_estimate=pl.CostEstimate(flops=flops, bytes_accessed=4 * moved, transcendentals=0),
        name=name,
    )(*args, *[v for ride in rides for v in ride.values])


def split_layout(shapes, width):
    layout = []
    for shape in shapes:
        pieces = []
        leads = [(c,) for c in range(shape[0])] if len(shape) == 3 else [()]
        for lead in leads:
            for c in range(0, shape[-1], width):
                for r in range(0, shape[-2], PIECE):
                    pieces.append([((*lead, slice(r, r + PIECE), slice(c, c + width)), ())])
        layout.append(pieces)
    return layout


def last_kernel(rides, small_in, *refs):
    refs = list(refs)
    take = lambda count: [refs.pop(0) for _ in range(count)]
    ins = [take(len(ride.values)) for ride in rides]
    (small_out,) = take(1)
    outs = [take(len(ride.out_shape())) for ride in rides]
    small, small_got, small_sem = take(3)
    for ride, got, out in zip(rides, ins, outs, strict=True):
        ride.bind(got, out, take(len(ride.scratch())))
    bits = sorted(ORDERS[0])

    def small_copy(step):
        if step < DEPTH:
            target = {"expert": partner_of(bits[step])[0]}
        else:
            target = {"tensor": 1 - lax.axis_index("tensor")}
        return pltpu.make_async_remote_copy(
            small.at[step],
            small_got.at[step],
            small_sem.at[0, step],
            small_sem.at[1, step],
            device_id=target,
            device_id_type=MESH,
        )

    for ride in rides:
        ride.begin()
    first = pltpu.make_async_copy(small_in, small.at[0], small_sem.at[2, 0])
    first.start()
    greet(True)

    def step(t, _):
        for ride in rides:
            ride.tick(t)
        for number in range(DEPTH + 2):

            @pl.when(t == number)
            def _(number=number):
                if number == 0:
                    first.wait()
                else:
                    small_copy(number - 1).wait()
                    small[number] = small[number - 1] + small_got[number - 1]
                if number < DEPTH + 1:
                    small_copy(number).start()

        return 0

    lax.fori_loop(0, max(ride.ticks for ride in rides), step, 0)
    out = pltpu.make_async_copy(small.at[DEPTH + 1], small_out, small_sem.at[2, 1])
    out.start()
    for ride in rides:
        ride.end()
    out.wait()


def alone_kernel(ride, *refs):
    count = len(ride.values)
    ride.bind(refs[:count], refs[count : count + 1], refs[count + 1 :])
    ride.begin()
    greet(False)

    def step(t, _):
        ride.tick(t)
        return 0

    lax.fori_loop(0, ride.ticks, step, 0)
    ride.end()


def ride_alone(ride, collective):
    return pl.pallas_call(
        functools.partial(alone_kernel, ride),
        in_specs=[any_spec] * len(ride.values),
        out_specs=[any_spec],
        out_shape=ride.out_shape(),
        scratch_shapes=ride.scratch(),
        compiler_params=pltpu.CompilerParams(
            collective_id=collective, has_side_effects=True, vmem_limit_bytes=62 * 1024 * 1024
        ),
        name="ride_alone",
    )(*ride.values)


def last_sums(rides, small):
    ride_outs = [ride.out_shape() for ride in rides]
    values = [v for ride in rides for v in ride.values]
    shapes = [shape for shapes in ride_outs for shape in shapes]
    return pl.pallas_call(
        functools.partial(last_kernel, rides),
        in_specs=[any_spec] * (1 + len(values)),
        out_specs=[any_spec] * (1 + len(shapes)),
        out_shape=[jax.ShapeDtypeStruct(small.shape, f32), *shapes],
        scratch_shapes=[
            pltpu.VMEM((DEPTH + 2, *small.shape), f32),
            pltpu.VMEM((DEPTH + 1, *small.shape), f32),
            pltpu.SemaphoreType.DMA((3, DEPTH + 1)),
            *[m for ride in rides for m in ride.scratch()],
        ],
        compiler_params=pltpu.CompilerParams(
            collective_id=4, has_side_effects=True, vmem_limit_bytes=62 * 1024 * 1024
        ),
        name="last_sums",
    )(small, *values)


def expert_data_phases(steps, step, x_ref, dy_ref, wu_ref, wd_ref, *refs):
    mine, act, dact, y_acc, dx_acc, sent, came, sems = refs
    rows = x_ref.shape[0] // 2
    half = x_ref.shape[1] // 2
    rank = lax.axis_index("tensor")

    def block(number):
        return slice(number * rows, (number + 1) * rows)

    def swap_copy(number):
        return pltpu.make_async_remote_copy(
            sent.at[block(number)],
            came.at[block(number)],
            sems.at[0, number],
            sems.at[1, number],
            device_id={"tensor": 1 - rank},
            device_id_type=MESH,
        )

    def cols(side):
        return slice(side * half, (side + 1) * half)

    def part(number):
        at = block(number)
        feed_rows(step == 0, at, x_ref, dy_ref, wu_ref, wd_ref, act, dact, y_acc, dx_acc)
        for side in range(2):

            @pl.when((step == steps - 1) & (rank == side))
            def _(side=side):
                sent[at, :half] = y_acc[at, cols(1 - side)].astype(bf16)
                sent[at, half:] = dx_acc[at, cols(1 - side)].astype(bf16)

        @pl.when(step == steps - 1)
        def _():
            swap_copy(number).start()

    def finish():
        part(1)

        @pl.when(step == steps - 1)
        def _():
            for number in range(2):
                swap_copy(number).wait()
                at = block(number)
                for side in range(2):

                    @pl.when(rank == side)
                    def _(side=side, at=at):
                        for cut, acc in ((slice(0, half), y_acc), (slice(half, 2 * half), dx_acc)):
                            total = acc[at, cols(side)] + came[at, cut].astype(f32)
                            mine[at, cut] = total.astype(bf16)

    return [functools.partial(part, 0), finish]


def expert_data(x, dy, w_up, w_down, ride):
    rows, width = x.shape
    hidden = w_up.shape[1]
    tile = min(HIDDEN, hidden)
    steps = hidden // tile
    inner = jax.ShapeDtypeStruct((rows, hidden), bf16)
    return carry(
        functools.partial(expert_data_phases, steps),
        steps,
        [
            one_buffer((rows, width)),
            one_buffer((rows, width)),
            pl.BlockSpec((width, tile), lambda i: (0, i)),
            pl.BlockSpec((tile, width), lambda i: (i, 0)),
        ],
        [
            one_buffer((rows, width)),
            *[pl.BlockSpec((rows, tile), lambda i: (0, i))] * 2,
        ],
        [jax.ShapeDtypeStruct((rows, width), bf16), inner, inner],
        [
            pltpu.VMEM((rows, width), f32),
            pltpu.VMEM((rows, width), f32),
            pltpu.VMEM((rows, width), bf16),
            pltpu.VMEM((rows, width), bf16),
            pltpu.SemaphoreType.DMA((2, 2)),
        ],
        [x, dy, w_up, w_down],
        [ride],
        "expert_data",
        8 * rows * width * hidden,
        1,
        True,
    )


def expert_weights_kernel(*refs):
    feed_down(*refs)
    feed_up(*refs)


def expert_weights(x, dy, act, dact):
    rows, width = x.shape
    hidden = act.shape[1]
    tile = min(HIDDEN, hidden)
    return pl.pallas_call(
        expert_weights_kernel,
        grid=(hidden // tile,),
        in_specs=[
            one_buffer((rows, width)),
            one_buffer((rows, width)),
            *[pl.BlockSpec((rows, tile), lambda i: (0, i))] * 2,
        ],
        out_specs=[
            pl.BlockSpec((width, tile), lambda i: (0, i)),
            pl.BlockSpec((tile, width), lambda i: (i, 0)),
        ],
        out_shape=[
            jax.ShapeDtypeStruct((width, hidden), f32),
            jax.ShapeDtypeStruct((hidden, width), f32),
        ],
        compiler_params=pltpu.CompilerParams(vmem_limit_bytes=56 * 1024 * 1024),
        cost_estimate=pl.CostEstimate(
            flops=4 * rows * width * hidden,
            bytes_accessed=8 * width * hidden + 4 * rows * width + 4 * rows * hidden,
            transcendentals=0,
        ),
        name="expert_weights",
    )(x, dy, act, dact)


def attention_back_phases(pairs, step, col_ref, row_ref, da_ref, wo_ref, *refs):
    halves, refs = refs[:6], refs[6:]
    wq_any, normed_any, gq_ref, dh_ref, *refs = refs
    cont_bias, tri_bias, do_s, d_s, dh_acc, wq, normed, sems, sent, came, *accs = refs
    rows = da_ref.shape[0]
    half = rows // 2
    copies = [
        pltpu.make_async_copy(source, dest, sems.at[number])
        for number, (source, dest) in enumerate(
            ((wq_any, wq), (normed_any, normed))
        )
    ]
    swap_copy = pltpu.make_async_remote_copy(
        sent,
        came,
        sems.at[2],
        sems.at[3],
        device_id={"tensor": 1 - lax.axis_index("tensor")},
        device_id_type=MESH,
    )
    turn = turned(True)
    lanes = pl.ds(pl.multiple_of(jnp.minimum(step, pairs - 1) * LANES, LANES), LANES)

    def attend_part(part):
        grads = [do_s.at[which, :, lanes] for which in (turn, 1 - turn)]
        out = d_s.at[:, :, :, lanes]
        attend_back_part(part, True, *halves, *grads, out, cont_bias, tri_bias, *accs)

    which = jnp.clip(step - pairs, 0, 2)

    def first():
        @pl.when(step == 0)
        def _():
            for copy in copies:
                copy.start()
            for number in range(2):
                at = slice(number * half, (number + 1) * half)
                do_s[number] = nt_dot(da_ref[at, :], wo_ref[...]).astype(bf16)
            fill_bias(col_ref, row_ref, cont_bias, tri_bias, True)

        @pl.when(step < pairs)
        def _():
            for acc in accs:
                acc[...] = jnp.zeros_like(acc)
            attend_part(0)

        @pl.when(step == pairs)
        def _():
            for copy in copies:
                copy.wait()
            dh_acc[...] = jnp.zeros_like(dh_acc)

        @pl.when((step >= pairs) & (step < pairs + 3))
        def _():
            for number in range(2):
                dh_acc[number] += nt_dot(d_s[which, number], wq[which])

    def second():
        @pl.when(step < pairs)
        def _():
            attend_part(1)
            for number, acc in enumerate(accs):
                place = (1 - turn) if number % 2 else turn
                d_s[1 + number // 2, place, :, lanes] = acc[...].astype(bf16)

        @pl.when(step == pairs + 2)
        def _():
            sent[...] = dh_acc[1].astype(bf16)
            swap_copy.start()

        @pl.when((step >= pairs) & (step < pairs + 3))
        def _():
            grads = d_s[which].reshape(rows, d_s.shape[-1])
            for at in range(0, normed.shape[1], CUT):
                gq_ref[which, at : at + CUT, :] = tn_dot(normed[:, at : at + CUT], grads).astype(
                    bf16
                )

        @pl.when(step == pairs + 2)
        def _():
            swap_copy.wait()
            dh_ref[...] = dh_acc[0] + came[...].astype(f32)

    return [first, second]


def attention_back(labels, projected, grad_attn, w_out, w_qkv, normed, rides):
    rows, cols = projected.shape[1:]
    width = normed.shape[1]
    cont = rows - PROMPT
    pairs = cols // LANES
    inputs = projected.reshape(3, 2, PROMPT, cols)
    return carry(
        functools.partial(attention_back_phases, pairs),
        pairs + 3,
        [
            one_buffer((cont, 1)),
            one_buffer((1, cont)),
            one_buffer((rows, width)),
            one_buffer((cols, width)),
            *[s for c in range(3) for s in half_specs(PROMPT, c, True, pairs)],
            *[any_spec] * 2,
        ],
        [
            one_buffer((3, width, cols)),
            one_buffer((rows // 2, width)),
        ],
        [
            jax.ShapeDtypeStruct((3, width, cols), bf16),
            jax.ShapeDtypeStruct((rows // 2, width), f32),
        ],
        [
            pltpu.VMEM((cont, cont), f32),
            pltpu.VMEM((BLOCK, BLOCK), f32),
            pltpu.VMEM((2, rows // 2, cols), bf16),
            pltpu.VMEM((3, 2, rows // 2, cols), bf16),
            pltpu.VMEM((2, rows // 2, width), f32),
            pltpu.VMEM(w_qkv.shape, bf16),
            pltpu.VMEM(normed.shape, bf16),
            pltpu.SemaphoreType.DMA((4,)),
            pltpu.VMEM((rows // 2, width), bf16),
            pltpu.VMEM((rows // 2, width), bf16),
            *[pltpu.VMEM((PROMPT, LANES), f32)] * 4,
        ],
        [labels[:, None], labels[None, :], grad_attn, w_out, *[inputs] * 6, w_qkv, normed],
        rides,
        "attention_back",
        2 * rows * rows * cols * 5,
        3,
        True,
    )


def paired():
    return lax.axis_size("tensor") == 2


def swap(values):
    return lax.ppermute(values, "tensor", [(0, 1), (1, 0)])


def gather_rows(own):
    if paired():
        return jnp.concatenate([own, swap(own)], axis=0)
    return lax.all_gather(own, "tensor", axis=0, tiled=True)


def scatter_rows(partial, kind=bf16):
    if paired():
        size = partial.shape[0] // 2
        return partial[:size] + swap(partial[size:].astype(kind)).astype(f32)
    return lax.psum_scatter(
        partial.astype(kind), "tensor", scatter_dimension=0, tiled=True
    ).astype(f32)


def own_rows_of(values):
    size = values.shape[0] // lax.axis_size("tensor")
    if paired():
        return values[:size]
    return lax.dynamic_slice_in_dim(values, lax.axis_index("tensor") * size, size, 0)


def local_order(values):
    if paired():
        size = values.shape[0] // 2
        turned = jnp.concatenate([values[size:], values[:size]], axis=0)
        return jnp.where(lax.axis_index("tensor") == 0, values, turned)
    return values


def scatter_cols(partial):
    size = partial.shape[1] // lax.axis_size("tensor")
    rank = lax.axis_index("tensor")
    if paired():
        keep = lax.dynamic_slice_in_dim(partial, rank * size, size, 1)
        away = lax.dynamic_slice_in_dim(partial, (1 - rank) * size, size, 1).astype(bf16)
        return (keep + swap(away).astype(f32)).astype(bf16)
    return lax.psum_scatter(partial.astype(bf16), "tensor", scatter_dimension=1, tiled=True)


def turn_pair(cols_mine, count):
    width = cols_mine.shape[1] // count
    if not paired():
        return [
            lax.all_to_all(cols_mine[:, at : at + width], "tensor", 0, 1, tiled=True)
            for at in range(0, count * width, width)
        ]
    size = cols_mine.shape[0] // 2
    own, other = cols_mine[:size], swap(cols_mine[size:])
    first = lax.axis_index("tensor") == 0
    left, right = jnp.where(first, own, other), jnp.where(first, other, own)
    return [
        jnp.concatenate([left[:, at : at + width], right[:, at : at + width]], axis=1)
        for at in range(0, count * width, width)
    ]


def join_kernel(own_ref, other_ref, *outs):
    size = own_ref.shape[1] // len(outs)
    rank = lax.axis_index("tensor")
    for side in range(2):

        @pl.when(rank == side)
        def _(side=side):
            for number, out in enumerate(outs):
                cols = slice(number * size, (number + 1) * size)
                out[:, side * size : (side + 1) * size] = own_ref[:, cols]
                out[:, (1 - side) * size : (2 - side) * size] = other_ref[:, cols]


def join_cols(own, count):
    rows, width = own.shape
    if not paired():
        whole = lax.all_gather(own.reshape(rows, count, -1), "tensor", axis=2, tiled=True)
        return [whole[:, number] for number in range(count)]
    step = min(rows, 256)
    outs = [jax.ShapeDtypeStruct((rows, 2 * width // count), own.dtype)] * count
    return pl.pallas_call(
        join_kernel,
        grid=(rows // step,),
        in_specs=[pl.BlockSpec((step, width), lambda i: (i, 0))] * 2,
        out_specs=[pl.BlockSpec((step, 2 * width // count), lambda i: (i, 0))] * count,
        out_shape=outs,
        cost_estimate=pl.CostEstimate(
            flops=0, bytes_accessed=8 * rows * width, transcendentals=0
        ),
        name="join_cols",
    )(own, swap(own))


def body(
    tokens,
    norm1_gain,
    w_qkv,
    w_out,
    norm2_gain,
    w_up,
    w_down,
    w_router,
    w_mix,
    w_exp_up,
    w_exp_down,
    routes,
    segments,
    cotangent,
):
    own_rows = tokens.shape[0]
    model_width = tokens.shape[1]
    tensor_size = lax.axis_size("tensor")
    tensor_rank = lax.axis_index("tensor")
    owner_count = lax.axis_size("expert")
    group_rows = own_rows * tensor_size
    own_cols = model_width // tensor_size
    experts_all = w_router.shape[1]
    local_experts = w_exp_up.shape[0]
    capacity = group_rows // experts_all
    slots = experts_all * capacity
    barrier = lax.optimization_barrier
    special = owner_count == 16 and tensor_size == 2 and local_experts == 1

    def my_cols(values):
        return lax.dynamic_slice_in_dim(values, tensor_rank * own_cols, own_cols, 1)

    route_ids = local_order(routes[:, 0])
    route_hot = route_ids[:, None] == jnp.arange(experts_all, dtype=jnp.int32)[None, :]
    hot_float = route_hot.astype(f32)
    positions = local_order(jnp.arange(group_rows, dtype=jnp.int32))
    before = (positions[None, :] < positions[:, None]).astype(bf16)
    earlier = jnp.dot(before, route_hot.astype(bf16), preferred_element_type=f32)
    slot_index = jnp.sum(earlier * hot_float, axis=1).astype(jnp.int32)
    slot_of = jnp.where(slot_index < capacity, route_ids * capacity + slot_index, slots)
    slot_ids = jnp.arange(slots, dtype=jnp.int32)
    pick_rows = barrier((slot_ids[:, None] == slot_of[None, :]).astype(bf16))
    pick_slots = barrier((slot_of[:, None] == slot_ids[None, :]).astype(bf16))

    def by_expert(values):
        return values.transpose(1, 0, 2, 3).reshape(slots, values.shape[-1])

    def send_slots(cols_mine):
        picked = jnp.dot(pick_rows, cols_mine, preferred_element_type=f32).astype(bf16)
        picked = picked.reshape(owner_count, local_experts * capacity, -1)
        arrived = lax.all_to_all(picked, "expert", split_axis=0, concat_axis=0, tiled=True)
        return by_expert(arrived.reshape(owner_count, local_experts, capacity, -1))

    def return_slots(mine):
        mine = by_expert(mine.reshape(local_experts, owner_count, capacity, -1))
        mine = mine.reshape(owner_count, local_experts * capacity, -1)
        back = lax.all_to_all(mine, "expert", split_axis=0, concat_axis=0, tiled=True)
        return back.reshape(slots, -1)

    def unslot(back):
        rows = jnp.dot(pick_slots, back, preferred_element_type=f32).astype(bf16)
        return [
            whole.astype(f32) for whole in turn_pair(rows, back.shape[1] // own_cols)
        ]

    cot_all = gather_rows(cotangent)
    token_f32 = tokens.astype(f32)
    normed_one = layer_norm(token_f32, norm1_gain).astype(bf16)
    normed_all = barrier(gather_rows(normed_one))
    projected = jnp.einsum("gd,cdk->cgk", normed_all, w_qkv, preferred_element_type=f32).astype(
        bf16
    )
    labels = segments[0]
    attn_heads = attend(labels, projected)
    attn_part = jnp.dot(attn_heads, w_out, preferred_element_type=f32)
    attn_own = scatter_rows(attn_part)
    middle = token_f32 + attn_own
    normed_two = layer_norm(middle, norm2_gain).astype(bf16)
    hidden_all = gather_rows(normed_two)

    gate_w = jnp.concatenate([w_router, w_mix], axis=1)

    def gates(logits, hot):
        router_soft = jax.nn.softmax(logits[:, :experts_all], axis=-1)
        return jax.nn.softmax(logits[:, experts_all:], axis=-1), jnp.sum(
            router_soft * hot, axis=-1
        )

    logits = jnp.dot(hidden_all, gate_w, preferred_element_type=f32)
    mix_all, gate_all = gates(logits, hot_float)

    expert_grad_rows = (my_cols(cot_all) * (mix_all[:, 1] * gate_all)[:, None]).astype(bf16)
    arrived = send_slots(jnp.concatenate([my_cols(hidden_all), expert_grad_rows], axis=1))

    dense_grad_rows = barrier((cot_all * mix_all[:, 0:1]).astype(bf16))
    if special:
        y_keep, y_away, dx_keep, dx_away, grad_w_up, grad_w_down = feed_forward(
            hidden_all, dense_grad_rows, w_up, w_down
        )
        dense_own = y_keep + swap(y_away).astype(f32)
        dense_back_own = dx_keep + swap(dx_away).astype(f32)
    else:
        pre_up = jnp.dot(hidden_all, w_up, preferred_element_type=f32)
        act_up = jax.nn.gelu(pre_up).astype(bf16)
        dense_own = scatter_rows(jnp.dot(act_up, w_down, preferred_element_type=f32))
        grad_act_up = jnp.einsum("gd,fd->gf", dense_grad_rows, w_down, preferred_element_type=f32)
        grad_pre_up = gelu_grad(pre_up, grad_act_up).astype(bf16)
        grad_w_down = jnp.einsum("gf,gd->fd", act_up, dense_grad_rows, preferred_element_type=f32)
        grad_w_up = jnp.einsum("gd,gf->df", hidden_all, grad_pre_up, preferred_element_type=f32)
        dense_back_own = scatter_rows(
            jnp.einsum("gf,df->gd", grad_pre_up, w_up, preferred_element_type=f32)
        )

    arrived, grad_w_up = barrier((arrived, grad_w_up))
    slots_in, grad_slots_in = join_cols(arrived, 2)
    if special:
        dense_shapes = [grad_w_up.shape, grad_w_down.shape]
        share = (6, 6, 4)
        mine, act_exp, dact_exp, state = expert_data(
            slots_in,
            grad_slots_in,
            w_exp_up[0],
            w_exp_down[0],
            Ride(0, 1, [grad_w_up, grad_w_down], dense_shapes, 1024, share, 2),
        )
        mine, act_exp = barrier((mine, act_exp))
        back = return_slots(mine)
        grad_w_exp_up, grad_w_exp_down = expert_weights(
            slots_in, grad_slots_in, act_exp, dact_exp
        )
        state, grad_w_exp_up = barrier((state, grad_w_exp_up))
        (state,) = ride_alone(Ride(1, MIDDLE, [state], dense_shapes, 1024, share, 2), 2)
        back, state = barrier((back, state))
        grad_w_exp_up, grad_w_exp_down = grad_w_exp_up[None], grad_w_exp_down[None]
        expert_own, grad_expert_own = unslot(back)
    else:
        slots_in, grad_slots_in = (
            v.reshape(local_experts, owner_count * capacity, model_width)
            for v in (slots_in, grad_slots_in)
        )
        pre_exp = jnp.einsum("lsd,ldf->lsf", slots_in, w_exp_up, preferred_element_type=f32)
        act_exp = jax.nn.gelu(pre_exp).astype(bf16)
        out_exp = jnp.einsum("lsf,lfd->lsd", act_exp, w_exp_down, preferred_element_type=f32)
        (expert_own,) = unslot(return_slots(scatter_cols(out_exp.reshape(slots, model_width))))
        grad_act_exp = jnp.einsum(
            "lsd,lfd->lsf", grad_slots_in, w_exp_down, preferred_element_type=f32
        )
        grad_pre_exp = gelu_grad(pre_exp, grad_act_exp).astype(bf16)
        grad_slots_out = jnp.einsum(
            "lsf,ldf->lsd", grad_pre_exp, w_exp_up, preferred_element_type=f32
        )
        back = return_slots(scatter_cols(grad_slots_out.reshape(slots, model_width)))
        (grad_expert_own,) = unslot(back)
        grad_w_exp_down = jnp.einsum(
            "lsf,lsd->lfd", act_exp, grad_slots_in, preferred_element_type=f32
        )
        grad_w_exp_up = jnp.einsum(
            "lsd,lsf->ldf", slots_in, grad_pre_exp, preferred_element_type=f32
        )

    logits_own, hot_own = own_rows_of(logits), own_rows_of(hot_float)
    (mix_own, gate_own), gates_pull = jax.vjp(lambda z: gates(z, hot_own), logits_own)
    output = (
        middle + mix_own[:, 0:1] * dense_own + (mix_own[:, 1] * gate_own)[:, None] * expert_own
    ).astype(bf16)
    grad_out = cotangent.astype(f32)
    dense_dot = jnp.sum(grad_out * dense_own, axis=1)
    expert_dot = jnp.sum(grad_out * expert_own, axis=1)
    grad_mix_coef = jnp.stack([dense_dot, gate_own * expert_dot], axis=1)
    (grad_logits,) = gates_pull((grad_mix_coef, mix_own[:, 1] * expert_dot))
    grad_gate_w = lax.dot_general(
        grad_logits,
        normed_two.astype(f32),
        (((0,), (0,)), ((), ())),
        precision=highest,
        preferred_element_type=f32,
    )
    grad_hidden_gate = lax.dot_general(
        grad_logits,
        gate_w.astype(f32),
        (((1,), (1,)), ((), ())),
        precision=highest,
        preferred_element_type=f32,
    )
    grad_hidden_own = dense_back_own + grad_expert_own + grad_hidden_gate
    _, norm_two_pull = jax.vjp(layer_norm, middle, norm2_gain)
    grad_middle_norm, grad_gain2 = norm_two_pull(grad_hidden_own)
    grad_middle = grad_out + grad_middle_norm

    grad_attn_all = gather_rows(grad_middle.astype(bf16))
    if special:
        grad_w_out = jnp.einsum(
            "gk,gd->kd", attn_heads, grad_attn_all, preferred_element_type=f32
        ).astype(bf16)
        rides = [
            Ride(MIDDLE, 8, [state], dense_shapes, 1024, share, RIDE_GAP),
            Ride(0, 4, [grad_w_out], [grad_w_out.shape], 512, (2, 1, 1), 2),
        ]
        grad_w_qkv, grad_normed_one, grad_w_up, grad_w_down, state = attention_back(
            labels, projected, grad_attn_all, w_out, w_qkv, normed_all, rides
        )
    else:
        grad_w_out = jnp.einsum("gk,gd->kd", attn_heads, grad_attn_all, preferred_element_type=f32)
        grad_heads = jnp.einsum(
            "gd,kd->gk", grad_attn_all, w_out, preferred_element_type=f32
        ).astype(bf16)
        grad_qkv = attend_back(labels, projected, grad_heads)
        grad_w_qkv = jnp.einsum("gd,cgk->cdk", normed_all, grad_qkv, preferred_element_type=f32)
        grad_normed_one = scatter_rows(
            jnp.einsum("cgk,cdk->gd", grad_qkv, w_qkv, preferred_element_type=f32)
        )
    _, norm_one_pull = jax.vjp(layer_norm, token_f32, norm1_gain)
    grad_token_norm, grad_gain1 = norm_one_pull(grad_normed_one)
    grad_tokens = grad_middle + grad_token_norm

    small = jnp.concatenate([grad_gain1[None], grad_gain2[None], grad_gate_w], axis=0)
    if special:
        padding = -small.shape[0] % 8
        rides = [
            Ride(0, 8, [grad_w_qkv], [grad_w_qkv.shape], 512, (4, 4, 4), (0, 2, 3, 4, 5, 6, 7, 8, 10)),
            Ride(4, 8, [state], [grad_w_out.shape], 512, (2, 1, 1)),
        ]
        small = jnp.pad(small, ((0, padding), (0, 0)))
        small, grad_w_qkv, grad_w_out = last_sums(rides, small)
    else:
        grad_w_up, grad_w_down, grad_w_qkv, grad_w_out = lax.psum(
            [g.astype(bf16) for g in (grad_w_up, grad_w_down, grad_w_qkv, grad_w_out)], "expert"
        )
        small = lax.psum(small, ("expert", "tensor"))
    grad_w_qkv, grad_w_out, grad_w_up, grad_w_down = (
        g.astype(f32) for g in (grad_w_qkv, grad_w_out, grad_w_up, grad_w_down)
    )
    return (
        output,
        grad_tokens,
        small[0],
        grad_w_qkv,
        grad_w_out,
        small[1],
        grad_w_up,
        grad_w_down,
        small[2 : 2 + experts_all].T,
        small[2 + experts_all : 4 + experts_all].T,
        grad_w_exp_up,
        grad_w_exp_down,
    )


def solution(mesh):
    return jax.shard_map(
        body,
        mesh=mesh,
        in_specs=(
            P(("expert", "tensor"), None),
            P(),
            P(None, None, "tensor"),
            P("tensor", None),
            P(),
            P(None, "tensor"),
            P("tensor", None),
            P(),
            P(),
            P("expert", None, "tensor"),
            P("expert", "tensor", None),
            P("expert", None),
            P("expert", None),
            P(("expert", "tensor"), None),
        ),
        out_specs=(
            P(("expert", "tensor"), None),
            P(("expert", "tensor"), None),
            P(),
            P(None, None, "tensor"),
            P("tensor", None),
            P(),
            P(None, "tensor"),
            P("tensor", None),
            P(),
            P(),
            P("expert", None, "tensor"),
            P("expert", "tensor", None),
        ),
        check_vma=False,
    )
```
